32 devices in a mesh: grp: 4 (over y, x), img: 8 (over z, core).
Axes of the slice: x: 2, y: 2, z: 4, core: 2. Of those that a mesh axis runs over, the one named last changes fastest.
Arguments:
- pixels: bfloat16 [128, 8, 196, 256], P(('grp', 'img')), may hold values from -6 to 6
- cotangent: bfloat16 [128, 196, 768], P(('grp', 'img')), may hold values from -6 to 6
- band_count: int32 [4], P('grp'), may hold values from 2 to 8, as said below
- wave_index: int32 [4, 8], P('grp'), may hold values from 0 to 255
- weight_tokens: float32 [128, 128], replicated, may hold values from -6 to 6
- bias_token: float32 [128], replicated, may hold values from -6 to 6
- hyper_qkv: float32 [128, 384], replicated, may hold values from -0.5 to 0.5
- hyper_qv_bias: float32 [256], replicated, may hold values from -3 to 3
- hyper_out: float32 [128, 128], replicated, may hold values from -1.5 to 1.5
- hyper_out_bias: float32 [128], replicated, may hold values from -3 to 3
- hyper_norm1_gain: float32 [128], replicated, may hold values from 0.1 to 1.9
- hyper_norm1_bias: float32 [128], replicated, may hold values from -3 to 3
- hyper_ff1: float32 [128, 2048], replicated, may hold values from -0.5 to 0.5
- hyper_ff1_bias: float32 [2048], replicated, may hold values from -3 to 3
- hyper_ff2: float32 [2048, 128], replicated, may hold values from -0.125 to 0.125
- hyper_ff2_bias: float32 [128], replicated, may hold values from -3 to 3
- hyper_norm2_gain: float32 [128], replicated, may hold values from 0.1 to 1.9
- hyper_norm2_bias: float32 [128], replicated, may hold values from -3 to 3
- kernel_gen: bfloat16 [256, 768, 128], P('img'), may hold values from -0.01171875 to 0.01171875
- kernel_gen_bias: bfloat16 [256, 768], P('img'), may hold values from -0.119628906 to 0.119628906
- conv_bias_gen: bfloat16 [768, 128], P('img'), may hold values from -0.5 to 0.5
- conv_bias_gen_bias: bfloat16 [768], P('img'), may hold values from -3 to 3
- norm1_gain: bfloat16 [768], P('img'), may hold values from 0.099609375 to 1.8984375
- norm1_bias: bfloat16 [768], P('img'), may hold values from -2 to 2
- qkv_weight: bfloat16 [768, 2304], P('img'), may hold values from -0.21875 to 0.21875
- qv_bias: bfloat16 [1536], P('img'), may hold values from -2 to 2
- proj_weight: bfloat16 [768, 768], P('img'), may hold values from -1.75 to 1.75
- proj_bias: bfloat16 [768], P('img'), may hold values from -2 to 2
- norm2_gain: bfloat16 [768], P('img'), may hold values from 0.099609375 to 1.8984375
- norm2_bias: bfloat16 [768], P('img'), may hold values from -2 to 2
- fc1_weight: bfloat16 [768, 3072], P('img'), may hold values from -0.21875 to 0.21875
- fc1_bias: bfloat16 [3072], P('img'), may hold values from -2 to 2
- fc2_weight: bfloat16 [3072, 768], P('img'), may hold values from -0.109375 to 0.109375
- fc2_bias: bfloat16 [768], P('img'), may hold values from -2 to 2
Outputs:
- block_out: float32 [128, 196, 768], P(('grp', 'img'))
- pixel_grad: float32 [128, 8, 196, 256], P(('grp', 'img'))
- grad_weight_tokens: float32 [128, 128], replicated
- grad_bias_token: float32 [128], replicated
- grad_hyper_qkv: float32 [128, 384], replicated
- grad_hyper_qv_bias: float32 [256], replicated
- grad_hyper_out: float32 [128, 128], replicated
- grad_hyper_out_bias: float32 [128], replicated
- grad_hyper_norm1_gain: float32 [128], replicated
- grad_hypernet_norm1_bias: float32 [128], replicated
- grad_hyper_ff1: float32 [128, 2048], replicated
- grad_hyper_ff1_bias: float32 [2048], replicated
- grad_hyper_ff2: float32 [2048, 128], replicated
- grad_hyper_ff2_bias: float32 [128], replicated
- grad_hyper_norm2_gain: float32 [128], replicated
- grad_hyper_norm2_bias: float32 [128], replicated
- grad_kernel_gen: float32 [256, 768, 128], P('img', 'grp')
- grad_kernel_gen_bias: float32 [256, 768], P('img', 'grp')
- grad_conv_bias_gen: float32 [768, 128], P(('grp', 'img'))
- grad_conv_bias_gen_bias: float32 [768], P(('grp', 'img'))
- grad_norm1_gain: float32 [768], P(('grp', 'img'))
- grad_norm1_bias: float32 [768], P(('grp', 'img'))
- grad_qkv_weight: float32 [768, 2304], P(('grp', 'img'))
- grad_qv_bias: float32 [1536], P(('grp', 'img'))
- grad_proj_weight: float32 [768, 768], P(('grp', 'img'))
- grad_proj_bias: float32 [768], P(('grp', 'img'))
- grad_norm2_gain: float32 [768], P(('grp', 'img'))
- grad_norm2_bias: float32 [768], P(('grp', 'img'))
- grad_fc1_weight: float32 [768, 3072], P(('grp', 'img'))
- grad_fc1_bias: float32 [3072], P(('grp', 'img'))
- grad_fc2_weight: float32 [3072, 768], P(('grp', 'img'))
- grad_fc2_bias: float32 [768], P(('grp', 'img'))
The draws below stay inside these ranges and needn't reach their ends.
Inputs may be any that keep to these rules, and one draw needn't show every extreme that they name: Group g's bands fill its first band_count[g] slots; one group has all 8 slots, each other group at most 4. `wave_index`: rows of a table of 256 wavelengths evenly spaced from 400 to 2500 nanometres.
All inputs are finite; a program needn't handle non-finite values.
Results may differ from the reference program's by a relative error of at most 0.015.
Values may be sent and summed in bfloat16 or wider, within the bound.
No kernel may reach another device: no remote copies, remote signals or barrier semaphores. Data moves between devices by JAX's collectives and lax.ppermute only.
A program may use at most 256 MiB of HBM per device.

```python
import math
import jax
import jax.numpy as jnp
from jax import lax

D = 768
HEADS = 12
FF = 3072
WDIM = 128
WHEADS = 4
WFF = 2048
WTOK = 128
PATCH = 256
TOK = 196
BANDS = 8
WAVES = 256
HEAD_DIM = 64
GROUPS = 4
IMAGES = 128


def draw_band_count(key, part):
    counts = jax.random.randint(key, (GROUPS,), 2, BANDS // 2 + 1)
    fullest = jax.random.randint(jax.random.fold_in(key, 7), (), 0, GROUPS)
    return jnp.where(jnp.arange(GROUPS) == fullest, BANDS, counts).astype(jnp.int32)


def place_ends(result, stream_key, least, top_value):
    index_at = [jax.random.randint(jax.random.fold_in(stream_key, axis), (), 0, length) for axis, length in enumerate(result.shape)]
    longest = result.shape.index(max(result.shape))
    next_to = index_at[:longest] + [(index_at[longest] + 1) % result.shape[longest]] + index_at[longest + 1:]
    return result.at[tuple(index_at)].set(least).at[tuple(next_to)].set(top_value)


def with_spikes(values, stream_key, source, target, parts, factor):
    owner, partner = [(jnp.arange(values.shape[dim]) // (values.shape[dim] // parts)).reshape([-1 if axis == dim else 1 for axis in range(values.ndim)]) for dim in (source, target)]
    chosen = jax.random.permutation(stream_key, parts)[partner]
    strong = (owner == chosen) | (owner == (partner + parts // 2) % parts)
    return jnp.where(strong, factor * values, values)


def block_levels(stream_key, shape, cuts, smallest, top_value):
    level, own = 1.0, jax.random.fold_in(stream_key, 6)
    for axis_at, blocks in cuts:
        steps = jnp.exp(jax.random.uniform(jax.random.fold_in(own, axis_at), (blocks,), jnp.float32, smallest / len(cuts), top_value / len(cuts)))
        level = level * jnp.repeat(steps, shape[axis_at] // blocks).reshape([-1 if axis == axis_at else 1 for axis in range(len(shape))])
    return level


def scatter_about(stream_key, shape, width, limit, pieces=(), kind=jnp.bfloat16):
    values = width * jax.random.normal(stream_key, shape, jnp.float32)
    if pieces:
        values = values * block_levels(stream_key, shape, pieces, -0.22, 0.18)
    return jnp.clip(values, -limit, limit).astype(kind)


def gaussian_with(own_key, extent, width, reach, split, heavy, kind=jnp.bfloat16):
    array = width * jax.random.normal(own_key, extent, jnp.float32)
    if split:
        array = array * block_levels(own_key, extent, split, -0.22, 0.18)
    return jnp.clip(with_spikes(array, jax.random.fold_in(own_key, 3), *heavy), -reach, reach).astype(kind)


def setup_inputs(seed: int = 0) -> dict:
    seeds = jax.random.split(jax.random.key(seed), 35)
    pixels = scatter_about(seeds[0], (IMAGES, BANDS, TOK, PATCH), 1.0, 6.0, ((0, 32),))
    cotangent = gaussian_with(seeds[1], (IMAGES, TOK, D), 1.0, 6.0, ((0, 32),), (0, 2, 32, 2.75))
    band_count = draw_band_count(jax.random.fold_in(seeds[34], 71), 0)
    wave_index = place_ends(jax.random.randint(seeds[3], (GROUPS, BANDS), 0, WAVES), jax.random.fold_in(seeds[3], 1), 0, WAVES - 1).astype(jnp.int32)
    weight_tokens = scatter_about(seeds[4], (WTOK, WDIM), 1.0, 6.0, (), jnp.float32)
    bias_token = scatter_about(seeds[5], (WDIM,), 1.0, 6.0, (), jnp.float32)
    hyper_qkv = scatter_about(seeds[6], (WDIM, 3 * WDIM), WDIM ** -0.5, 0.5, (), jnp.float32)
    hyper_qv_bias = scatter_about(seeds[7], (2 * WDIM,), 0.5, 3.0, (), jnp.float32)
    hyper_out = scatter_about(seeds[8], (WDIM, WDIM), (WDIM // 8) ** -0.5, 1.5, (), jnp.float32)
    hyper_out_bias = scatter_about(seeds[9], (WDIM,), 0.5, 3.0, (), jnp.float32)
    hyper_norm1_gain = jnp.clip(1.0 + 0.18 * jax.random.normal(seeds[10], (WDIM,), jnp.float32), 0.1, 1.9)
    hyper_norm1_bias = scatter_about(seeds[11], (WDIM,), 0.5, 3.0, (), jnp.float32)
    hyper_ff1 = scatter_about(seeds[12], (WDIM, WFF), WDIM ** -0.5, 0.5, (), jnp.float32)
    hyper_ff1_bias = scatter_about(seeds[13], (WFF,), 0.5, 3.0, (), jnp.float32)
    hyper_ff2 = scatter_about(seeds[14], (WFF, WDIM), WFF ** -0.5, 0.125, (), jnp.float32)
    hyper_ff2_bias = scatter_about(seeds[15], (WDIM,), 0.5, 3.0, (), jnp.float32)
    hyper_norm2_gain = jnp.clip(1.0 + 0.18 * jax.random.normal(seeds[16], (WDIM,), jnp.float32), 0.1, 1.9)
    hyper_norm2_bias = scatter_about(seeds[17], (WDIM,), 0.5, 3.0, (), jnp.float32)
    kernel_gen = scatter_about(seeds[18], (PATCH, D, WDIM), (WDIM * PATCH * 8) ** -0.5, 0.01171875, ((0, 8),))
    kernel_gen_bias = scatter_about(seeds[19], (PATCH, D), 0.02, 0.119628906, ((0, 8),))
    conv_bias_gen = scatter_about(seeds[20], (D, WDIM), WDIM ** -0.5, 0.5, ((0, 8),))
    conv_bias_gen_bias = scatter_about(seeds[21], (D,), 0.5, 3.0, ((0, 8),))
    norm1_gain = jnp.clip(1.0 + 0.18 * jax.random.normal(seeds[22], (D,), jnp.float32), 0.099609375, 1.8984375).astype(jnp.bfloat16)
    norm1_bias = scatter_about(seeds[23], (D,), 0.3, 2.0, ((0, 8),))
    qkv_weight = scatter_about(seeds[24], (D, 3 * D), D ** -0.5, 0.21875, ((0, 8),))
    qv_bias = scatter_about(seeds[25], (2 * D,), 0.3, 2.0, ((0, 8),))
    proj_weight = scatter_about(seeds[26], (D, D), (D // 64) ** -0.5, 1.75, ((0, 8),))
    proj_bias = scatter_about(seeds[27], (D,), 0.3, 2.0, ((0, 8),))
    norm2_gain = jnp.clip(1.0 + 0.18 * jax.random.normal(seeds[28], (D,), jnp.float32), 0.099609375, 1.8984375).astype(jnp.bfloat16)
    norm2_bias = scatter_about(seeds[29], (D,), 0.3, 2.0, ((0, 8),))
    fc1_weight = scatter_about(seeds[30], (D, FF), D ** -0.5, 0.21875, ((0, 8),))
    fc1_bias = scatter_about(seeds[31], (FF,), 0.3, 2.0, ((0, 8),))
    fc2_weight = scatter_about(seeds[32], (FF, D), FF ** -0.5, 0.109375, ((0, 8),))
    fc2_bias = scatter_about(seeds[33], (D,), 0.3, 2.0, ((0, 8),))
    return dict(pixels=pixels, cotangent=cotangent, band_count=band_count, wave_index=wave_index, weight_tokens=weight_tokens, bias_token=bias_token, hyper_qkv=hyper_qkv, hyper_qv_bias=hyper_qv_bias, hyper_out=hyper_out, hyper_out_bias=hyper_out_bias, hyper_norm1_gain=hyper_norm1_gain, hyper_norm1_bias=hyper_norm1_bias, hyper_ff1=hyper_ff1, hyper_ff1_bias=hyper_ff1_bias, hyper_ff2=hyper_ff2, hyper_ff2_bias=hyper_ff2_bias, hyper_norm2_gain=hyper_norm2_gain, hyper_norm2_bias=hyper_norm2_bias, kernel_gen=kernel_gen, kernel_gen_bias=kernel_gen_bias, conv_bias_gen=conv_bias_gen, conv_bias_gen_bias=conv_bias_gen_bias, norm1_gain=norm1_gain, norm1_bias=norm1_bias, qkv_weight=qkv_weight, qv_bias=qv_bias, proj_weight=proj_weight, proj_bias=proj_bias, norm2_gain=norm2_gain, norm2_bias=norm2_bias, fc1_weight=fc1_weight, fc1_bias=fc1_bias, fc2_weight=fc2_weight, fc2_bias=fc2_bias)


@jax.custom_vjp
def low(v):
    return lax.optimization_barrier(v.astype(jnp.bfloat16)).astype(jnp.float32)

@jax.custom_vjp
def low_back(v):
    return v

def low_keep(v):
    return (low(v), None)

def low_pass(kept, grad):
    return (grad,)

def back_keep(v):
    return (v, None)

def back_low(kept, grad):
    return (low(grad),)
low.defvjp(low_keep, low_pass)
low_back.defvjp(back_keep, back_low)
norm_eps = 1e-06
hyper_eps = 1e-05
highest_precision = lax.Precision.HIGHEST

def layer_norm(values, norm_gain, norm_shift, epsilon):
    centre = values - lax.optimization_barrier(jnp.mean(values, axis=-1, keepdims=True))
    spread = lax.optimization_barrier(jnp.mean(centre * centre, axis=-1, keepdims=True))
    return centre * lax.rsqrt(spread + epsilon) * norm_gain + norm_shift

def gelu_exact(values):
    return jax.nn.gelu(values, approximate=False)

def wave_embed(indices, hyper_width):
    half_model_width = hyper_width // 2
    wavelength = 400.0 + 2100.0 * indices.astype(jnp.float32) / (WAVES - 1)
    frequency = 1.0 / 10000.0 ** (jnp.arange(half_model_width, dtype=jnp.float32) / half_model_width)
    angles = wavelength[:, None] * frequency[None, :]
    return jnp.concatenate([jnp.sin(angles), jnp.cos(angles)], axis=-1)

def hyper_forward(params, indices, band_total):
    tokens, bias_tok, qkv_w, qv_b, out_w, out_b, gain_one, shift_one, ff_in, ff_in_b, ff_out, ff_out_b, gain_two, shift_two = params
    hyper_width = tokens.shape[1]
    slot_count = indices.shape[0]
    token_rows = tokens.shape[0]
    head_dim = hyper_width // WHEADS
    waves = wave_embed(indices, hyper_width)
    joined = jnp.concatenate([tokens, waves, bias_tok[None, :]], axis=0)
    query_rows = joined[token_rows:]
    queries = (jnp.dot(query_rows, qkv_w[:, :hyper_width], precision=highest_precision) + qv_b[:hyper_width]).reshape(slot_count + 1, WHEADS, head_dim)
    key_rows = jnp.dot(joined, qkv_w[:, hyper_width:2 * hyper_width], precision=highest_precision).reshape(-1, WHEADS, head_dim)
    values = (jnp.dot(joined, qkv_w[:, 2 * hyper_width:], precision=highest_precision) + qv_b[hyper_width:]).reshape(-1, WHEADS, head_dim)
    scores = jnp.einsum('qhd,khd->hqk', queries, key_rows, precision=highest_precision) * head_dim ** (-0.5)
    offsets = jnp.arange(joined.shape[0]) - token_rows
    usable = (offsets < band_total) | (offsets == slot_count)
    scores = jnp.where(usable[None, None, :], scores, -1e+30)
    weights = jax.nn.softmax(scores, axis=-1)
    mixture = jnp.einsum('hqk,khd->qhd', weights, values, precision=highest_precision).reshape(slot_count + 1, hyper_width)
    normed_one = layer_norm(query_rows + jnp.dot(mixture, out_w, precision=highest_precision) + out_b, gain_one, shift_one, hyper_eps)
    hidden = gelu_exact(jnp.dot(normed_one, ff_in, precision=highest_precision) + ff_in_b)
    normed_two = layer_norm(normed_one + jnp.dot(hidden, ff_out, precision=highest_precision) + ff_out_b, gain_two, shift_two, hyper_eps)
    return (normed_two[:slot_count] + waves, normed_two[slot_count])

def embed_block(block_of_pixels, patch_kernels, convolution_bias, block_params):
    gain_one, shift_one, qkv_weight, qv_bias, proj_weight, proj_bias, gain_two, shift_two, fc1_weight, fc1_bias, fc2_weight, fc2_bias = block_params
    images = block_of_pixels.shape[0]
    row_count = images * TOK
    embedded_tokens = jnp.einsum('lfhz,fzp->lhp', block_of_pixels, patch_kernels, precision=highest_precision) + convolution_bias
    embedded_tokens = low_back(embedded_tokens).reshape(row_count, D)
    normed = low(layer_norm(embedded_tokens, gain_one, shift_one, norm_eps))
    full_bias = jnp.concatenate([qv_bias[:D], jnp.zeros((D,), jnp.float32), qv_bias[D:]])
    projected = low_back(low(jnp.dot(normed, qkv_weight, precision=highest_precision) + full_bias))
    shaped = projected.reshape(images, TOK, 3, HEADS, HEAD_DIM)
    queries = shaped[:, :, 0]
    key_rows = shaped[:, :, 1]
    value_rows = shaped[:, :, 2]
    scores = low_back(jnp.einsum('ithd,ishd->ihts', queries, key_rows, precision=highest_precision) * HEAD_DIM ** (-0.5))
    attn_probs = low(jax.nn.softmax(scores, axis=-1))
    attended = low_back(low(jnp.einsum('ihts,ishd->ithd', attn_probs, value_rows, precision=highest_precision).reshape(row_count, D)))
    branch = low_back(jnp.dot(attended, proj_weight, precision=highest_precision) + proj_bias)
    middle = embedded_tokens + branch
    normed_two = low(layer_norm(middle, gain_two, shift_two, norm_eps))
    gate_in = low_back(jnp.dot(normed_two, fc1_weight, precision=highest_precision) + fc1_bias)
    activated = low(gelu_exact(gate_in))
    update = low_back(jnp.dot(activated, fc2_weight, precision=highest_precision) + fc2_bias)
    return (middle + update).reshape(images, TOK, D)

def forward(hyper_params, kernel_gen, kernel_gen_bias, conv_bias_gen, conv_bias_gen_bias, block_params, pixel_values, band_count, wave_index):
    per_group = IMAGES // GROUPS
    step_images = math.gcd(per_group, 16)
    outputs = []
    for sensor in range(GROUPS):
        band_total = band_count[sensor]
        hidden, bias_row = hyper_forward(hyper_params, wave_index[sensor], band_total)
        band_mask = (jnp.arange(BANDS) < band_total).astype(jnp.float32)
        kernel_pre = jnp.einsum('be,pde->bpd', low(hidden), kernel_gen, precision=highest_precision) + kernel_gen_bias[None]
        patch_kernels = low(kernel_pre * band_mask[:, None, None])
        convolution_bias = jnp.dot(conv_bias_gen, bias_row, precision=highest_precision) + conv_bias_gen_bias
        group_pixels = pixel_values[sensor * per_group:(sensor + 1) * per_group].reshape(per_group // step_images, step_images, BANDS, TOK, PATCH)

        def scan_step(scan_state, block_of_pixels, patch_kernels=patch_kernels, convolution_bias=convolution_bias):
            return (scan_state, jax.checkpoint(embed_block)(block_of_pixels, patch_kernels, convolution_bias, block_params))
        _, results = lax.scan(scan_step, jnp.zeros((), jnp.float32), group_pixels)
        outputs.append(results.reshape(per_group, TOK, D))
    return jnp.concatenate(outputs, axis=0)

def reference(pixels, cotangent, band_count, wave_index, weight_tokens, bias_token, hyper_qkv, hyper_qv_bias, hyper_out, hyper_out_bias, hyper_norm1_gain, hyper_norm1_bias, hyper_ff1, hyper_ff1_bias, hyper_ff2, hyper_ff2_bias, hyper_norm2_gain, hyper_norm2_bias, kernel_gen, kernel_gen_bias, conv_bias_gen, conv_bias_gen_bias, norm1_gain, norm1_bias, qkv_weight, qv_bias, proj_weight, proj_bias, norm2_gain, norm2_bias, fc1_weight, fc1_bias, fc2_weight, fc2_bias):
    hyper_params = (weight_tokens, bias_token, hyper_qkv, hyper_qv_bias, hyper_out, hyper_out_bias, hyper_norm1_gain, hyper_norm1_bias, hyper_ff1, hyper_ff1_bias, hyper_ff2, hyper_ff2_bias, hyper_norm2_gain, hyper_norm2_bias)
    block_params = tuple((member.astype(jnp.float32) for member in (norm1_gain, norm1_bias, qkv_weight, qv_bias, proj_weight, proj_bias, norm2_gain, norm2_bias, fc1_weight, fc1_bias, fc2_weight, fc2_bias)))

    def wrapped(hyper_p, gen_w, gen_b, bias_w, bias_b, block_p, pixel_values):
        return forward(hyper_p, gen_w, gen_b, bias_w, bias_b, block_p, pixel_values, band_count, wave_index)
    block_out, pull = jax.vjp(wrapped, hyper_params, kernel_gen.astype(jnp.float32), kernel_gen_bias.astype(jnp.float32), conv_bias_gen.astype(jnp.float32), conv_bias_gen_bias.astype(jnp.float32), block_params, pixels.astype(jnp.float32))
    hyper_grads, grad_gen, grad_gen_bias, grad_bias_gen, grad_bias_gen_bias, block_grads, pixel_grad = pull(cotangent.astype(jnp.float32))
    return (block_out, pixel_grad, hyper_grads[0], hyper_grads[1], hyper_grads[2], hyper_grads[3], hyper_grads[4], hyper_grads[5], hyper_grads[6], hyper_grads[7], hyper_grads[8], hyper_grads[9], hyper_grads[10], hyper_grads[11], hyper_grads[12], hyper_grads[13], grad_gen, grad_gen_bias, grad_bias_gen, grad_bias_gen_bias, block_grads[0], block_grads[1], block_grads[2], block_grads[3], block_grads[4], block_grads[5], block_grads[6], block_grads[7], block_grads[8], block_grads[9], block_grads[10], block_grads[11])
```

```python
import functools

import jax
import jax.numpy as jnp
from jax import lax
from jax.experimental import pallas as pl
from jax.experimental.pallas import tpu as pltpu
from jax.sharding import PartitionSpec as P

HEADS = 12
WHEADS = 4
WAVES = 256


norm_eps = 1e-06
hyper_eps = 1e-05
highest_precision = lax.Precision.HIGHEST


def layer_norm(values, norm_gain, norm_shift, epsilon):
    centre = values - jnp.mean(values, axis=-1, keepdims=True)
    spread = jnp.mean(centre * centre, axis=-1, keepdims=True)
    return centre * lax.rsqrt(spread + epsilon) * norm_gain + norm_shift


def gelu_exact(values):
    return jax.nn.gelu(values, approximate=False)


def wave_embed(indices, hyper_width):
    half_model_width = hyper_width // 2
    wavelength = 400.0 + 2100.0 * indices.astype(jnp.float32) / (WAVES - 1)
    frequency = 1.0 / 10000.0 ** (
        jnp.arange(half_model_width, dtype=jnp.float32) / half_model_width
    )
    angles = wavelength[:, None] * frequency[None, :]
    return jnp.concatenate([jnp.sin(angles), jnp.cos(angles)], axis=-1)


def hyper_forward(params, indices, band_total):
    (
        tokens,
        bias_tok,
        qkv_w,
        qv_b,
        out_w,
        out_b,
        gain_one,
        shift_one,
        ff_in,
        ff_in_b,
        ff_out,
        ff_out_b,
        gain_two,
        shift_two,
    ) = params
    hyper_width = tokens.shape[1]
    slot_count = indices.shape[0]
    token_rows = tokens.shape[0]
    head_dim = hyper_width // WHEADS
    waves = wave_embed(indices, hyper_width)
    joined = jnp.concatenate([tokens, waves, bias_tok[None, :]], axis=0)
    query_rows = joined[token_rows:]
    queries = (
        jnp.dot(query_rows, qkv_w[:, :hyper_width], precision=highest_precision)
        + qv_b[:hyper_width]
    ).reshape(slot_count + 1, WHEADS, head_dim)
    key_rows = jnp.dot(
        joined, qkv_w[:, hyper_width : 2 * hyper_width], precision=highest_precision
    ).reshape(-1, WHEADS, head_dim)
    values = (
        jnp.dot(joined, qkv_w[:, 2 * hyper_width :], precision=highest_precision)
        + qv_b[hyper_width:]
    ).reshape(-1, WHEADS, head_dim)
    scores = jnp.einsum(
        "qhd,khd->hqk", queries, key_rows, precision=highest_precision
    ) * head_dim ** (-0.5)
    offsets = jnp.arange(joined.shape[0]) - token_rows
    usable = (offsets < band_total) | (offsets == slot_count)
    scores = jnp.where(usable[None, None, :], scores, -1e30)
    weights = jax.nn.softmax(scores, axis=-1)
    mixture = jnp.einsum("hqk,khd->qhd", weights, values, precision=highest_precision).reshape(
        slot_count + 1, hyper_width
    )
    normed_one = layer_norm(
        query_rows + jnp.dot(mixture, out_w, precision=highest_precision) + out_b,
        gain_one,
        shift_one,
        hyper_eps,
    )
    hidden = gelu_exact(jnp.dot(normed_one, ff_in, precision=highest_precision) + ff_in_b)
    normed_two = layer_norm(
        normed_one + jnp.dot(hidden, ff_out, precision=highest_precision) + ff_out_b,
        gain_two,
        shift_two,
        hyper_eps,
    )
    return (normed_two[:slot_count] + waves, normed_two[slot_count])


BOTH = ("grp", "img")


def torus_block():
    return lax.axis_size("grp") == 4 and lax.axis_size("img") == 8


def flipped(index, bit):
    return index ^ bit


def swap(value, bit):
    return lax.ppermute(value, BOTH, [(i, i ^ bit) for i in range(32)])


def along_z(value, step, senders):
    moves = [(i, i + 2 * step) for i in range(32) if (i % 8) // 2 in senders]
    return lax.ppermute(value, BOTH, moves)


def pick(value, index, axis=0):
    return lax.dynamic_index_in_dim(value, index, axis, keepdims=False)


def add_low(left, right):
    return (left.astype(jnp.float32) + right.astype(jnp.float32)).astype(jnp.bfloat16)


def line_scatter(chunks):
    z = (lax.axis_index("img") // 2).astype(jnp.int32)
    up = down = None
    for step in range(1, 4):
        up_term = pick(chunks, jnp.clip(4 - step + z, 0, 3))
        down_term = pick(chunks, jnp.clip(z - 4 + step, 0, 3))
        if step > 1:
            up_term = add_low(up_term, up)
            down_term = add_low(down_term, down)
        up = along_z(up_term, 1, range(step))
        down = along_z(down_term, -1, range(4 - step, 4))
    own = pick(chunks, z)
    return own.astype(jnp.float32) + up.astype(jnp.float32) + down.astype(jnp.float32)


def line_gather(own):
    z = (lax.axis_index("img") // 2).astype(jnp.int32)
    up = down = own
    by_offset = {0: own}
    for step in range(1, 4):
        up = along_z(up, 1, range(step - 1, 3))
        down = along_z(down, -1, range(1, 5 - step))
        by_offset[-step] = up
        by_offset[step] = down
    rows = []
    for place in range(4):
        row = by_offset[place]
        for z_at in range(1, 4):
            row = jnp.where(z == z_at, by_offset[place - z_at], row)
        rows.append(row)
    return jnp.stack(rows)


def scatter_all(value):
    if not torus_block():
        return lax.psum_scatter(value, BOTH, scatter_dimension=0, tiled=True)[0].astype(jnp.float32)
    core = lax.axis_index("img") % 2
    x = lax.axis_index("grp") % 2
    y = lax.axis_index("grp") // 2
    value = value.reshape((2, 2, 4, 2) + value.shape[1:])
    value = add_low(pick(value, core, 3), swap(pick(value, 1 - core, 3), 1))
    first, second = value[:, :, :2], value[:, :, 2:]
    first_in = swap(pick(first, 1 - x, 1), 8)
    second_in = swap(pick(second, 1 - y, 0), 16)
    first = add_low(pick(first, x, 1), first_in)
    second = add_low(pick(second, y, 0), second_in)
    first_in = swap(pick(first, 1 - y), 16)
    second_in = swap(pick(second, 1 - x), 8)
    first = add_low(pick(first, y), first_in)
    second = add_low(pick(second, x), second_in)
    return line_scatter(jnp.concatenate([first, second]))


def scatter_shards(value):
    if not torus_block():
        return lax.psum_scatter(value, "img", scatter_dimension=0, tiled=True)[0].astype(jnp.float32)
    core = lax.axis_index("img") % 2
    value = value.reshape((4, 2) + value.shape[1:])
    value = add_low(pick(value, core, 1), swap(pick(value, 1 - core, 1), 1))
    return line_scatter(value)


def gather_shards(value):
    if not torus_block():
        return lax.all_gather(value, "img", axis=0, tiled=False)
    core = lax.axis_index("img") % 2
    line = line_gather(value)
    other = swap(line, 1)
    both = jnp.stack([jnp.where(core == 0, line, other), jnp.where(core == 0, other, line)], axis=1)
    return both.reshape((8,) + value.shape)


def lane_half(shape):
    return lax.broadcasted_iota(jnp.int32, shape, len(shape) - 1) % 128 < 64


def attention_forward_kernel(tokens, projected_ref, attended_ref, probs_ref):
    width = projected_ref.shape[1] // 3
    rows = projected_ref.shape[0]
    low_half = lane_half((rows, 128))
    real_key = lax.broadcasted_iota(jnp.int32, (rows, rows), 0) < tokens
    for pair in range(width // 128):
        at = pair * 128
        queries = projected_ref[:, at : at + 128] * jnp.bfloat16(0.125)
        key_rows = projected_ref[:, width + at : width + at + 128]
        values = projected_ref[:, 2 * width + at : 2 * width + at + 128]
        halves = []
        for half in range(2):
            chosen = low_half if half == 0 else ~low_half
            own_queries = jnp.where(chosen, queries, jnp.bfloat16(0))
            scores = lax.dot_general(
                key_rows, own_queries, (((1,), (1,)), ((), ())), preferred_element_type=jnp.float32
            )
            scores = jnp.where(real_key, scores, -1e30)
            raised = jnp.exp(scores - jnp.max(scores, axis=0, keepdims=True))
            probs = raised * (1.0 / jnp.sum(raised, axis=0, keepdims=True))
            probs = probs.astype(jnp.bfloat16)
            probs_ref[2 * pair + half] = probs
            halves.append(
                lax.dot_general(
                    probs, values, (((0,), (0,)), ((), ())), preferred_element_type=jnp.float32
                )
            )
        attended_ref[:, at : at + 128] = jnp.where(low_half, halves[0], halves[1]).astype(
            jnp.bfloat16
        )


def attention_forward(projected, images, tokens):
    rows = projected.shape[0] // images
    width = projected.shape[1] // 3
    heads = width // 64
    return pl.pallas_call(
        functools.partial(attention_forward_kernel, tokens),
        grid=(images,),
        in_specs=[pl.BlockSpec((rows, 3 * width), lambda i: (i, 0))],
        out_specs=[
            pl.BlockSpec((rows, width), lambda i: (i, 0)),
            pl.BlockSpec((None, heads, rows, rows), lambda i: (i, 0, 0, 0)),
        ],
        out_shape=[
            jax.ShapeDtypeStruct((images * rows, width), jnp.bfloat16),
            jax.ShapeDtypeStruct((images, heads, rows, rows), jnp.bfloat16),
        ],
        compiler_params=pltpu.CompilerParams(vmem_limit_bytes=24 << 20),
        cost_estimate=pl.CostEstimate(
            flops=images * heads * rows * rows * 64 * 4,
            bytes_accessed=images * rows * (8 * width + 2 * heads * rows),
            transcendentals=images * heads * rows * rows,
        ),
        name="attention_forward",
    )(projected)


def attention_backward_kernel(projected_ref, probs_ref, grad_ref, out_ref, sums_ref):
    width = projected_ref.shape[1] // 3
    rows = projected_ref.shape[0]
    low_half = lane_half((rows, 128))

    @pl.when(pl.program_id(0) == 0)
    def _():
        sums_ref[...] = jnp.zeros_like(sums_ref)

    for pair in range(width // 128):
        at = pair * 128
        queries = projected_ref[:, at : at + 128]
        key_rows = projected_ref[:, width + at : width + at + 128]
        values = projected_ref[:, 2 * width + at : 2 * width + at + 128]
        grads = grad_ref[:, at : at + 128]
        found = []
        for half in range(2):
            chosen = low_half if half == 0 else ~low_half
            probs = probs_ref[2 * pair + half]
            own_grads = jnp.where(chosen, grads, jnp.bfloat16(0))
            grad_values = jnp.dot(probs, grads, preferred_element_type=jnp.float32)
            grad_probs = lax.dot_general(
                values, own_grads, (((1,), (1,)), ((), ())), preferred_element_type=jnp.float32
            )
            wide = probs.astype(jnp.float32)
            weighted = grad_probs * wide
            total = jnp.sum(weighted, axis=0, keepdims=True)
            grad_scores = (weighted - wide * total).astype(jnp.bfloat16)
            grad_keys = jnp.dot(grad_scores, queries, preferred_element_type=jnp.float32) * 0.125
            grad_queries = (
                lax.dot_general(
                    grad_scores,
                    key_rows,
                    (((0,), (0,)), ((), ())),
                    preferred_element_type=jnp.float32,
                )
                * 0.125
            )
            found.append((grad_queries, grad_keys, grad_values))
        for kind in range(3):
            joined = jnp.where(low_half, found[0][kind], found[1][kind]).astype(jnp.bfloat16)
            place = slice(kind * width + at, kind * width + at + 128)
            out_ref[:, place] = joined
            sums_ref[:, place] += jnp.sum(
                joined.astype(jnp.float32).reshape(rows // 8, 8, 128), axis=0
            )


def attention_backward(projected, probs, grad_attended, images):
    rows = projected.shape[0] // images
    width = projected.shape[1] // 3
    heads = width // 64
    return pl.pallas_call(
        attention_backward_kernel,
        grid=(images,),
        in_specs=[
            pl.BlockSpec((rows, 3 * width), lambda i: (i, 0)),
            pl.BlockSpec((None, heads, rows, rows), lambda i: (i, 0, 0, 0)),
            pl.BlockSpec((rows, width), lambda i: (i, 0)),
        ],
        out_specs=[
            pl.BlockSpec((rows, 3 * width), lambda i: (i, 0)),
            pl.BlockSpec((8, 3 * width), lambda i: (0, 0)),
        ],
        out_shape=[
            jax.ShapeDtypeStruct((images * rows, 3 * width), jnp.bfloat16),
            jax.ShapeDtypeStruct((8, 3 * width), jnp.float32),
        ],
        compiler_params=pltpu.CompilerParams(vmem_limit_bytes=24 << 20),
        cost_estimate=pl.CostEstimate(
            flops=images * heads * rows * rows * 64 * 10,
            bytes_accessed=images * rows * (14 * width + 2 * heads * rows),
            transcendentals=0,
        ),
        name="attention_backward",
    )(projected, probs, grad_attended)


def ordered_gather(value, axis):
    total = lax.axis_size(axis)
    at = lax.axis_index(axis)
    slots = jnp.arange(total).reshape((total,) + (1,) * value.ndim)
    gathered = jnp.where(slots == at, value[None], jnp.zeros((), value.dtype))
    for shift in range(1, total):
        moved = lax.ppermute(value, axis, [(i, (i + shift) % total) for i in range(total)])
        gathered = jnp.where(slots == (at - shift) % total, moved[None], gathered)
    return gathered


def local(
    pixels,
    cotangent,
    band_count,
    wave_index,
    weight_tokens,
    bias_token,
    hyper_qkv,
    hyper_qv_bias,
    hyper_out,
    hyper_out_bias,
    hyper_norm1_gain,
    hyper_norm1_bias,
    hyper_ff1,
    hyper_ff1_bias,
    hyper_ff2,
    hyper_ff2_bias,
    hyper_norm2_gain,
    hyper_norm2_bias,
    kernel_gen,
    kernel_gen_bias,
    conv_bias_gen,
    conv_bias_gen_bias,
    norm1_gain,
    norm1_bias,
    qkv_weight,
    qv_bias,
    proj_weight,
    proj_bias,
    norm2_gain,
    norm2_bias,
    fc1_weight,
    fc1_bias,
    fc2_weight,
    fc2_bias,
):
    group_total = lax.axis_size("grp")
    shard_total = lax.axis_size("img")
    group_at = lax.axis_index("grp")
    shard_at = lax.axis_index("img")
    small_lengths = [
        member.shape[0]
        for member in (
            conv_bias_gen_bias,
            norm1_gain,
            norm1_bias,
            qv_bias,
            proj_bias,
            norm2_gain,
            norm2_bias,
            fc1_bias,
            fc2_bias,
        )
    ]
    small_flat = jnp.concatenate(
        [
            conv_bias_gen_bias,
            norm1_gain,
            norm1_bias,
            qv_bias,
            proj_bias,
            norm2_gain,
            norm2_bias,
            fc1_bias,
            fc2_bias,
        ]
    )
    hyper_wide = conv_bias_gen.shape[1]
    qkv_full = lax.all_gather(qkv_weight, "img", axis=0, tiled=True)
    proj_full = lax.all_gather(proj_weight, "img", axis=0, tiled=True)
    fc1_full = lax.all_gather(fc1_weight, "img", axis=0, tiled=True)
    fc2_full = lax.all_gather(fc2_weight, "img", axis=0, tiled=True)
    images = pixels.shape[0]
    slot_count = pixels.shape[1]
    tokens = pixels.shape[2]
    patch = pixels.shape[3]
    model_width = cotangent.shape[2]
    padded = -(-tokens // 16) * 16
    row_count = images * padded

    def pad_rows(value):
        return jnp.pad(value, ((0, 0), (0, padded - tokens), (0, 0))).reshape(row_count, -1)

    band_total = band_count[0]
    band_mask = (jnp.arange(slot_count) < band_total).astype(jnp.float32)
    hyper_params = (
        weight_tokens,
        bias_token,
        hyper_qkv,
        hyper_qv_bias,
        hyper_out,
        hyper_out_bias,
        hyper_norm1_gain,
        hyper_norm1_bias,
        hyper_ff1,
        hyper_ff1_bias,
        hyper_ff2,
        hyper_ff2_bias,
        hyper_norm2_gain,
        hyper_norm2_bias,
    )
    hidden, bias_row = hyper_forward(hyper_params, wave_index[0], band_total)
    table = jnp.concatenate([band_count, wave_index[0]])
    tables = ordered_gather(table, "grp")
    (hidden_all, bias_row_all), hyper_pull = jax.vjp(
        lambda params: jax.vmap(lambda indices, total: hyper_forward(params, indices, total))(
            tables[:, 1:], tables[:, 0]
        ),
        hyper_params,
    )
    hidden_low = hidden.astype(jnp.bfloat16)
    kernel_rows = (
        jnp.einsum("be,pde->bpd", hidden_low, kernel_gen, preferred_element_type=jnp.float32)
        + kernel_gen_bias.astype(jnp.float32)[None]
    )
    kernel_shard = (kernel_rows * band_mask[:, None, None]).astype(jnp.bfloat16)
    cb_rows = conv_bias_gen.shape[0]
    small_flat = jnp.concatenate([conv_bias_gen.reshape(-1), small_flat])
    small_rows = -(-small_flat.shape[0] // (8 * model_width)) * 8
    small_flat = jnp.pad(small_flat, (0, small_rows * model_width - small_flat.shape[0]))
    shard_patch = kernel_gen.shape[0]
    kernel_rows_here = slot_count * shard_patch
    gathered = gather_shards(
        jnp.concatenate(
            [
                kernel_shard.reshape(kernel_rows_here, model_width),
                small_flat.reshape(small_rows, model_width),
            ]
        )
    )
    patch_kernels = (
        gathered[:, :kernel_rows_here]
        .reshape(shard_total, slot_count, shard_patch, model_width)
        .transpose(1, 0, 2, 3)
        .reshape(slot_count * patch, model_width)
    )
    small_vectors = gathered[:, kernel_rows_here:].reshape(shard_total, small_rows * model_width)
    cb_weight = small_vectors[:, : cb_rows * hyper_wide].reshape(shard_total * cb_rows, hyper_wide)
    unpacked = []
    small_at = cb_rows * hyper_wide
    for length in small_lengths:
        unpacked.append(small_vectors[:, small_at : small_at + length].reshape(-1))
        small_at += length
    (
        cb_shift,
        gain_one,
        shift_one,
        qv_full,
        proj_shift,
        gain_two,
        shift_two,
        fc1_shift,
        fc2_shift,
    ) = unpacked
    conv_shift = jnp.dot(
        cb_weight.astype(jnp.float32), bias_row, precision=highest_precision
    ) + cb_shift.astype(jnp.float32)
    pixel_rows = pad_rows(pixels.transpose(0, 2, 1, 3).reshape(images, tokens, slot_count * patch))
    stream = jnp.dot(pixel_rows, patch_kernels, preferred_element_type=jnp.float32) + conv_shift
    normed_one, norm_one_pull = jax.vjp(
        lambda values, norm_gain, norm_shift: layer_norm(values, norm_gain, norm_shift, norm_eps),
        stream,
        gain_one.astype(jnp.float32),
        shift_one.astype(jnp.float32),
    )
    normed_low = normed_one.astype(jnp.bfloat16)
    full_bias = jnp.concatenate(
        [
            qv_full[:model_width].astype(jnp.float32),
            jnp.zeros((model_width,), jnp.float32),
            qv_full[model_width:].astype(jnp.float32),
        ]
    )
    projected = (
        jnp.dot(normed_low, qkv_full, preferred_element_type=jnp.float32) + full_bias
    ).astype(jnp.bfloat16)
    attended, attn_probs = attention_forward(projected, images, tokens)
    middle = (
        stream
        + jnp.dot(attended, proj_full, preferred_element_type=jnp.float32)
        + proj_shift.astype(jnp.float32)
    )
    normed_two, norm_two_pull = jax.vjp(
        lambda values, norm_gain, norm_shift: layer_norm(values, norm_gain, norm_shift, norm_eps),
        middle,
        gain_two.astype(jnp.float32),
        shift_two.astype(jnp.float32),
    )
    normed_two_low = normed_two.astype(jnp.bfloat16)
    gate_in = jnp.dot(
        normed_two_low, fc1_full, preferred_element_type=jnp.float32
    ) + fc1_shift.astype(jnp.float32)
    activated, gelu_pull = jax.vjp(gelu_exact, gate_in)
    activated_low = activated.astype(jnp.bfloat16)
    block_out = (
        middle
        + jnp.dot(activated_low, fc2_full, preferred_element_type=jnp.float32)
        + fc2_shift.astype(jnp.float32)
    )
    upstream_low = pad_rows(cotangent)
    upstream = upstream_low.astype(jnp.float32)
    grad_fc2_shift = jnp.sum(upstream_low.astype(jnp.float32), axis=0)
    grad_fc2 = jnp.einsum(
        "tf,td->fd", activated_low, upstream_low, preferred_element_type=jnp.float32
    )
    grad_activated = jnp.einsum(
        "td,fd->tf", upstream_low, fc2_full, preferred_element_type=jnp.float32
    )
    (grad_gate,) = gelu_pull(grad_activated)
    gate_low = grad_gate.astype(jnp.bfloat16)
    grad_fc1_shift = jnp.sum(gate_low.astype(jnp.float32), axis=0)
    grad_fc1 = jnp.einsum("td,tf->df", normed_two_low, gate_low, preferred_element_type=jnp.float32)
    fc1_low = grad_fc1.astype(jnp.bfloat16)
    early_blocks = [
        fc1_low[:, at : at + model_width].reshape(group_total * shard_total, -1, model_width)
        for at in range(0, fc1_low.shape[1], model_width)
    ] + [grad_fc2.astype(jnp.bfloat16).reshape(group_total * shard_total, -1, model_width)]
    gate_low, early_block = lax.optimization_barrier(
        (gate_low, jnp.concatenate(early_blocks, axis=1))
    )
    early_sum = lax.psum_scatter(early_block, BOTH, scatter_dimension=0, tiled=True)[0]
    grad_normed_two = jnp.einsum(
        "tf,df->td", gate_low, fc1_full, preferred_element_type=jnp.float32
    )
    grad_middle_part, grad_gain_two, grad_shift_two = norm_two_pull(grad_normed_two)
    grad_middle = upstream + grad_middle_part
    middle_low = grad_middle.astype(jnp.bfloat16)
    grad_proj_shift = jnp.sum(middle_low.astype(jnp.float32), axis=0)
    grad_proj = jnp.einsum("td,te->de", attended, middle_low, preferred_element_type=jnp.float32)
    grad_attended = jnp.einsum(
        "te,de->td", middle_low, proj_full, preferred_element_type=jnp.float32
    ).astype(jnp.bfloat16)
    grad_projected, projected_sums = attention_backward(
        projected, attn_probs, grad_attended, images
    )
    projected_sums = jnp.sum(projected_sums, axis=0)
    grad_qv = jnp.concatenate([projected_sums[:model_width], projected_sums[2 * model_width :]])
    grad_qkv = jnp.einsum(
        "td,te->de", normed_low, grad_projected, preferred_element_type=jnp.float32
    )
    grad_normed_one = jnp.einsum(
        "te,de->td", grad_projected, qkv_full, preferred_element_type=jnp.float32
    )
    grad_stream_part, grad_gain_one, grad_shift_one = norm_one_pull(grad_normed_one)
    residual_reduced = (grad_middle + grad_stream_part).astype(jnp.bfloat16)
    grad_conv_shift = jnp.sum(residual_reduced.astype(jnp.float32), axis=0)
    grad_kernels = jnp.einsum(
        "tk,td->kd", pixel_rows, residual_reduced, preferred_element_type=jnp.float32
    ).astype(jnp.bfloat16)
    grad_pixels = jnp.einsum(
        "td,kd->tk", residual_reduced, patch_kernels, preferred_element_type=jnp.float32
    )
    grad_pixels = (
        grad_pixels.reshape(images, padded, slot_count, patch)[:, :tokens].transpose(0, 2, 1, 3)
    )
    grad_bias_row_part = jnp.dot(
        grad_conv_shift, cb_weight.astype(jnp.float32), precision=highest_precision
    )
    group_kernels = scatter_shards(
        grad_kernels.reshape(slot_count, shard_total, shard_patch, model_width).transpose(1, 0, 2, 3)
    )
    grad_pre = group_kernels * band_mask[:, None, None]
    grad_hidden_part = jnp.einsum(
        "bpd,pde->be", grad_pre, kernel_gen.astype(jnp.float32), precision=highest_precision
    )
    code_grads = jnp.concatenate([grad_hidden_part, grad_bias_row_part[None]])
    code_grads = jnp.sum(ordered_gather(code_grads, "img"), axis=0)
    code_grads = ordered_gather(code_grads, "grp")
    (hyper_total,) = hyper_pull((code_grads[:, :slot_count], code_grads[:, slot_count]))
    group_width = model_width // group_total
    swapped = lax.all_to_all(
        grad_pre.reshape(slot_count, shard_patch, group_total, group_width).transpose(2, 0, 1, 3),
        "grp",
        0,
        0,
    ).reshape(group_total * slot_count, shard_patch, group_width)
    code_all = hidden_all.astype(jnp.bfloat16).astype(jnp.float32)
    grad_gen = jnp.einsum(
        "kpd,ke->pde",
        swapped,
        code_all.reshape(group_total * slot_count, hyper_wide),
        precision=highest_precision,
    )
    grad_gen_shift = jnp.sum(swapped, axis=0)
    device_total = group_total * shard_total
    own_group = (jnp.arange(group_total) == group_at).astype(jnp.float32)
    vectors = [
        grad_gain_one,
        grad_shift_one,
        grad_qv,
        grad_proj_shift,
        grad_gain_two,
        grad_shift_two,
        grad_fc1_shift,
        grad_fc2_shift,
    ] + [grad_conv_shift * own_group[group] for group in range(group_total)]
    vector_block = jnp.concatenate(
        [member.reshape(device_total, -1) for member in vectors], axis=1
    ).astype(jnp.bfloat16)
    vector_lengths = [member.shape[0] // device_total for member in vectors]
    block_rows = model_width // device_total

    def blocks_of(value):
        value = value.astype(jnp.bfloat16)
        return [
            value[:, at : at + model_width].reshape(device_total, -1, model_width)
            for at in range(0, value.shape[1], model_width)
        ]

    late = blocks_of(grad_qkv) + blocks_of(grad_proj)
    late_rows = sum(member.shape[1] for member in late)
    extra = -(-vector_block.shape[1] // model_width)
    extra += -(late_rows + extra) % 8
    vector_block = jnp.pad(
        vector_block, ((0, 0), (0, extra * model_width - vector_block.shape[1]))
    ).reshape(device_total, extra, model_width)
    late_out = scatter_all(jnp.concatenate(late + [vector_block], axis=1))
    early_out = early_sum.astype(jnp.float32)

    def columns_of(value, total):
        return jnp.concatenate(
            [value[at * block_rows : (at + 1) * block_rows] for at in range(total)], axis=1
        )

    fc1_out = columns_of(early_out, grad_fc1.shape[1] // model_width)
    fc2_out = early_out[fc1_out.size // model_width :]
    qkv_out = columns_of(late_out, 3)
    proj_out = late_out[3 * block_rows : 4 * block_rows]
    vector_out = late_out[4 * block_rows :].reshape(-1)
    parts = []
    vector_at = 0
    for length in vector_lengths:
        parts.append(vector_out[vector_at : vector_at + length])
        vector_at += length
    conv_parts = jnp.stack(parts[8:])
    grad_cb_weight = jnp.dot(conv_parts.T, bias_row_all, precision=highest_precision)
    reduced = (
        grad_cb_weight,
        jnp.sum(conv_parts, axis=0),
        parts[0],
        parts[1],
        qkv_out,
        parts[2],
        proj_out,
        parts[3],
        parts[4],
        parts[5],
        fc1_out,
        parts[6],
        fc2_out,
        parts[7],
    )
    return (
        block_out.reshape(images, padded, model_width)[:, :tokens],
        grad_pixels,
        hyper_total[0],
        hyper_total[1],
        hyper_total[2],
        hyper_total[3],
        hyper_total[4],
        hyper_total[5],
        hyper_total[6],
        hyper_total[7],
        hyper_total[8],
        hyper_total[9],
        hyper_total[10],
        hyper_total[11],
        hyper_total[12],
        hyper_total[13],
        grad_gen,
        grad_gen_shift,
        reduced[0],
        reduced[1],
        reduced[2],
        reduced[3],
        reduced[4],
        reduced[5],
        reduced[6],
        reduced[7],
        reduced[8],
        reduced[9],
        reduced[10],
        reduced[11],
        reduced[12],
        reduced[13],
    )


def solution(mesh):
    return jax.shard_map(
        local,
        mesh=mesh,
        in_specs=(
            P(("grp", "img"), None, None, None),
            P(("grp", "img"), None, None),
            P("grp"),
            P("grp", None),
            P(),
            P(),
            P(),
            P(),
            P(),
            P(),
            P(),
            P(),
            P(),
            P(),
            P(),
            P(),
            P(),
            P(),
            P("img", None, None),
            P("img", None),
            P("img", None),
            P("img"),
            P("img"),
            P("img"),
            P("img", None),
            P("img"),
            P("img", None),
            P("img"),
            P("img"),
            P("img"),
            P("img", None),
            P("img"),
            P("img", None),
            P("img"),
        ),
        out_specs=(
            P(("grp", "img"), None, None),
            P(("grp", "img"), None, None, None),
            P(),
            P(),
            P(),
            P(),
            P(),
            P(),
            P(),
            P(),
            P(),
            P(),
            P(),
            P(),
            P(),
            P(),
            P("img", "grp", None),
            P("img", "grp"),
            P(("grp", "img"), None),
            P(("grp", "img")),
            P(("grp", "img")),
            P(("grp", "img")),
            P(("grp", "img"), None),
            P(("grp", "img")),
            P(("grp", "img"), None),
            P(("grp", "img")),
            P(("grp", "img")),
            P(("grp", "img")),
            P(("grp", "img"), None),
            P(("grp", "img")),
            P(("grp", "img"), None),
            P(("grp", "img")),
        ),
        check_vma=False,
    )
```

```python
import functools

import jax
import jax.numpy as jnp
from jax import lax
from jax.experimental import pallas as pl
from jax.experimental.pallas import tpu as pltpu
from jax.sharding import PartitionSpec as P

HEADS = 12
WHEADS = 4
WAVES = 256


norm_eps = 1e-06
hyper_eps = 1e-05
highest_precision = lax.Precision.HIGHEST


def layer_norm(values, norm_gain, norm_shift, epsilon):
    centre = values - jnp.mean(values, axis=-1, keepdims=True)
    spread = jnp.mean(centre * centre, axis=-1, keepdims=True)
    return centre * lax.rsqrt(spread + epsilon) * norm_gain + norm_shift


def gelu_exact(values):
    return jax.nn.gelu(values, approximate=False)


def wave_embed(indices, hyper_width):
    half_model_width = hyper_width // 2
    wavelength = 400.0 + 2100.0 * indices.astype(jnp.float32) / (WAVES - 1)
    frequency = 1.0 / 10000.0 ** (
        jnp.arange(half_model_width, dtype=jnp.float32) / half_model_width
    )
    angles = wavelength[:, None] * frequency[None, :]
    return jnp.concatenate([jnp.sin(angles), jnp.cos(angles)], axis=-1)


def hyper_forward(params, indices, band_total):
    (
        tokens,
        bias_tok,
        qkv_w,
        qv_b,
        out_w,
        out_b,
        gain_one,
        shift_one,
        ff_in,
        ff_in_b,
        ff_out,
        ff_out_b,
        gain_two,
        shift_two,
    ) = params
    hyper_width = tokens.shape[1]
    slot_count = indices.shape[0]
    token_rows = tokens.shape[0]
    head_dim = hyper_width // WHEADS
    waves = wave_embed(indices, hyper_width)
    joined = jnp.concatenate([tokens, waves, bias_tok[None, :]], axis=0)
    query_rows = joined[token_rows:]
    queries = (
        jnp.dot(query_rows, qkv_w[:, :hyper_width], precision=highest_precision)
        + qv_b[:hyper_width]
    ).reshape(slot_count + 1, WHEADS, head_dim)
    key_rows = jnp.dot(
        joined, qkv_w[:, hyper_width : 2 * hyper_width], precision=highest_precision
    ).reshape(-1, WHEADS, head_dim)
    values = (
        jnp.dot(joined, qkv_w[:, 2 * hyper_width :], precision=highest_precision)
        + qv_b[hyper_width:]
    ).reshape(-1, WHEADS, head_dim)
    scores = jnp.einsum(
        "qhd,khd->hqk", queries, key_rows, precision=highest_precision
    ) * head_dim ** (-0.5)
    offsets = jnp.arange(joined.shape[0]) - token_rows
    usable = (offsets < band_total) | (offsets == slot_count)
    scores = jnp.where(usable[None, None, :], scores, -1e30)
    weights = jax.nn.softmax(scores, axis=-1)
    mixture = jnp.einsum("hqk,khd->qhd", weights, values, precision=highest_precision).reshape(
        slot_count + 1, hyper_width
    )
    normed_one = layer_norm(
        query_rows + jnp.dot(mixture, out_w, precision=highest_precision) + out_b,
        gain_one,
        shift_one,
        hyper_eps,
    )
    hidden = gelu_exact(jnp.dot(normed_one, ff_in, precision=highest_precision) + ff_in_b)
    normed_two = layer_norm(
        normed_one + jnp.dot(hidden, ff_out, precision=highest_precision) + ff_out_b,
        gain_two,
        shift_two,
        hyper_eps,
    )
    return (normed_two[:slot_count] + waves, normed_two[slot_count])


BOTH = ("grp", "img")


def torus_block():
    return lax.axis_size("grp") == 4 and lax.axis_size("img") == 8


def flipped(index, bit):
    return index ^ bit


def swap(value, bit):
    return lax.ppermute(value, BOTH, [(i, i ^ bit) for i in range(32)])


def along_z(value, step, senders):
    moves = [(i, i + 2 * step) for i in range(32) if (i % 8) // 2 in senders]
    return lax.ppermute(value, BOTH, moves)


def pick(value, index, axis=0):
    return lax.dynamic_index_in_dim(value, index, axis, keepdims=False)


def add_low(left, right):
    return (left.astype(jnp.float32) + right.astype(jnp.float32)).astype(jnp.bfloat16)


def z_index():
    return (lax.axis_index("img") // 2).astype(jnp.int32)


def scatter_step(chunks, held, step):
    z = z_index()
    up_term = pick(chunks, jnp.clip(4 - step + z, 0, 3))
    down_term = pick(chunks, jnp.clip(z - 4 + step, 0, 3))
    if held is not None:
        up_term = add_low(up_term, held[0])
        down_term = add_low(down_term, held[1])
    return along_z(up_term, 1, range(step)), along_z(down_term, -1, range(4 - step, 4))


def scatter_end(chunks, held):
    own = pick(chunks, z_index())
    return own.astype(jnp.float32) + held[0].astype(jnp.float32) + held[1].astype(jnp.float32)


def gather_step(held, step):
    return along_z(held[0], 1, range(step - 1, 3)), along_z(held[1], -1, range(1, 5 - step))


def gather_end(own, steps):
    z = z_index()
    by_offset = {0: own}
    for at, (up, down) in enumerate(steps):
        by_offset[-1 - at] = up
        by_offset[1 + at] = down
    rows = []
    for place in range(4):
        row = by_offset[place]
        for z_at in range(1, 4):
            row = jnp.where(z == z_at, by_offset[place - z_at], row)
        rows.append(row)
    return jnp.stack(rows)


def in_order(bit, own, other, axis):
    return jnp.stack(
        [jnp.where(bit == 0, own, other), jnp.where(bit == 0, other, own)], axis=axis
    )


def together(*values):
    return lax.optimization_barrier(values)


def core_half(value, axis):
    core = lax.axis_index("img") % 2
    return pick(value, core, axis), pick(value, 1 - core, axis)


def gather_small(value):
    if not torus_block():
        return lax.all_gather(value, "img", axis=0, tiled=False)
    shard = lax.axis_index("img")
    value = in_order(shard % 2, value, swap(value, 1), 0)
    value = in_order(shard // 2 % 2, value, swap(value, 2), 0)
    value = in_order(shard // 4, value, swap(value, 4), 0)
    return value.reshape((8,) + value.shape[3:])


def gather_hidden(fc1_weight, fc2_weight):
    shard, hidden = fc1_weight.shape
    width = fc2_weight.shape[1]
    part = hidden // 4
    if not torus_block():
        fc1 = lax.all_gather(fc1_weight, "img", axis=0, tiled=True)
        fc2 = lax.all_gather(fc2_weight, "img", axis=0, tiled=True)
        fc1 = fc1.reshape(8, -1, 4, part).transpose(2, 0, 1, 3)
        fc2 = fc2.reshape(8, 4, -1, width).transpose(1, 0, 2, 3)
        return jnp.concatenate([fc1, fc2], axis=2)
    group = lax.axis_index("grp")
    own = jnp.concatenate(
        [
            lax.dynamic_slice_in_dim(fc1_weight, group * part, part, 1),
            lax.dynamic_slice_in_dim(fc2_weight, group * shard, shard, 0),
        ]
    )
    return lax.all_gather(own, BOTH, axis=0, tiled=False).reshape(4, 8, 2 * shard, width)


def gather_kernels(kernels, rows_call):
    if not torus_block():
        kernels = lax.all_gather(kernels, "img", axis=0, tiled=False)
        kernels = kernels.reshape((-1, 2) + kernels.shape[1:])
        return core_half(kernels, 1) + (rows_call(None),)
    one = gather_step((kernels, kernels), 1)
    rows = rows_call(kernels)
    one, rows = together(one, rows)
    two = gather_step(one, 2)
    three = gather_step(two, 3)
    line = gather_end(kernels, [one, two, three])
    return line, swap(line, 1), rows


def start_late(late, later):
    if not torus_block():
        late = lax.psum_scatter(late, BOTH, scatter_dimension=0, tiled=True)[0]
        return late.astype(jnp.float32), later
    keep, send = core_half(late.reshape((2, 2, 4, 2) + late.shape[1:]), 3)
    send_in = swap(send, 1)
    keep, later = together(keep, later)
    return (keep, send_in), later


def reduce_late(grad_kernels, late, code_call, fill_calls, gen_call):
    if not torus_block():
        kernels = lax.psum_scatter(grad_kernels, "img", scatter_dimension=0, tiled=True)[0]
        kernels = kernels.astype(jnp.float32)
        code = jnp.sum(ordered_gather(code_call(kernels), "img"), axis=0)
        filled = [call(None) for call in fill_calls] + [gen_call(kernels)]
        return lambda tie: late, ordered_gather(code, "grp"), filled
    group = lax.axis_index("grp")
    x, y = group % 2, group // 2
    shape = grad_kernels.shape
    keep, send = core_half(grad_kernels.reshape(4, 2, shape[1] * shape[2], shape[3]), 1)
    send_in = swap(send, 1)
    late = add_low(*late)
    send_in, late = together(send_in, late)
    chunks = add_low(keep, send_in)
    kernels_one = scatter_step(chunks, None, 1)
    first, second = late[:, :, :2], late[:, :, 2:]
    first_in = swap(pick(first, 1 - x, 1), 8)
    second_in = swap(pick(second, 1 - y, 0), 16)
    filled = [fill_calls[0](chunks)]
    kernels_one, filled[0] = together(kernels_one, filled[0])
    kernels_two = scatter_step(chunks, kernels_one, 2)
    filled.append(fill_calls[1](kernels_one))
    kernels_two, first_in, second_in, filled[1] = together(
        kernels_two, first_in, second_in, filled[1]
    )
    kernels_three = scatter_step(chunks, kernels_two, 3)
    first = add_low(pick(first, x, 1), first_in)
    second = add_low(pick(second, y, 0), second_in)
    first_in = swap(pick(first, 1 - y), 16)
    second_in = swap(pick(second, 1 - x), 8)
    kernels = scatter_end(chunks, kernels_three).reshape(shape[1:])
    code = code_call(kernels)
    code = code + swap(code, 1)
    code = code + swap(code, 2)
    code, kernels, first_in, second_in = together(code, kernels, first_in, second_in)
    code_in = swap(code, 4)
    late = jnp.concatenate(
        [add_low(pick(first, y), first_in), add_low(pick(second, x), second_in)]
    )
    late_one = scatter_step(late, None, 1)
    code = code + code_in
    code = in_order(x, code, swap(code, 8), 0)
    code = in_order(y, code, swap(code, 16), 0).reshape((4,) + code.shape[1:])
    code, kernels, late_one = together(code, kernels, late_one)
    late_two = scatter_step(late, late_one, 2)
    filled.append(gen_call(kernels))

    def late_end(tie):
        late_here, _ = together(late_two, tie)
        return scatter_end(late, scatter_step(late, late_here, 3))

    return late_end, code, filled


def lane_half(shape):
    return lax.broadcasted_iota(jnp.int32, shape, len(shape) - 1) % 128 < 64


def attention_forward_kernel(tokens, projected_ref, attended_ref, probs_ref):
    _, rows, width = projected_ref.shape
    low_half = lane_half((rows, 128))
    real_key = lax.broadcasted_iota(jnp.int32, (rows, rows), 0) < tokens
    for pair in range(width // 128):
        at = pair * 128
        queries = projected_ref[0, :, at : at + 128] * jnp.bfloat16(0.125)
        key_rows = projected_ref[1, :, at : at + 128]
        values = projected_ref[2, :, at : at + 128]
        halves = []
        for half in range(2):
            chosen = low_half if half == 0 else ~low_half
            own_queries = jnp.where(chosen, queries, jnp.bfloat16(0))
            scores = lax.dot_general(
                key_rows, own_queries, (((1,), (1,)), ((), ())), preferred_element_type=jnp.float32
            )
            scores = jnp.where(real_key, scores, -1e30)
            raised = jnp.exp(scores - jnp.max(scores, axis=0, keepdims=True))
            probs = raised * (1.0 / jnp.sum(raised, axis=0, keepdims=True))
            probs = probs.astype(jnp.bfloat16)
            probs_ref[2 * pair + half] = probs
            halves.append(
                lax.dot_general(
                    probs, values, (((0,), (0,)), ((), ())), preferred_element_type=jnp.float32
                )
            )
        attended_ref[:, at : at + 128] = jnp.where(low_half, halves[0], halves[1]).astype(
            jnp.bfloat16
        )


def attention_forward(projected, images, tokens):
    _, total, width = projected.shape
    rows = total // images
    heads = width // 64
    return pl.pallas_call(
        functools.partial(attention_forward_kernel, tokens),
        grid=(images,),
        in_specs=[pl.BlockSpec((3, rows, width), lambda i: (0, i, 0))],
        out_specs=[
            pl.BlockSpec((rows, width), lambda i: (i, 0)),
            pl.BlockSpec((None, heads, rows, rows), lambda i: (i, 0, 0, 0)),
        ],
        out_shape=[
            jax.ShapeDtypeStruct((images * rows, width), jnp.bfloat16),
            jax.ShapeDtypeStruct((images, heads, rows, rows), jnp.bfloat16),
        ],
        compiler_params=pltpu.CompilerParams(vmem_limit_bytes=48 << 20),
        cost_estimate=pl.CostEstimate(
            flops=images * heads * rows * rows * 64 * 4,
            bytes_accessed=images * rows * (8 * width + 2 * heads * rows),
            transcendentals=images * heads * rows * rows,
        ),
        name="attention_forward",
    )(projected)


def attention_backward_kernel(projected_ref, probs_ref, grad_ref, out_ref, sums_ref):
    _, rows, width = projected_ref.shape
    low_half = lane_half((rows, 128))

    @pl.when(pl.program_id(0) == 0)
    def _():
        sums_ref[...] = jnp.zeros_like(sums_ref)

    for pair in range(width // 128):
        at = pair * 128
        queries = projected_ref[0, :, at : at + 128]
        key_rows = projected_ref[1, :, at : at + 128]
        values = projected_ref[2, :, at : at + 128]
        grads = grad_ref[:, at : at + 128]
        found = []
        for half in range(2):
            chosen = low_half if half == 0 else ~low_half
            probs = probs_ref[2 * pair + half]
            own_grads = jnp.where(chosen, grads, jnp.bfloat16(0))
            grad_values = jnp.dot(probs, grads, preferred_element_type=jnp.float32)
            grad_probs = lax.dot_general(
                values, own_grads, (((1,), (1,)), ((), ())), preferred_element_type=jnp.float32
            )
            wide = probs.astype(jnp.float32)
            weighted = grad_probs * wide
            total = jnp.sum(weighted, axis=0, keepdims=True)
            grad_scores = (weighted - wide * total).astype(jnp.bfloat16)
            grad_keys = jnp.dot(grad_scores, queries, preferred_element_type=jnp.float32) * 0.125
            grad_queries = (
                lax.dot_general(
                    grad_scores,
                    key_rows,
                    (((0,), (0,)), ((), ())),
                    preferred_element_type=jnp.float32,
                )
                * 0.125
            )
            found.append((grad_queries, grad_keys, grad_values))
        for kind in range(3):
            joined = jnp.where(low_half, found[0][kind], found[1][kind]).astype(jnp.bfloat16)
            place = slice(at, at + 128)
            out_ref[kind, :, place] = joined
            sums_ref[kind, :, place] += jnp.sum(
                joined.astype(jnp.float32).reshape(rows // 8, 8, 128), axis=0
            )


def attention_backward(projected, probs, grad_attended, images):
    _, total, width = projected.shape
    rows = total // images
    heads = width // 64
    return pl.pallas_call(
        attention_backward_kernel,
        grid=(images,),
        in_specs=[
            pl.BlockSpec((3, rows, width), lambda i: (0, i, 0)),
            pl.BlockSpec((None, heads, rows, rows), lambda i: (i, 0, 0, 0)),
            pl.BlockSpec((rows, width), lambda i: (i, 0)),
        ],
        out_specs=[
            pl.BlockSpec((3, rows, width), lambda i: (0, i, 0)),
            pl.BlockSpec((3, 8, width), lambda i: (0, 0, 0)),
        ],
        out_shape=[
            jax.ShapeDtypeStruct((3, total, width), jnp.bfloat16),
            jax.ShapeDtypeStruct((3, 8, width), jnp.float32),
        ],
        compiler_params=pltpu.CompilerParams(vmem_limit_bytes=48 << 20),
        cost_estimate=pl.CostEstimate(flops=0, bytes_accessed=0, transcendentals=0),
        name="attention_backward",
    )(projected, probs, grad_attended)


SLOT_ROWS = 16


def exact_dot(left, right, contract=((1,), (0,))):
    return lax.dot_general(
        left,
        right,
        (contract, ((), ())),
        precision=highest_precision,
        preferred_element_type=jnp.float32,
    )


def rows_norm(values, norm_gain, norm_shift, epsilon):
    centre = values - jnp.mean(values, axis=-1, keepdims=True)
    spread = jnp.mean(centre * centre, axis=-1, keepdims=True)
    return centre * lax.rsqrt(spread + epsilon) * norm_gain + norm_shift


def gelu_rows(values):
    return values * (0.5 + 0.5 * lax.erf(values * 0.7071067811865476))


def hyper_rows(params, waves, usable, slots):
    (
        tokens,
        bias_tok,
        qkv_w,
        qv_b,
        out_w,
        out_b,
        gain_one,
        shift_one,
        ff_in,
        ff_in_b,
        ff_out,
        ff_out_b,
        gain_two,
        shift_two,
    ) = params
    width = tokens.shape[1]
    head_dim = width // WHEADS
    total = waves.shape[0]
    place = lax.broadcasted_iota(jnp.int32, (total, 1), 0) & (SLOT_ROWS - 1)
    query_rows = jnp.where(place == slots, jnp.broadcast_to(bias_tok, (total, width)), waves)
    joined = jnp.concatenate([tokens, query_rows], axis=0)
    queries = exact_dot(query_rows, qkv_w[:, :width]) + qv_b[:, :width]
    key_rows = exact_dot(joined, qkv_w[:, width : 2 * width])
    values = exact_dot(joined, qkv_w[:, 2 * width :]) + qv_b[:, width:]
    head_at = lax.broadcasted_iota(jnp.int32, (1, width), 1)
    mixture = jnp.zeros((total, width), jnp.float32)
    for head in range(WHEADS):
        own = ((head_at >= head * head_dim) & (head_at < (head + 1) * head_dim)).astype(jnp.float32)
        scores = exact_dot(queries * own, key_rows, ((1,), (1,))) * head_dim ** (-0.5)
        scores = jnp.where(usable > 0, scores, -1e30)
        raised = jnp.exp(scores - lax.stop_gradient(jnp.max(scores, axis=-1, keepdims=True)))
        weights = raised / jnp.sum(raised, axis=-1, keepdims=True)
        mixture = mixture + exact_dot(weights, values) * own
    first = rows_norm(query_rows + exact_dot(mixture, out_w) + out_b, gain_one, shift_one, hyper_eps)
    hidden = gelu_rows(exact_dot(first, ff_in) + ff_in_b)
    return rows_norm(first + exact_dot(hidden, ff_out) + ff_out_b, gain_two, shift_two, hyper_eps)


def usable_rows(band_counts, slots, token_rows):
    groups = band_counts.shape[0]
    total = groups * SLOT_ROWS
    row = jnp.arange(total)
    own_group = row[:, None] // SLOT_ROWS == row[None, :] // SLOT_ROWS
    place = row % SLOT_ROWS
    present = (place < jnp.repeat(band_counts, SLOT_ROWS)) | (place == slots)
    return jnp.concatenate(
        [jnp.ones((total, token_rows)), (own_group & present[None, :]).astype(jnp.float32)], axis=1
    )


def hyper_params_2d(params):
    return tuple(member[None] if member.ndim == 1 else member for member in params)


def wave_rows(indices, width):
    groups, slots = indices.shape
    waves = jax.vmap(lambda row: wave_embed(row, width))(indices)
    return jnp.pad(waves, ((0, 0), (0, SLOT_ROWS - slots), (0, 0))).reshape(-1, width)


def hyper_forward_kernel(slots, waves_ref, usable_ref, *refs):
    refs[-1][...] = hyper_rows(
        tuple(ref[...] for ref in refs[:-1]), waves_ref[...], usable_ref[...], slots
    )


def hyper_backward_kernel(slots, waves_ref, usable_ref, grads_ref, *refs):
    count = len(refs) // 2
    waves, usable = waves_ref[...], usable_ref[...]
    _, pull = jax.vjp(
        lambda params: hyper_rows(params, waves, usable, slots),
        tuple(ref[...] for ref in refs[:count]),
    )
    (found,) = pull(grads_ref[...])
    for ref, value in zip(refs[count:], found):
        ref[...] = value


def hyper_forward_call(params, waves, usable, slots):
    return pl.pallas_call(
        functools.partial(hyper_forward_kernel, slots),
        out_shape=jax.ShapeDtypeStruct(waves.shape, jnp.float32),
        name="hyper_forward",
    )(waves, usable, *params)


def hyper_backward_call(params, waves, usable, grads, slots):
    return pl.pallas_call(
        functools.partial(hyper_backward_kernel, slots),
        out_shape=[jax.ShapeDtypeStruct(member.shape, jnp.float32) for member in params],
        name="hyper_backward",
    )(waves, usable, grads, *params)


def embed_kernel(
    bands, small_at, core_ref, line_ref, other_ref, pixels_ref, kernels_ref, stream_ref, normed_ref, rows_ref
):
    chips, _, width = line_ref.shape
    part = kernels_ref.shape[0] // (2 * chips * bands)
    shard = width // (2 * chips)

    @pl.when(pl.program_id(0) == 0)
    def _():
        for core in range(2):
            low_ref, high_ref = (line_ref, other_ref) if core == 0 else (other_ref, line_ref)

            @pl.when((core_ref[0] == 0) == (core == 0))
            def _():
                for chip in range(chips):
                    for band in range(bands):
                        place = (band * chips + chip) * 2 * part
                        here = slice(band * part, (band + 1) * part)
                        kernels_ref[place : place + part] = low_ref[chip, here]
                        kernels_ref[place + part : place + 2 * part] = high_ref[chip, here]
                    for which, ref in enumerate((low_ref, high_ref)):
                        small = ref[chip, small_at : small_at + 16, :shard].astype(jnp.float32)
                        at = (chip * 2 + which) * shard
                        rows_ref[:, at : at + shard] = small

    shift = rows_ref[0:1] + rows_ref[1:2]
    stream = (
        jnp.dot(pixels_ref[...], kernels_ref[...], preferred_element_type=jnp.float32) + shift
    )
    stream_ref[...] = stream
    centre = stream - jnp.mean(stream, axis=-1, keepdims=True)
    spread = jnp.mean(centre * centre, axis=-1, keepdims=True)
    normed = centre * lax.rsqrt(spread + norm_eps) * rows_ref[2:3] + rows_ref[3:4]
    normed_ref[...] = normed.astype(jnp.bfloat16)


def embed(core, line, other, pixel_rows, images, bands, small_at):
    width = line.shape[2]
    total, depth = pixel_rows.shape
    rows = total // images
    part_spec = pl.BlockSpec(line.shape, lambda i, core_ref: (0, 0, 0))
    row = pl.BlockSpec((rows, width), lambda i, core_ref: (i, 0))
    return pl.pallas_call(
        functools.partial(embed_kernel, bands, small_at),
        grid_spec=pltpu.PrefetchScalarGridSpec(
            num_scalar_prefetch=1,
            grid=(images,),
            in_specs=[
                part_spec,
                part_spec,
                pl.BlockSpec((rows, depth), lambda i, core_ref: (i, 0)),
            ],
            out_specs=[pl.BlockSpec((depth, width), lambda i, core_ref: (0, 0)), row, row],
            scratch_shapes=[pltpu.VMEM((16, width), jnp.float32)],
        ),
        out_shape=[
            jax.ShapeDtypeStruct((depth, width), jnp.bfloat16),
            jax.ShapeDtypeStruct((total, width), jnp.float32),
            jax.ShapeDtypeStruct((total, width), jnp.bfloat16),
        ],
        compiler_params=pltpu.CompilerParams(vmem_limit_bytes=48 << 20),
        cost_estimate=pl.CostEstimate(
            flops=2 * total * width * depth,
            bytes_accessed=total * (2 * depth + 6 * width) + 4 * depth * width,
            transcendentals=total,
        ),
        name="embed",
    )(core, line, other, pixel_rows)


def first_backward_kernel(
    projected_ref,
    query_ref,
    key_ref,
    value_ref,
    stream_ref,
    residual_ref,
    gain_ref,
    pixels_ref,
    out_ref,
    kernels_ref,
    sums_ref,
    total_ref,
):
    rows, width = stream_ref.shape
    shards, bands, part, _ = kernels_ref.shape

    @pl.when(pl.program_id(0) == 0)
    def _():
        sums_ref[...] = jnp.zeros_like(sums_ref)
        total_ref[...] = jnp.zeros_like(total_ref)

    def folded(value):
        return jnp.sum(value.reshape(rows // 8, 8, width), axis=0)

    grads = sum(
        lax.dot_general(
            projected_ref[at],
            ref[...],
            (((1,), (1,)), ((), ())),
            preferred_element_type=jnp.float32,
        )
        for at, ref in enumerate((query_ref, key_ref, value_ref))
    )
    stream = stream_ref[...]
    centre = stream - jnp.mean(stream, axis=-1, keepdims=True)
    spread = jnp.mean(centre * centre, axis=-1, keepdims=True)
    scale = lax.rsqrt(spread + norm_eps)
    normed = centre * scale
    sums_ref[0] += folded(grads * normed)
    sums_ref[1] += folded(grads)
    grads = grads * gain_ref[...]
    grads = scale * (
        grads
        - jnp.mean(grads, axis=-1, keepdims=True)
        - normed * jnp.mean(grads * normed, axis=-1, keepdims=True)
    )
    low = (residual_ref[...] + grads).astype(jnp.bfloat16)
    out_ref[...] = low
    sums_ref[2] += folded(low.astype(jnp.float32))
    total_ref[...] += lax.dot_general(
        pixels_ref[...], low, (((0,), (0,)), ((), ())), preferred_element_type=jnp.float32
    )

    @pl.when(pl.program_id(0) == pl.num_programs(0) - 1)
    def _():
        for shard in range(shards):
            for band in range(bands):
                place = (band * shards + shard) * part
                kernels_ref[shard, band] = total_ref[place : place + part].astype(jnp.bfloat16)


def first_backward(grad_projected, weights, stream, residual, gain, pixel_rows, images, shards, bands):
    total, width = stream.shape
    rows = total // images
    depth = pixel_rows.shape[1]
    row = pl.BlockSpec((rows, width), lambda i: (i, 0))
    made = (shards, bands, depth // (shards * bands), width)
    return pl.pallas_call(
        first_backward_kernel,
        grid=(images,),
        in_specs=[
            pl.BlockSpec((3, rows, width), lambda i: (0, i, 0)),
            pl.BlockSpec((width, width), lambda i: (0, 0)),
            pl.BlockSpec((width, width), lambda i: (0, 1)),
            pl.BlockSpec((width, width), lambda i: (0, 2)),
            row,
            row,
            pl.BlockSpec((1, width), lambda i: (0, 0)),
            pl.BlockSpec((rows, depth), lambda i: (i, 0)),
        ],
        out_specs=[
            row,
            pl.BlockSpec(made, lambda i: (0, 0, 0, 0)),
            pl.BlockSpec((3, 8, width), lambda i: (0, 0, 0)),
        ],
        out_shape=[
            jax.ShapeDtypeStruct((total, width), jnp.bfloat16),
            jax.ShapeDtypeStruct(made, jnp.bfloat16),
            jax.ShapeDtypeStruct((3, 8, width), jnp.float32),
        ],
        scratch_shapes=[pltpu.VMEM((depth, width), jnp.float32)],
        compiler_params=pltpu.CompilerParams(vmem_limit_bytes=48 << 20),
        cost_estimate=pl.CostEstimate(flops=0, bytes_accessed=0, transcendentals=0),
        name="first_backward",
    )(grad_projected, weights, weights, weights, stream, residual, gain, pixel_rows)


def mlp_kernel(
    block,
    devices,
    rows_ref,
    upstream_ref,
    first_weight_ref,
    second_weight_ref,
    b1_ref,
    sums_ref,
    out_ref,
    grad_ref,
    packed_ref,
    turned_ref,
    act_ref,
    gate_ref,
    first_ref,
    second_ref,
    sems,
):
    at_step = pl.program_id(0)
    steps = pl.num_programs(0)
    total, width = rows_ref.shape
    eighths, shard, hidden_block = first_weight_ref.shape
    quarters, group, _, _ = second_weight_ref.shape
    w1 = first_weight_ref[...].reshape(width, hidden_block)
    w2 = jnp.concatenate(
        [second_weight_ref[at, eighth] for eighth in range(group) for at in range(quarters)]
    )
    first_rows = width // devices
    second_devices = devices // steps
    second_rows = hidden_block // second_devices

    def copies(step):
        return (
            pltpu.make_async_copy(
                first_ref, packed_ref.at[:, pl.ds(step * first_rows, first_rows), :], sems.at[0]
            ),
            pltpu.make_async_copy(
                second_ref,
                packed_ref.at[
                    pl.ds(step * second_devices, second_devices),
                    pl.ds(steps * first_rows, second_rows),
                    :,
                ],
                sems.at[1],
            ),
        )

    @pl.when(at_step == 0)
    def _():
        out_ref[...] = jnp.zeros_like(out_ref)
        grad_ref[...] = jnp.zeros_like(grad_ref)
        turned_ref[...] = rows_ref[...].T

    for at in range(0, total, block):
        here = slice(at, at + block)
        gate_in = (
            jnp.dot(rows_ref[here], w1, preferred_element_type=jnp.float32) + b1_ref[...]
        )
        grad_act = lax.dot_general(
            upstream_ref[here],
            w2,
            (((1,), (1,)), ((), ())),
            preferred_element_type=jnp.float32,
        )
        chance = 0.5 + 0.5 * lax.erf(gate_in * 0.7071067811865476)
        density = 0.3989422804014327 * jnp.exp(-0.5 * gate_in * gate_in)
        act = (gate_in * chance).astype(jnp.bfloat16)
        gate = (grad_act * (chance + gate_in * density)).astype(jnp.bfloat16)
        act_ref[here] = act
        gate_ref[here] = gate
        wide = gate.astype(jnp.float32)
        part = jnp.sum(wide.reshape(block // 8, 8, wide.shape[1]), axis=0)
        sums_ref[...] = part if at == 0 else sums_ref[...] + part
        out_ref[here] += jnp.dot(act, w2, preferred_element_type=jnp.float32)
        grad_ref[here] += lax.dot_general(
            gate, w1, (((1,), (1,)), ((), ())), preferred_element_type=jnp.float32
        )

    @pl.when(at_step > 0)
    def _():
        for copy in copies(at_step - 1):
            copy.wait()

    first = jnp.dot(turned_ref[...], gate_ref[...], preferred_element_type=jnp.float32)
    first_ref[...] = first.astype(jnp.bfloat16).reshape(first_ref.shape)
    second = lax.dot_general(
        act_ref[...], upstream_ref[...], (((0,), (0,)), ((), ())), preferred_element_type=jnp.float32
    )
    second_ref[...] = second.astype(jnp.bfloat16).reshape(second_ref.shape)
    for copy in copies(at_step):
        copy.start()

    @pl.when(at_step == steps - 1)
    def _():
        for copy in copies(at_step):
            copy.wait()


def mlp(rows, upstream, weights, b1, row_block, devices):
    total, width = rows.shape
    steps, eighths, shard, hidden_block = weights.shape
    shard //= 2
    hidden = steps * hidden_block
    whole = pl.BlockSpec((total, width), lambda i: (0, 0))
    packed_rows = (width * steps + hidden) // devices
    return pl.pallas_call(
        functools.partial(mlp_kernel, row_block, devices),
        grid=(steps,),
        in_specs=[
            whole,
            whole,
            pl.BlockSpec((None, eighths, shard, hidden_block), lambda i: (i, 0, 0, 0)),
            pl.BlockSpec((steps, eighths // steps, shard, width), lambda i: (0, i, 1, 0)),
            pl.BlockSpec((1, hidden_block), lambda i: (0, i)),
        ],
        out_specs=[
            pl.BlockSpec((8, hidden_block), lambda i: (0, i)),
            whole,
            whole,
            pl.BlockSpec(memory_space=pl.ANY),
        ],
        out_shape=[
            jax.ShapeDtypeStruct((8, hidden), jnp.float32),
            jax.ShapeDtypeStruct((total, width), jnp.float32),
            jax.ShapeDtypeStruct((total, width), jnp.float32),
            jax.ShapeDtypeStruct((devices, packed_rows, width), jnp.bfloat16),
        ],
        scratch_shapes=[
            pltpu.VMEM((width, total), jnp.bfloat16),
            pltpu.VMEM((total, hidden_block), jnp.bfloat16),
            pltpu.VMEM((total, hidden_block), jnp.bfloat16),
            pltpu.VMEM((devices, width // devices, width), jnp.bfloat16),
            pltpu.VMEM((devices // steps, hidden // devices, width), jnp.bfloat16),
            pltpu.SemaphoreType.DMA((2,)),
        ],
        compiler_params=pltpu.CompilerParams(vmem_limit_bytes=52 << 20),
        cost_estimate=pl.CostEstimate(
            flops=12 * total * width * hidden,
            bytes_accessed=8 * width * hidden + 12 * total * width,
            transcendentals=2 * total * hidden,
        ),
        name="mlp",
    )(rows, upstream, weights, weights, b1)


def pixel_grad_kernel(grad_ref, kernels_ref, out_ref):
    tokens, bands, patch = out_ref.shape
    for band in range(bands):
        found = lax.dot_general(
            grad_ref[...],
            kernels_ref[band * patch : (band + 1) * patch, :],
            (((1,), (1,)), ((), ())),
            preferred_element_type=jnp.float32,
        )
        out_ref[:, band, :] = found[:tokens]


def pixel_grad(grads, kernels, images, tokens, bands):
    total, width = grads.shape
    patch = kernels.shape[0] // bands
    return pl.pallas_call(
        pixel_grad_kernel,
        grid=(images,),
        in_specs=[
            pl.BlockSpec((total // images, width), lambda i: (i, 0)),
            pl.BlockSpec(kernels.shape, lambda i: (0, 0)),
        ],
        out_specs=pl.BlockSpec((None, tokens, bands, patch), lambda i: (i, 0, 0, 0)),
        out_shape=jax.ShapeDtypeStruct((images, tokens, bands, patch), jnp.float32),
        compiler_params=pltpu.CompilerParams(vmem_limit_bytes=48 << 20),
        cost_estimate=pl.CostEstimate(flops=0, bytes_accessed=0, transcendentals=0),
        name="pixel_grad",
    )(grads, kernels)


def repack(packed, devices):
    few, rows, width = packed.shape
    each = width // few
    more = devices // few
    first = packed[:, : rows // 2].reshape(few, -1, more, each // more, width)
    first = first.transpose(0, 2, 1, 3, 4).reshape(devices, -1, width)
    return jnp.concatenate([first, packed[:, rows // 2 :].reshape(devices, -1, width)], axis=1)


def ordered_gather(value, axis):
    total = lax.axis_size(axis)
    at = lax.axis_index(axis)
    slots = jnp.arange(total).reshape((total,) + (1,) * value.ndim)
    gathered = jnp.where(slots == at, value[None], jnp.zeros((), value.dtype))
    for shift in range(1, total):
        moved = lax.ppermute(value, axis, [(i, (i + shift) % total) for i in range(total)])
        gathered = jnp.where(slots == (at - shift) % total, moved[None], gathered)
    return gathered


def local(
    pixels,
    cotangent,
    band_count,
    wave_index,
    weight_tokens,
    bias_token,
    hyper_qkv,
    hyper_qv_bias,
    hyper_out,
    hyper_out_bias,
    hyper_norm1_gain,
    hyper_norm1_bias,
    hyper_ff1,
    hyper_ff1_bias,
    hyper_ff2,
    hyper_ff2_bias,
    hyper_norm2_gain,
    hyper_norm2_bias,
    kernel_gen,
    kernel_gen_bias,
    conv_bias_gen,
    conv_bias_gen_bias,
    norm1_gain,
    norm1_bias,
    qkv_weight,
    qv_bias,
    proj_weight,
    proj_bias,
    norm2_gain,
    norm2_bias,
    fc1_weight,
    fc1_bias,
    fc2_weight,
    fc2_bias,
):
    group_total = lax.axis_size("grp")
    shard_total = lax.axis_size("img")
    group_at = lax.axis_index("grp")
    shard_at = lax.axis_index("img")
    images = pixels.shape[0]
    slot_count = pixels.shape[1]
    tokens = pixels.shape[2]
    patch = pixels.shape[3]
    model_width = cotangent.shape[2]
    padded = -(-tokens // 16) * 16
    row_count = images * padded

    def pad_rows(value):
        return jnp.pad(value, ((0, 0), (0, padded - tokens), (0, 0))).reshape(row_count, -1)

    band_total = band_count[0]
    band_mask = (jnp.arange(slot_count) < band_total).astype(jnp.float32)
    hyper_params = (
        weight_tokens,
        bias_token,
        hyper_qkv,
        hyper_qv_bias,
        hyper_out,
        hyper_out_bias,
        hyper_norm1_gain,
        hyper_norm1_bias,
        hyper_ff1,
        hyper_ff1_bias,
        hyper_ff2,
        hyper_ff2_bias,
        hyper_norm2_gain,
        hyper_norm2_bias,
    )
    hyper_wide = weight_tokens.shape[1]
    flat_params = hyper_params_2d(hyper_params)
    shard_patch = kernel_gen.shape[0]
    shard_rows = proj_weight.shape[0]
    lanes = hyper_wide
    folds = model_width // lanes
    fold_rows = shard_rows // folds
    small = [
        conv_bias_gen_bias,
        norm1_gain,
        norm1_bias,
        qv_bias,
        proj_bias,
        norm2_gain,
        norm2_bias,
        fc1_bias,
        fc2_bias,
    ]
    kernel_total = slot_count * shard_patch
    tables = ordered_gather(jnp.concatenate([band_count, wave_index[0]]), "grp")
    own_waves = wave_rows(wave_index, hyper_wide)
    own_usable = usable_rows(band_count, slot_count, weight_tokens.shape[0])

    def hyper_call():
        return hyper_forward_call(flat_params, own_waves, own_usable, slot_count)

    def all_call(tie):
        every = tables if tie is None else together(tables, tie)[0]
        waves = wave_rows(every[:, 1:], hyper_wide)
        usable = usable_rows(every[:, 0], slot_count, weight_tokens.shape[0])
        return waves, usable, hyper_forward_call(flat_params, waves, usable, slot_count)

    def kernel_call(rows):
        hidden = (rows[:slot_count] + own_waves[:slot_count]).astype(jnp.bfloat16)
        made = (
            jnp.einsum("be,pde->bpd", hidden, kernel_gen, preferred_element_type=jnp.float32)
            + kernel_gen_bias.astype(jnp.float32)[None]
        )
        made = (made * band_mask[:, None, None]).astype(jnp.bfloat16)
        *members, small_gen, _ = together(*small, conv_bias_gen, rows)
        shift = jnp.dot(
            small_gen.astype(jnp.float32), rows[slot_count], precision=highest_precision
        ) + members[0].astype(jnp.float32)
        upper = lax.optimization_barrier(shift.astype(jnp.bfloat16))
        lower = (shift - upper.astype(jnp.float32)).astype(jnp.bfloat16)
        small_rows = jnp.stack(
            [
                jnp.pad(member, (0, model_width - member.shape[0]))
                for member in [upper, lower] + members[1:]
            ]
        )
        folded = jnp.concatenate(
            [small_gen[at * fold_rows : (at + 1) * fold_rows] for at in range(folds)], axis=1
        )
        packed = jnp.concatenate([jnp.pad(small_rows, ((0, 16 - len(small) - 1), (0, 0))), folded])
        packed = jnp.pad(packed, ((0, -packed.shape[0] % 16), (0, 0)))
        return jnp.concatenate([made.reshape(kernel_total, model_width), packed])

    def rows_call(tie):
        pixels_here, cotangent_here = pixels, cotangent
        if tie is not None:
            pixels_here, cotangent_here, _ = together(pixels, cotangent, tie)
        pixel_rows = pixels_here.transpose(0, 2, 1, 3).reshape(images, tokens, slot_count * patch)
        return pad_rows(pixel_rows), pad_rows(cotangent_here)

    attention_full = lax.all_gather(
        jnp.concatenate([qkv_weight, proj_weight], axis=1), "img", axis=0, tiled=True
    )
    hidden_full = gather_hidden(fc1_weight, fc2_weight)
    line, other, (pixel_rows, upstream_low) = gather_kernels(kernel_call(hyper_call()), rows_call)
    patch_kernels, stream, normed_low = embed(
        (lax.axis_index("img") % 2).astype(jnp.int32).reshape(1),
        line,
        other,
        pixel_rows,
        images,
        slot_count,
        kernel_total,
    )
    found_small = line[:, kernel_total:], other[:, kernel_total:]
    small_line, small_other, _ = together(*found_small, normed_low)
    packed = in_order(lax.axis_index("img") % 2, small_line, small_other, 1)
    packed = packed.reshape((shard_total,) + packed.shape[2:])
    folded = packed[:, 16 : 16 + fold_rows]
    cb_weight = jnp.concatenate(
        [folded[:, :, at : at + lanes] for at in range(0, model_width, lanes)], axis=1
    ).reshape(model_width, lanes)
    gain_one, _, qv_full, proj_shift, gain_two, shift_two, fc1_shift, fc2_shift = (
        packed[:, 2 + at, : member.shape[0]].reshape(-1) for at, member in enumerate(small[1:])
    )
    proj_full = attention_full[:, 3 * model_width :]
    full_bias = jnp.stack(
        [qv_full[:model_width], jnp.zeros((model_width,), jnp.bfloat16), qv_full[model_width:]]
    ).astype(jnp.float32)
    projected = jnp.stack(
        [
            (
                jnp.dot(
                    normed_low,
                    attention_full[:, at * model_width : (at + 1) * model_width],
                    preferred_element_type=jnp.float32,
                )
                + full_bias[at]
            ).astype(jnp.bfloat16)
            for at in range(3)
        ]
    )
    attended, attn_probs = attention_forward(projected, images, tokens)
    all_waves, all_usable, all_rows = all_call(attended)
    attended, all_rows = together(attended, all_rows)
    all_rows = all_rows.reshape(group_total, SLOT_ROWS, hyper_wide)
    hidden_all = all_rows[:, :slot_count] + all_waves.reshape(all_rows.shape)[:, :slot_count]
    bias_row_all = all_rows[:, slot_count]
    middle = (
        stream
        + jnp.dot(attended, proj_full, preferred_element_type=jnp.float32)
        + proj_shift.astype(jnp.float32)
    )
    normed_two, norm_two_pull = jax.vjp(
        lambda values, norm_gain, norm_shift: layer_norm(values, norm_gain, norm_shift, norm_eps),
        middle,
        gain_two.astype(jnp.float32),
        shift_two.astype(jnp.float32),
    )
    normed_two_low = normed_two.astype(jnp.bfloat16)
    upstream = upstream_low.astype(jnp.float32)
    gate_sums, update, grad_normed_two, early_block = mlp(
        normed_two_low,
        upstream_low,
        hidden_full,
        fc1_shift.astype(jnp.float32)[None],
        row_count // 2,
        group_total * shard_total if torus_block() else 32,
    )
    grad_fc2_shift = jnp.sum(upstream, axis=0)
    grad_fc1_shift = jnp.sum(gate_sums, axis=0)
    if not torus_block():
        early_block = repack(early_block, group_total * shard_total)
    early_sum = lax.psum_scatter(early_block, BOTH, scatter_dimension=0, tiled=True)[0]
    grad_middle_part, grad_gain_two, grad_shift_two = norm_two_pull(grad_normed_two)
    grad_middle = upstream + grad_middle_part
    middle_low = grad_middle.astype(jnp.bfloat16)
    grad_proj_shift = jnp.sum(middle_low.astype(jnp.float32), axis=0)
    grad_attended = jnp.einsum(
        "te,de->td", middle_low, proj_full, preferred_element_type=jnp.float32
    ).astype(jnp.bfloat16)
    grad_projected, projected_sums = attention_backward(
        projected, attn_probs, grad_attended, images
    )
    projected_sums = jnp.sum(projected_sums, axis=1)
    grad_qv = jnp.concatenate([projected_sums[0], projected_sums[2]])
    device_total = group_total * shard_total
    block_rows = model_width // device_total

    def blocks_of(value):
        value = value.astype(jnp.bfloat16)
        return [
            value[:, at : at + model_width].reshape(device_total, -1, model_width)
            for at in range(0, value.shape[1], model_width)
        ]

    vectors = [
        grad_qv,
        grad_proj_shift,
        grad_gain_two,
        grad_shift_two,
        grad_fc1_shift,
        grad_fc2_shift,
    ]
    vector_lengths = [member.shape[0] // device_total for member in vectors]

    def late_call():
        grad_qkv = [
            jnp.einsum(
                "td,te->de", normed_low, grad_projected[at], preferred_element_type=jnp.float32
            )
            for at in range(3)
        ]
        grad_proj = jnp.einsum(
            "td,te->de", attended, middle_low, preferred_element_type=jnp.float32
        )
        vector_block = jnp.concatenate(
            [member.reshape(device_total, -1) for member in vectors], axis=1
        ).astype(jnp.bfloat16)
        late = [block for member in grad_qkv + [grad_proj] for block in blocks_of(member)]
        late_rows = sum(member.shape[1] for member in late)
        extra = -(-vector_block.shape[1] // model_width)
        extra += -(late_rows + extra) % 8
        vector_block = jnp.pad(
            vector_block, ((0, 0), (0, extra * model_width - vector_block.shape[1]))
        ).reshape(device_total, extra, model_width)
        return jnp.concatenate(late + [vector_block], axis=1)

    late, grad_projected = start_late(late_call(), grad_projected)
    residual_reduced, shard_kernels, first_sums = first_backward(
        grad_projected,
        attention_full,
        stream,
        grad_middle,
        gain_one.astype(jnp.float32)[None],
        pixel_rows,
        images,
        shard_total,
        slot_count,
    )
    grad_gain_one, grad_shift_one, grad_conv_shift = jnp.sum(first_sums, axis=1)

    def pixels_call(tie):
        grads = residual_reduced if tie is None else together(residual_reduced, tie)[0]
        return pixel_grad(grads, patch_kernels, images, tokens, slot_count).transpose(0, 2, 1, 3)

    def out_call(tie):
        here = update if tie is None else together(update, tie)[0]
        block_out = middle + here + fc2_shift.astype(jnp.float32)
        return block_out.reshape(images, padded, model_width)[:, :tokens]

    grad_bias_row_part = jnp.dot(
        grad_conv_shift, cb_weight.astype(jnp.float32), precision=highest_precision
    )
    def code_call(group_kernels):
        grad_hidden_part = jnp.einsum(
            "bpd,pde->be",
            group_kernels * band_mask[:, None, None],
            kernel_gen.astype(jnp.float32),
            precision=highest_precision,
        )
        return jnp.concatenate(
            [grad_hidden_part, grad_bias_row_part[None]]
            + [
                member.reshape(-1, hyper_wide)
                for member in (grad_conv_shift, grad_gain_one, grad_shift_one)
            ]
        )

    group_width = model_width // group_total
    code_all = hidden_all.astype(jnp.bfloat16).astype(jnp.float32)

    def gen_call(group_kernels):
        grad_pre = group_kernels * band_mask[:, None, None]
        swapped = lax.all_to_all(
            grad_pre.reshape(slot_count, shard_patch, group_total, group_width).transpose(
                2, 0, 1, 3
            ),
            "grp",
            0,
            0,
        ).reshape(group_total * slot_count, shard_patch, group_width)
        grad_gen = jnp.einsum(
            "kpd,ke->pde",
            swapped,
            code_all.reshape(group_total * slot_count, hyper_wide),
            precision=highest_precision,
        )
        return grad_gen, jnp.sum(swapped, axis=0)

    late_end, code_grads, filled = reduce_late(
        shard_kernels, late, code_call, [pixels_call, out_call], gen_call
    )
    grad_pixels, block_out, (grad_gen, grad_gen_shift) = filled
    fold_total = model_width // hyper_wide
    conv_parts, gain_parts, shift_parts = (
        code_grads[:, slot_count + 1 + at * fold_total : slot_count + 1 + (at + 1) * fold_total].reshape(
            group_total, model_width
        )
        for at in range(3)
    )
    code_grads = jnp.pad(
        code_grads[:, : slot_count + 1], ((0, 0), (0, SLOT_ROWS - slot_count - 1), (0, 0))
    ).reshape(-1, hyper_wide)
    hyper_total = hyper_backward_call(flat_params, all_waves, all_usable, code_grads, slot_count)
    late_out = late_end(hyper_total[0])
    *hyper_total, early_sum = together(*hyper_total, early_sum)
    hyper_total = [
        member.reshape(param.shape) for member, param in zip(hyper_total, hyper_params)
    ]
    early_out = early_sum.astype(jnp.float32)

    def columns_of(value, total):
        return jnp.concatenate(
            [value[at * block_rows : (at + 1) * block_rows] for at in range(total)], axis=1
        )

    fc1_out = columns_of(early_out, hidden_full.shape[0])
    fc2_out = early_out[fc1_out.size // model_width :]
    qkv_out = columns_of(late_out, 3)
    proj_out = late_out[3 * block_rows : 4 * block_rows]
    vector_out = late_out[4 * block_rows :].reshape(-1)
    parts = []
    vector_at = 0
    for length in vector_lengths:
        parts.append(vector_out[vector_at : vector_at + length])
        vector_at += length
    device_at = group_at * shard_total + shard_at

    def own_part(value):
        return lax.dynamic_slice_in_dim(value, device_at * block_rows, block_rows, 1)

    conv_parts = own_part(conv_parts)
    grad_cb_weight = jnp.dot(conv_parts.T, bias_row_all, precision=highest_precision)
    reduced = (
        grad_cb_weight,
        jnp.sum(conv_parts, axis=0),
        jnp.sum(own_part(gain_parts), axis=0),
        jnp.sum(own_part(shift_parts), axis=0),
        qkv_out,
        parts[0],
        proj_out,
        parts[1],
        parts[2],
        parts[3],
        fc1_out,
        parts[4],
        fc2_out,
        parts[5],
    )
    return (
        block_out,
        grad_pixels,
        hyper_total[0],
        hyper_total[1],
        hyper_total[2],
        hyper_total[3],
        hyper_total[4],
        hyper_total[5],
        hyper_total[6],
        hyper_total[7],
        hyper_total[8],
        hyper_total[9],
        hyper_total[10],
        hyper_total[11],
        hyper_total[12],
        hyper_total[13],
        grad_gen,
        grad_gen_shift,
        reduced[0],
        reduced[1],
        reduced[2],
        reduced[3],
        reduced[4],
        reduced[5],
        reduced[6],
        reduced[7],
        reduced[8],
        reduced[9],
        reduced[10],
        reduced[11],
        reduced[12],
        reduced[13],
    )


def solution(mesh):
    return jax.shard_map(
        local,
        mesh=mesh,
        in_specs=(
            P(("grp", "img"), None, None, None),
            P(("grp", "img"), None, None),
            P("grp"),
            P("grp", None),
            P(),
            P(),
            P(),
            P(),
            P(),
            P(),
            P(),
            P(),
            P(),
            P(),
            P(),
            P(),
            P(),
            P(),
            P("img", None, None),
            P("img", None),
            P("img", None),
            P("img"),
            P("img"),
            P("img"),
            P("img", None),
            P("img"),
            P("img", None),
            P("img"),
            P("img"),
            P("img"),
            P("img", None),
            P("img"),
            P("img", None),
            P("img"),
        ),
        out_specs=(
            P(("grp", "img"), None, None),
            P(("grp", "img"), None, None, None),
            P(),
            P(),
            P(),
            P(),
            P(),
            P(),
            P(),
            P(),
            P(),
            P(),
            P(),
            P(),
            P(),
            P(),
            P("img", "grp", None),
            P("img", "grp"),
            P(("grp", "img"), None),
            P(("grp", "img")),
            P(("grp", "img")),
            P(("grp", "img")),
            P(("grp", "img"), None),
            P(("grp", "img")),
            P(("grp", "img"), None),
            P(("grp", "img")),
            P(("grp", "img")),
            P(("grp", "img")),
            P(("grp", "img"), None),
            P(("grp", "img")),
            P(("grp", "img"), None),
            P(("grp", "img")),
        ),
        check_vma=False,
    )
```

```python
import functools

import jax
import jax.numpy as jnp
from jax import lax
from jax.experimental import pallas as pl
from jax.experimental.pallas import tpu as pltpu
from jax.sharding import PartitionSpec as P

HEADS = 12
WHEADS = 4
WAVES = 256


norm_eps = 1e-06
hyper_eps = 1e-05
highest_precision = lax.Precision.HIGHEST


def layer_norm(values, norm_gain, norm_shift, epsilon):
    centre = values - jnp.mean(values, axis=-1, keepdims=True)
    spread = jnp.mean(centre * centre, axis=-1, keepdims=True)
    return centre * lax.rsqrt(spread + epsilon) * norm_gain + norm_shift


def gelu_exact(values):
    return jax.nn.gelu(values, approximate=False)


def wave_embed(indices, hyper_width):
    half_model_width = hyper_width // 2
    wavelength = 400.0 + 2100.0 * indices.astype(jnp.float32) / (WAVES - 1)
    frequency = 1.0 / 10000.0 ** (
        jnp.arange(half_model_width, dtype=jnp.float32) / half_model_width
    )
    angles = wavelength[:, None] * frequency[None, :]
    return jnp.concatenate([jnp.sin(angles), jnp.cos(angles)], axis=-1)


def hyper_forward(params, indices, band_total):
    (
        tokens,
        bias_tok,
        qkv_w,
        qv_b,
        out_w,
        out_b,
        gain_one,
        shift_one,
        ff_in,
        ff_in_b,
        ff_out,
        ff_out_b,
        gain_two,
        shift_two,
    ) = params
    hyper_width = tokens.shape[1]
    slot_count = indices.shape[0]
    token_rows = tokens.shape[0]
    head_dim = hyper_width // WHEADS
    waves = wave_embed(indices, hyper_width)
    joined = jnp.concatenate([tokens, waves, bias_tok[None, :]], axis=0)
    query_rows = joined[token_rows:]
    queries = (
        jnp.dot(query_rows, qkv_w[:, :hyper_width], precision=highest_precision)
        + qv_b[:hyper_width]
    ).reshape(slot_count + 1, WHEADS, head_dim)
    key_rows = jnp.dot(
        joined, qkv_w[:, hyper_width : 2 * hyper_width], precision=highest_precision
    ).reshape(-1, WHEADS, head_dim)
    values = (
        jnp.dot(joined, qkv_w[:, 2 * hyper_width :], precision=highest_precision)
        + qv_b[hyper_width:]
    ).reshape(-1, WHEADS, head_dim)
    scores = jnp.einsum(
        "qhd,khd->hqk", queries, key_rows, precision=highest_precision
    ) * head_dim ** (-0.5)
    offsets = jnp.arange(joined.shape[0]) - token_rows
    usable = (offsets < band_total) | (offsets == slot_count)
    scores = jnp.where(usable[None, None, :], scores, -1e30)
    weights = jax.nn.softmax(scores, axis=-1)
    mixture = jnp.einsum("hqk,khd->qhd", weights, values, precision=highest_precision).reshape(
        slot_count + 1, hyper_width
    )
    normed_one = layer_norm(
        query_rows + jnp.dot(mixture, out_w, precision=highest_precision) + out_b,
        gain_one,
        shift_one,
        hyper_eps,
    )
    hidden = gelu_exact(jnp.dot(normed_one, ff_in, precision=highest_precision) + ff_in_b)
    normed_two = layer_norm(
        normed_one + jnp.dot(hidden, ff_out, precision=highest_precision) + ff_out_b,
        gain_two,
        shift_two,
        hyper_eps,
    )
    return (normed_two[:slot_count] + waves, normed_two[slot_count])


BOTH = ("grp", "img")


def torus_block():
    return lax.axis_size("grp") == 4 and lax.axis_size("img") == 8


def flipped(index, bit):
    return index ^ bit


def swap(value, bit):
    return lax.ppermute(value, BOTH, [(i, i ^ bit) for i in range(32)])


def around_z(value, shift):
    moves = [(i, i - i % 8 + (i % 8 // 2 + shift) % 4 * 2 + i % 2) for i in range(32)]
    return lax.ppermute(value, BOTH, moves)


def pick(value, index, axis=0):
    return lax.dynamic_index_in_dim(value, index, axis, keepdims=False)


def add_low(left, right):
    return (left.astype(jnp.float32) + right.astype(jnp.float32)).astype(jnp.bfloat16)


def z_index():
    return (lax.axis_index("img") // 2).astype(jnp.int32)


def scatter_start(chunks):
    z = z_index()
    return [pick(chunks, z)] + [
        around_z(pick(chunks, (z + shift) % 4), shift) for shift in range(1, 4)
    ]


def scatter_end(terms):
    return sum(term.astype(jnp.float32) for term in terms)


def gather_start(value):
    return [value] + [around_z(value, shift) for shift in range(1, 4)]


def gather_end(held):
    z = z_index()
    rows = []
    for place in range(4):
        row = held[(0 - place) % 4]
        for z_at in range(1, 4):
            row = jnp.where(z == z_at, held[(z_at - place) % 4], row)
        rows.append(row)
    return jnp.stack(rows)


def in_order(bit, own, other, axis):
    return jnp.stack(
        [jnp.where(bit == 0, own, other), jnp.where(bit == 0, other, own)], axis=axis
    )


def together(*values):
    return lax.optimization_barrier(values)


def core_half(value, axis):
    core = lax.axis_index("img") % 2
    return pick(value, core, axis), pick(value, 1 - core, axis)


def gather_small(value):
    if not torus_block():
        return lax.all_gather(value, "img", axis=0, tiled=False)
    shard = lax.axis_index("img")
    value = in_order(shard % 2, value, swap(value, 1), 0)
    value = in_order(shard // 2 % 2, value, swap(value, 2), 0)
    value = in_order(shard // 4, value, swap(value, 4), 0)
    return value.reshape((8,) + value.shape[3:])


def gather_weights(qkv_weight, proj_weight, fc1_weight, fc2_weight):
    width = proj_weight.shape[1]
    hidden = fc1_weight.shape[1]
    part = hidden // 4
    if not torus_block():
        both = jnp.concatenate([qkv_weight, proj_weight], axis=1)
        both = lax.all_gather(both, "img", axis=0, tiled=True)
        fc1 = lax.all_gather(fc1_weight, "img", axis=0, tiled=True)
        fc2 = lax.all_gather(fc2_weight, "img", axis=0, tiled=True)
        both = both.reshape(8, -1, 4, width).transpose(2, 0, 1, 3)
        fc1 = fc1.reshape(8, -1, 4, part).transpose(2, 0, 1, 3)
        fc2 = fc2.reshape(8, 4, -1, width).transpose(1, 0, 2, 3)
        return jnp.concatenate([both, fc1, fc2], axis=2)
    shard = proj_weight.shape[0]
    group = lax.axis_index("grp")
    own = jnp.concatenate(
        [
            jnp.where(
                group == 3,
                proj_weight,
                lax.dynamic_slice_in_dim(qkv_weight, jnp.minimum(group, 2) * width, width, 1),
            ),
            lax.dynamic_slice_in_dim(fc1_weight, group * part, part, 1),
            lax.dynamic_slice_in_dim(fc2_weight, group * shard, shard, 0),
        ]
    )
    return lax.all_gather(own, BOTH, axis=0, tiled=False).reshape(4, 8, 3 * shard, width)


def gather_kernels(kernels, rows_call):
    if not torus_block():
        kernels = lax.all_gather(kernels, "img", axis=0, tiled=False)
        kernels = kernels.reshape((-1, 2) + kernels.shape[1:])
        return core_half(kernels, 1) + (rows_call(None),)
    held = gather_start(kernels)
    held, rows = together(held, rows_call(kernels))
    line = gather_end(held)
    return line, swap(line, 1), rows


def start_late(keep, send, later):
    if not torus_block():
        late = in_order(lax.axis_index("img") % 2, keep, send, 1)
        late = late.reshape((-1,) + keep.shape[1:])
        return lax.psum_scatter(late, BOTH, scatter_dimension=0, tiled=True)[0], later
    send_in = swap(send, 1)
    keep, later = together(keep, later)
    return (keep, send_in), later


def reduce_late(keep, send, late, code_call, fill_calls, gen_call):
    if not torus_block():
        kernels = in_order(lax.axis_index("img") % 2, keep, send, 1)
        kernels = kernels.reshape((-1,) + keep.shape[1:])
        kernels = lax.psum_scatter(kernels, "img", scatter_dimension=0, tiled=True)[0]
        kernels = kernels.astype(jnp.float32)
        code = jnp.sum(ordered_gather(code_call(kernels), "img"), axis=0)
        filled = [call(None) for call in fill_calls] + [gen_call(kernels)]
        return [late], ordered_gather(code, "grp"), filled
    group = lax.axis_index("grp")
    x, y = group % 2, group // 2
    send_in = swap(send, 1)
    late = add_low(*late).reshape((2, 2, 4) + late[0].shape[1:])
    first, second = late[:, :, :2], late[:, :, 2:]
    send_in, late_out, late_other = together(
        send_in, pick(first, 1 - x, 1), pick(second, 1 - y, 0)
    )
    first_in, second_in = swap(late_out, 8), swap(late_other, 16)
    chunks = add_low(keep, send_in)
    terms = scatter_start(chunks)
    filled = [fill_calls[0](chunks)]
    first_in, second_in, filled[0] = together(first_in, second_in, filled[0])
    first = add_low(pick(first, x, 1), first_in)
    second = add_low(pick(second, y, 0), second_in)
    first_in = swap(pick(first, 1 - y), 16)
    second_in = swap(pick(second, 1 - x), 8)
    filled.append(fill_calls[1](first))
    first_in, second_in, filled[1] = together(first_in, second_in, filled[1])
    late = jnp.concatenate(
        [add_low(pick(first, y), first_in), add_low(pick(second, x), second_in)]
    )
    terms, late = together(terms, late)
    late_terms = scatter_start(late)
    kernels = scatter_end(terms)
    code = code_call(kernels)
    code = code + swap(code, 1)
    code = code + swap(code, 2)
    code, kernels = together(code, kernels)
    code = code + swap(code, 4)
    code = in_order(x, code, swap(code, 8), 0)
    code = in_order(y, code, swap(code, 16), 0).reshape((4,) + code.shape[1:])
    filled.append(gen_call(kernels))
    return late_terms, code, filled


def lane_half(shape):
    return lax.broadcasted_iota(jnp.int32, shape, len(shape) - 1) % 128 < 64


def attention_forward_kernel(
    tokens, rows_ref, query_ref, key_ref, value_ref, bias_ref, projected_ref, attended_ref, probs_ref
):
    rows, width = rows_ref.shape
    for at, ref in enumerate((query_ref, key_ref, value_ref)):
        made = jnp.dot(
            rows_ref[...], ref[...].reshape(width, width), preferred_element_type=jnp.float32
        )
        projected_ref[at] = (made + bias_ref[at]).astype(jnp.bfloat16)
    low_half = lane_half((rows, 128))
    real_key = lax.broadcasted_iota(jnp.int32, (rows, rows), 0) < tokens
    for pair in range(width // 128):
        at = pair * 128
        queries = projected_ref[0, :, at : at + 128] * jnp.bfloat16(0.125)
        key_rows = projected_ref[1, :, at : at + 128]
        values = projected_ref[2, :, at : at + 128]
        halves = []
        for half in range(2):
            chosen = low_half if half == 0 else ~low_half
            own_queries = jnp.where(chosen, queries, jnp.bfloat16(0))
            scores = lax.dot_general(
                key_rows, own_queries, (((1,), (1,)), ((), ())), preferred_element_type=jnp.float32
            )
            scores = jnp.where(real_key, scores, -1e30)
            raised = jnp.exp(scores - jnp.max(scores, axis=0, keepdims=True))
            probs = raised * (1.0 / jnp.sum(raised, axis=0, keepdims=True))
            probs = probs.astype(jnp.bfloat16)
            probs_ref[2 * pair + half] = probs
            halves.append(
                lax.dot_general(
                    probs, values, (((0,), (0,)), ((), ())), preferred_element_type=jnp.float32
                )
            )
        attended_ref[:, at : at + 128] = jnp.where(low_half, halves[0], halves[1]).astype(
            jnp.bfloat16
        )


def weight_spec(weights, column, section=0):
    _, eighths, rows, width = weights.shape
    return pl.BlockSpec((None, eighths, rows // 3, width), lambda i: (column, 0, section, 0))


def attention_forward(normed, weights, bias, images, tokens):
    total, width = normed.shape
    rows = total // images
    heads = width // 64
    return pl.pallas_call(
        functools.partial(attention_forward_kernel, tokens),
        grid=(images,),
        in_specs=[
            pl.BlockSpec((rows, width), lambda i: (i, 0)),
            weight_spec(weights, 0),
            weight_spec(weights, 1),
            weight_spec(weights, 2),
            pl.BlockSpec((3, 1, width), lambda i: (0, 0, 0)),
        ],
        out_specs=[
            pl.BlockSpec((3, rows, width), lambda i: (0, i, 0)),
            pl.BlockSpec((rows, width), lambda i: (i, 0)),
            pl.BlockSpec((None, heads, rows, rows), lambda i: (i, 0, 0, 0)),
        ],
        out_shape=[
            jax.ShapeDtypeStruct((3, total, width), jnp.bfloat16),
            jax.ShapeDtypeStruct((total, width), jnp.bfloat16),
            jax.ShapeDtypeStruct((images, heads, rows, rows), jnp.bfloat16),
        ],
        compiler_params=pltpu.CompilerParams(vmem_limit_bytes=48 << 20),
        cost_estimate=pl.CostEstimate(
            flops=images * heads * rows * rows * 64 * 4 + 6 * total * width * width,
            bytes_accessed=images * rows * (8 * width + 2 * heads * rows) + 6 * width * width,
            transcendentals=images * heads * rows * rows,
        ),
        name="attention_forward",
    )(normed, weights, weights, weights, bias)


def attention_backward_kernel(projected_ref, probs_ref, grad_ref, out_ref, sums_ref):
    _, rows, width = projected_ref.shape
    low_half = lane_half((rows, 128))

    @pl.when(pl.program_id(0) == 0)
    def _():
        sums_ref[...] = jnp.zeros_like(sums_ref)

    for pair in range(width // 128):
        at = pair * 128
        queries = projected_ref[0, :, at : at + 128]
        key_rows = projected_ref[1, :, at : at + 128]
        values = projected_ref[2, :, at : at + 128]
        grads = grad_ref[:, at : at + 128]
        found = []
        for half in range(2):
            chosen = low_half if half == 0 else ~low_half
            probs = probs_ref[2 * pair + half]
            own_grads = jnp.where(chosen, grads, jnp.bfloat16(0))
            grad_values = jnp.dot(probs, grads, preferred_element_type=jnp.float32)
            grad_probs = lax.dot_general(
                values, own_grads, (((1,), (1,)), ((), ())), preferred_element_type=jnp.float32
            )
            wide = probs.astype(jnp.float32)
            weighted = grad_probs * wide
            total = jnp.sum(weighted, axis=0, keepdims=True)
            grad_scores = (weighted - wide * total).astype(jnp.bfloat16)
            grad_keys = jnp.dot(grad_scores, queries, preferred_element_type=jnp.float32) * 0.125
            grad_queries = (
                lax.dot_general(
                    grad_scores,
                    key_rows,
                    (((0,), (0,)), ((), ())),
                    preferred_element_type=jnp.float32,
                )
                * 0.125
            )
            found.append((grad_queries, grad_keys, grad_values))
        for kind in range(3):
            joined = jnp.where(low_half, found[0][kind], found[1][kind]).astype(jnp.bfloat16)
            place = slice(at, at + 128)
            out_ref[kind, :, place] = joined
            sums_ref[kind, :, place] += jnp.sum(
                joined.astype(jnp.float32).reshape(rows // 8, 8, 128), axis=0
            )


def attention_backward(projected, probs, grad_attended, images):
    _, total, width = projected.shape
    rows = total // images
    heads = width // 64
    return pl.pallas_call(
        attention_backward_kernel,
        grid=(images,),
        in_specs=[
            pl.BlockSpec((3, rows, width), lambda i: (0, i, 0)),
            pl.BlockSpec((None, heads, rows, rows), lambda i: (i, 0, 0, 0)),
            pl.BlockSpec((rows, width), lambda i: (i, 0)),
        ],
        out_specs=[
            pl.BlockSpec((3, rows, width), lambda i: (0, i, 0)),
            pl.BlockSpec((3, 8, width), lambda i: (0, 0, 0)),
        ],
        out_shape=[
            jax.ShapeDtypeStruct((3, total, width), jnp.bfloat16),
            jax.ShapeDtypeStruct((3, 8, width), jnp.float32),
        ],
        compiler_params=pltpu.CompilerParams(vmem_limit_bytes=48 << 20),
        cost_estimate=pl.CostEstimate(flops=0, bytes_accessed=0, transcendentals=0),
        name="attention_backward",
    )(projected, probs, grad_attended)


SLOT_ROWS = 16


def exact_dot(left, right, contract=((1,), (0,))):
    return lax.dot_general(
        left,
        right,
        (contract, ((), ())),
        precision=highest_precision,
        preferred_element_type=jnp.float32,
    )


def rows_norm(values, norm_gain, norm_shift, epsilon):
    centre = values - jnp.mean(values, axis=-1, keepdims=True)
    spread = jnp.mean(centre * centre, axis=-1, keepdims=True)
    return centre * lax.rsqrt(spread + epsilon) * norm_gain + norm_shift


def gelu_rows(values):
    return values * (0.5 + 0.5 * lax.erf(values * 0.7071067811865476))


def hyper_rows(params, waves, usable, slots):
    (
        tokens,
        bias_tok,
        qkv_w,
        qv_b,
        out_w,
        out_b,
        gain_one,
        shift_one,
        ff_in,
        ff_in_b,
        ff_out,
        ff_out_b,
        gain_two,
        shift_two,
    ) = params
    width = tokens.shape[1]
    head_dim = width // WHEADS
    total = waves.shape[0]
    place = lax.broadcasted_iota(jnp.int32, (total, 1), 0) & (SLOT_ROWS - 1)
    query_rows = jnp.where(place == slots, jnp.broadcast_to(bias_tok, (total, width)), waves)
    joined = jnp.concatenate([tokens, query_rows], axis=0)
    queries = exact_dot(query_rows, qkv_w[:, :width]) + qv_b[:, :width]
    key_rows = exact_dot(joined, qkv_w[:, width : 2 * width])
    values = exact_dot(joined, qkv_w[:, 2 * width :]) + qv_b[:, width:]
    head_at = lax.broadcasted_iota(jnp.int32, (1, width), 1)
    mixture = jnp.zeros((total, width), jnp.float32)
    for head in range(WHEADS):
        own = ((head_at >= head * head_dim) & (head_at < (head + 1) * head_dim)).astype(jnp.float32)
        scores = exact_dot(queries * own, key_rows, ((1,), (1,))) * head_dim ** (-0.5)
        scores = jnp.where(usable > 0, scores, -1e30)
        raised = jnp.exp(scores - lax.stop_gradient(jnp.max(scores, axis=-1, keepdims=True)))
        weights = raised / jnp.sum(raised, axis=-1, keepdims=True)
        mixture = mixture + exact_dot(weights, values) * own
    first = rows_norm(query_rows + exact_dot(mixture, out_w) + out_b, gain_one, shift_one, hyper_eps)
    hidden = gelu_rows(exact_dot(first, ff_in) + ff_in_b)
    return rows_norm(first + exact_dot(hidden, ff_out) + ff_out_b, gain_two, shift_two, hyper_eps)


def usable_rows(band_counts, slots, token_rows):
    groups = band_counts.shape[0]
    total = groups * SLOT_ROWS
    row = jnp.arange(total)
    own_group = row[:, None] // SLOT_ROWS == row[None, :] // SLOT_ROWS
    place = row % SLOT_ROWS
    present = (place < jnp.repeat(band_counts, SLOT_ROWS)) | (place == slots)
    return jnp.concatenate(
        [jnp.ones((total, token_rows)), (own_group & present[None, :]).astype(jnp.float32)], axis=1
    )


def hyper_params_2d(params):
    return tuple(member[None] if member.ndim == 1 else member for member in params)


def wave_rows(indices, width):
    groups, slots = indices.shape
    waves = jax.vmap(lambda row: wave_embed(row, width))(indices)
    return jnp.pad(waves, ((0, 0), (0, SLOT_ROWS - slots), (0, 0))).reshape(-1, width)


def hyper_forward_kernel(slots, waves_ref, usable_ref, *refs):
    refs[-1][...] = hyper_rows(
        tuple(ref[...] for ref in refs[:-1]), waves_ref[...], usable_ref[...], slots
    )


def hyper_backward_kernel(slots, waves_ref, usable_ref, grads_ref, *refs):
    count = len(refs) // 2
    waves, usable = waves_ref[...], usable_ref[...]
    _, pull = jax.vjp(
        lambda params: hyper_rows(params, waves, usable, slots),
        tuple(ref[...] for ref in refs[:count]),
    )
    (found,) = pull(grads_ref[...])
    for ref, value in zip(refs[count:], found):
        ref[...] = value


def hyper_forward_call(params, waves, usable, slots):
    return pl.pallas_call(
        functools.partial(hyper_forward_kernel, slots),
        out_shape=jax.ShapeDtypeStruct(waves.shape, jnp.float32),
        name="hyper_forward",
    )(waves, usable, *params)


def hyper_backward_call(params, waves, usable, grads, slots):
    return pl.pallas_call(
        functools.partial(hyper_backward_kernel, slots),
        out_shape=[jax.ShapeDtypeStruct(member.shape, jnp.float32) for member in params],
        name="hyper_backward",
    )(waves, usable, grads, *params)


def embed_kernel(
    bands, small_at, core_ref, line_ref, other_ref, pixels_ref, kernels_ref, stream_ref, normed_ref, rows_ref
):
    chips, _, width = line_ref.shape
    part = kernels_ref.shape[0] // (2 * chips * bands)
    shard = width // (2 * chips)

    @pl.when(pl.program_id(0) == 0)
    def _():
        for core in range(2):
            low_ref, high_ref = (line_ref, other_ref) if core == 0 else (other_ref, line_ref)

            @pl.when((core_ref[0] == 0) == (core == 0))
            def _():
                for chip in range(chips):
                    for band in range(bands):
                        place = (band * chips + chip) * 2 * part
                        here = slice(band * part, (band + 1) * part)
                        kernels_ref[place : place + part] = low_ref[chip, here]
                        kernels_ref[place + part : place + 2 * part] = high_ref[chip, here]
                    for which, ref in enumerate((low_ref, high_ref)):
                        small = ref[chip, small_at : small_at + 16, :shard].astype(jnp.float32)
                        at = (chip * 2 + which) * shard
                        rows_ref[:, at : at + shard] = small

    shift = rows_ref[0:1] + rows_ref[1:2]
    stream = (
        jnp.dot(pixels_ref[...], kernels_ref[...], preferred_element_type=jnp.float32) + shift
    )
    stream_ref[...] = stream
    centre = stream - jnp.mean(stream, axis=-1, keepdims=True)
    spread = jnp.mean(centre * centre, axis=-1, keepdims=True)
    normed = centre * lax.rsqrt(spread + norm_eps) * rows_ref[2:3] + rows_ref[3:4]
    normed_ref[...] = normed.astype(jnp.bfloat16)


def embed(core, line, other, pixel_rows, images, bands, small_at):
    width = line.shape[2]
    total, depth = pixel_rows.shape
    rows = total // images
    part_spec = pl.BlockSpec(line.shape, lambda i, core_ref: (0, 0, 0))
    row = pl.BlockSpec((rows, width), lambda i, core_ref: (i, 0))
    return pl.pallas_call(
        functools.partial(embed_kernel, bands, small_at),
        grid_spec=pltpu.PrefetchScalarGridSpec(
            num_scalar_prefetch=1,
            grid=(images,),
            in_specs=[
                part_spec,
                part_spec,
                pl.BlockSpec((rows, depth), lambda i, core_ref: (i, 0)),
            ],
            out_specs=[pl.BlockSpec((depth, width), lambda i, core_ref: (0, 0)), row, row],
            scratch_shapes=[pltpu.VMEM((16, width), jnp.float32)],
        ),
        out_shape=[
            jax.ShapeDtypeStruct((depth, width), jnp.bfloat16),
            jax.ShapeDtypeStruct((total, width), jnp.float32),
            jax.ShapeDtypeStruct((total, width), jnp.bfloat16),
        ],
        compiler_params=pltpu.CompilerParams(vmem_limit_bytes=48 << 20),
        cost_estimate=pl.CostEstimate(
            flops=2 * total * width * depth,
            bytes_accessed=total * (2 * depth + 6 * width) + 4 * depth * width,
            transcendentals=total,
        ),
        name="embed",
    )(core, line, other, pixel_rows)


def first_backward_kernel(
    bands,
    core_ref,
    projected_ref,
    query_ref,
    key_ref,
    value_ref,
    stream_ref,
    residual_ref,
    gain_ref,
    pixels_ref,
    out_ref,
    keep_ref,
    send_ref,
    sums_ref,
    total_ref,
):
    rows, width = stream_ref.shape
    chips, part, _ = keep_ref.shape
    part //= bands

    @pl.when(pl.program_id(0) == 0)
    def _():
        sums_ref[...] = jnp.zeros_like(sums_ref)
        total_ref[...] = jnp.zeros_like(total_ref)

    def folded(value):
        return jnp.sum(value.reshape(rows // 8, 8, width), axis=0)

    grads = sum(
        lax.dot_general(
            projected_ref[at],
            ref[...].reshape(width, width),
            (((1,), (1,)), ((), ())),
            preferred_element_type=jnp.float32,
        )
        for at, ref in enumerate((query_ref, key_ref, value_ref))
    )
    stream = stream_ref[...]
    centre = stream - jnp.mean(stream, axis=-1, keepdims=True)
    spread = jnp.mean(centre * centre, axis=-1, keepdims=True)
    scale = lax.rsqrt(spread + norm_eps)
    normed = centre * scale
    sums_ref[0] += folded(grads * normed)
    sums_ref[1] += folded(grads)
    grads = grads * gain_ref[...]
    grads = scale * (
        grads
        - jnp.mean(grads, axis=-1, keepdims=True)
        - normed * jnp.mean(grads * normed, axis=-1, keepdims=True)
    )
    low = (residual_ref[...] + grads).astype(jnp.bfloat16)
    out_ref[...] = low
    sums_ref[2] += folded(low.astype(jnp.float32))
    total_ref[...] += lax.dot_general(
        pixels_ref[...], low, (((0,), (0,)), ((), ())), preferred_element_type=jnp.float32
    )

    for core in range(2):
        low_ref, high_ref = (keep_ref, send_ref) if core == 0 else (send_ref, keep_ref)

        @pl.when((pl.program_id(0) == pl.num_programs(0) - 1) & ((core_ref[0] == 0) == (core == 0)))
        def _():
            for chip in range(chips):
                for band in range(bands):
                    place = (band * chips + chip) * 2 * part
                    here = slice(band * part, (band + 1) * part)
                    made = total_ref[place : place + 2 * part].astype(jnp.bfloat16)
                    low_ref[chip, here] = made[:part]
                    high_ref[chip, here] = made[part:]


def first_backward(
    core, grad_projected, weights, stream, residual, gain, pixel_rows, images, shards, bands
):
    total, width = stream.shape
    rows = total // images
    depth = pixel_rows.shape[1]
    row = pl.BlockSpec((rows, width), lambda i, core_ref: (i, 0))
    made = (shards // 2, depth // shards, width)
    part = pl.BlockSpec(made, lambda i, core_ref: (0, 0, 0))

    def column(at):
        _, eighths, shard, _ = weights.shape
        return pl.BlockSpec(
            (None, eighths, shard // 3, width), lambda i, core_ref: (at, 0, 0, 0)
        )

    return pl.pallas_call(
        functools.partial(first_backward_kernel, bands),
        grid_spec=pltpu.PrefetchScalarGridSpec(
            num_scalar_prefetch=1,
            grid=(images,),
        in_specs=[
            pl.BlockSpec((3, rows, width), lambda i, core_ref: (0, i, 0)),
            column(0),
            column(1),
            column(2),
            row,
            row,
            pl.BlockSpec((1, width), lambda i, core_ref: (0, 0)),
            pl.BlockSpec((rows, depth), lambda i, core_ref: (i, 0)),
        ],
        out_specs=[
            row,
            part,
            part,
            pl.BlockSpec((3, 8, width), lambda i, core_ref: (0, 0, 0)),
        ],
        scratch_shapes=[pltpu.VMEM((depth, width), jnp.float32)],
        ),
        out_shape=[
            jax.ShapeDtypeStruct((total, width), jnp.bfloat16),
            jax.ShapeDtypeStruct(made, jnp.bfloat16),
            jax.ShapeDtypeStruct(made, jnp.bfloat16),
            jax.ShapeDtypeStruct((3, 8, width), jnp.float32),
        ],
        compiler_params=pltpu.CompilerParams(vmem_limit_bytes=48 << 20),
        cost_estimate=pl.CostEstimate(flops=0, bytes_accessed=0, transcendentals=0),
        name="first_backward",
    )(core, grad_projected, weights, weights, weights, stream, residual, gain, pixel_rows)


def late_kernel(
    core_ref,
    normed_ref,
    attended_ref,
    projected_ref,
    branch_ref,
    vectors_ref,
    keep_ref,
    send_ref,
    turned_ref,
    made_ref,
):
    at_step = pl.program_id(0)
    width = normed_ref.shape[1]
    pairs = keep_ref.shape[0]
    each = width // (2 * pairs)

    @pl.when(at_step == 0)
    def _():
        turned_ref[...] = normed_ref[...].T

    @pl.when(at_step == 3)
    def _():
        turned_ref[...] = attended_ref[...].T

    @pl.when(at_step < 3)
    def _():
        made = jnp.dot(turned_ref[...], projected_ref[...], preferred_element_type=jnp.float32)
        made_ref[...] = made.astype(jnp.bfloat16).reshape(made_ref.shape)

    @pl.when(at_step == 3)
    def _():
        made = jnp.dot(turned_ref[...], branch_ref[...], preferred_element_type=jnp.float32)
        made_ref[...] = made.astype(jnp.bfloat16).reshape(made_ref.shape)

    for core in range(2):
        low_ref, high_ref = (keep_ref, send_ref) if core == 0 else (send_ref, keep_ref)
        for step in range(4):

            @pl.when((at_step == step) & ((core_ref[0] == 0) == (core == 0)))
            def _():
                here = slice(step * each, (step + 1) * each)
                for pair in range(pairs):
                    low_ref[pair, here] = made_ref[2 * pair]
                    high_ref[pair, here] = made_ref[2 * pair + 1]
                    if step == 0:
                        low_ref[pair, 4 * each :] = vectors_ref[2 * pair]
                        high_ref[pair, 4 * each :] = vectors_ref[2 * pair + 1]


def late_gradients(core, normed, attended, grad_projected, branch, vectors):
    total, width = normed.shape
    devices, extra, _ = vectors.shape
    each = width // devices
    made = (devices // 2, 4 * each + extra, width)
    whole = pl.BlockSpec((total, width), lambda i, core_ref: (0, 0))
    part = pl.BlockSpec(made, lambda i, core_ref: (0, 0, 0))
    return pl.pallas_call(
        late_kernel,
        grid_spec=pltpu.PrefetchScalarGridSpec(
            num_scalar_prefetch=1,
            grid=(4,),
            in_specs=[
                whole,
                whole,
                pl.BlockSpec((None, total, width), lambda i, core_ref: (jnp.minimum(i, 2), 0, 0)),
                whole,
                pl.BlockSpec(vectors.shape, lambda i, core_ref: (0, 0, 0)),
            ],
            out_specs=[part, part],
            scratch_shapes=[
                pltpu.VMEM((width, total), jnp.bfloat16),
                pltpu.VMEM((devices, each, width), jnp.bfloat16),
            ],
        ),
        out_shape=[jax.ShapeDtypeStruct(made, jnp.bfloat16)] * 2,
        compiler_params=pltpu.CompilerParams(vmem_limit_bytes=48 << 20),
        cost_estimate=pl.CostEstimate(flops=0, bytes_accessed=0, transcendentals=0),
        name="late_gradients",
    )(core, normed, attended, grad_projected, branch, vectors)


def mlp_kernel(
    block,
    devices,
    rows_ref,
    upstream_ref,
    first_weight_ref,
    second_weight_ref,
    b1_ref,
    sums_ref,
    out_ref,
    grad_ref,
    packed_ref,
    turned_ref,
    act_ref,
    gate_ref,
    first_ref,
    second_ref,
    sems,
):
    at_step = pl.program_id(0)
    steps = pl.num_programs(0)
    total, width = rows_ref.shape
    eighths, shard, hidden_block = first_weight_ref.shape
    quarters, group, _, _ = second_weight_ref.shape
    w1 = first_weight_ref[...].reshape(width, hidden_block)
    w2 = jnp.concatenate(
        [second_weight_ref[at, eighth] for eighth in range(group) for at in range(quarters)]
    )
    first_rows = width // devices
    second_devices = devices // steps
    second_rows = hidden_block // second_devices

    def copies(step):
        return (
            pltpu.make_async_copy(
                first_ref, packed_ref.at[:, pl.ds(step * first_rows, first_rows), :], sems.at[0]
            ),
            pltpu.make_async_copy(
                second_ref,
                packed_ref.at[
                    pl.ds(step * second_devices, second_devices),
                    pl.ds(steps * first_rows, second_rows),
                    :,
                ],
                sems.at[1],
            ),
        )

    @pl.when(at_step == 0)
    def _():
        out_ref[...] = jnp.zeros_like(out_ref)
        grad_ref[...] = jnp.zeros_like(grad_ref)
        turned_ref[...] = rows_ref[...].T

    for at in range(0, total, block):
        here = slice(at, at + block)
        gate_in = (
            jnp.dot(rows_ref[here], w1, preferred_element_type=jnp.float32) + b1_ref[...]
        )
        grad_act = lax.dot_general(
            upstream_ref[here],
            w2,
            (((1,), (1,)), ((), ())),
            preferred_element_type=jnp.float32,
        )
        chance = 0.5 + 0.5 * lax.erf(gate_in * 0.7071067811865476)
        density = 0.3989422804014327 * jnp.exp(-0.5 * gate_in * gate_in)
        act = (gate_in * chance).astype(jnp.bfloat16)
        gate = (grad_act * (chance + gate_in * density)).astype(jnp.bfloat16)
        act_ref[here] = act
        gate_ref[here] = gate
        wide = gate.astype(jnp.float32)
        part = jnp.sum(wide.reshape(block // 8, 8, wide.shape[1]), axis=0)
        sums_ref[...] = part if at == 0 else sums_ref[...] + part
        out_ref[here] += jnp.dot(act, w2, preferred_element_type=jnp.float32)
        grad_ref[here] += lax.dot_general(
            gate, w1, (((1,), (1,)), ((), ())), preferred_element_type=jnp.float32
        )

    @pl.when(at_step > 0)
    def _():
        for copy in copies(at_step - 1):
            copy.wait()

    first = jnp.dot(turned_ref[...], gate_ref[...], preferred_element_type=jnp.float32)
    first_ref[...] = first.astype(jnp.bfloat16).reshape(first_ref.shape)
    second = lax.dot_general(
        act_ref[...], upstream_ref[...], (((0,), (0,)), ((), ())), preferred_element_type=jnp.float32
    )
    second_ref[...] = second.astype(jnp.bfloat16).reshape(second_ref.shape)
    for copy in copies(at_step):
        copy.start()

    @pl.when(at_step == steps - 1)
    def _():
        for copy in copies(at_step):
            copy.wait()


def mlp(rows, upstream, weights, b1, row_block, devices):
    total, width = rows.shape
    steps, eighths, shard, hidden_block = weights.shape
    shard //= 3
    hidden = steps * hidden_block
    whole = pl.BlockSpec((total, width), lambda i: (0, 0))
    packed_rows = (width * steps + hidden) // devices
    return pl.pallas_call(
        functools.partial(mlp_kernel, row_block, devices),
        grid=(steps,),
        in_specs=[
            whole,
            whole,
            pl.BlockSpec((None, eighths, shard, hidden_block), lambda i: (i, 0, 1, 0)),
            pl.BlockSpec((steps, eighths // steps, shard, width), lambda i: (0, i, 2, 0)),
            pl.BlockSpec((1, hidden_block), lambda i: (0, i)),
        ],
        out_specs=[
            pl.BlockSpec((8, hidden_block), lambda i: (0, i)),
            whole,
            whole,
            pl.BlockSpec(memory_space=pl.ANY),
        ],
        out_shape=[
            jax.ShapeDtypeStruct((8, hidden), jnp.float32),
            jax.ShapeDtypeStruct((total, width), jnp.float32),
            jax.ShapeDtypeStruct((total, width), jnp.float32),
            jax.ShapeDtypeStruct((devices, packed_rows, width), jnp.bfloat16),
        ],
        scratch_shapes=[
            pltpu.VMEM((width, total), jnp.bfloat16),
            pltpu.VMEM((total, hidden_block), jnp.bfloat16),
            pltpu.VMEM((total, hidden_block), jnp.bfloat16),
            pltpu.VMEM((devices, width // devices, width), jnp.bfloat16),
            pltpu.VMEM((devices // steps, hidden // devices, width), jnp.bfloat16),
            pltpu.SemaphoreType.DMA((2,)),
        ],
        compiler_params=pltpu.CompilerParams(vmem_limit_bytes=52 << 20),
        cost_estimate=pl.CostEstimate(
            flops=12 * total * width * hidden,
            bytes_accessed=8 * width * hidden + 12 * total * width,
            transcendentals=2 * total * hidden,
        ),
        name="mlp",
    )(rows, upstream, weights, weights, b1)


def pixel_grad_kernel(grad_ref, kernels_ref, out_ref):
    tokens, bands, patch = out_ref.shape
    for band in range(bands):
        found = lax.dot_general(
            grad_ref[...],
            kernels_ref[band * patch : (band + 1) * patch, :],
            (((1,), (1,)), ((), ())),
            preferred_element_type=jnp.float32,
        )
        out_ref[:, band, :] = found[:tokens]


def pixel_grad(grads, kernels, images, tokens, bands):
    total, width = grads.shape
    patch = kernels.shape[0] // bands
    return pl.pallas_call(
        pixel_grad_kernel,
        grid=(images,),
        in_specs=[
            pl.BlockSpec((total // images, width), lambda i: (i, 0)),
            pl.BlockSpec(kernels.shape, lambda i: (0, 0)),
        ],
        out_specs=pl.BlockSpec((None, tokens, bands, patch), lambda i: (i, 0, 0, 0)),
        out_shape=jax.ShapeDtypeStruct((images, tokens, bands, patch), jnp.float32),
        compiler_params=pltpu.CompilerParams(vmem_limit_bytes=48 << 20),
        cost_estimate=pl.CostEstimate(flops=0, bytes_accessed=0, transcendentals=0),
        name="pixel_grad",
    )(grads, kernels)


def repack(packed, devices):
    few, rows, width = packed.shape
    each = width // few
    more = devices // few
    first = packed[:, : rows // 2].reshape(few, -1, more, each // more, width)
    first = first.transpose(0, 2, 1, 3, 4).reshape(devices, -1, width)
    return jnp.concatenate([first, packed[:, rows // 2 :].reshape(devices, -1, width)], axis=1)


def ordered_gather(value, axis):
    total = lax.axis_size(axis)
    at = lax.axis_index(axis)
    slots = jnp.arange(total).reshape((total,) + (1,) * value.ndim)
    gathered = jnp.where(slots == at, value[None], jnp.zeros((), value.dtype))
    for shift in range(1, total):
        moved = lax.ppermute(value, axis, [(i, (i + shift) % total) for i in range(total)])
        gathered = jnp.where(slots == (at - shift) % total, moved[None], gathered)
    return gathered


def local(
    pixels,
    cotangent,
    band_count,
    wave_index,
    weight_tokens,
    bias_token,
    hyper_qkv,
    hyper_qv_bias,
    hyper_out,
    hyper_out_bias,
    hyper_norm1_gain,
    hyper_norm1_bias,
    hyper_ff1,
    hyper_ff1_bias,
    hyper_ff2,
    hyper_ff2_bias,
    hyper_norm2_gain,
    hyper_norm2_bias,
    kernel_gen,
    kernel_gen_bias,
    conv_bias_gen,
    conv_bias_gen_bias,
    norm1_gain,
    norm1_bias,
    qkv_weight,
    qv_bias,
    proj_weight,
    proj_bias,
    norm2_gain,
    norm2_bias,
    fc1_weight,
    fc1_bias,
    fc2_weight,
    fc2_bias,
):
    group_total = lax.axis_size("grp")
    shard_total = lax.axis_size("img")
    group_at = lax.axis_index("grp")
    shard_at = lax.axis_index("img")
    images = pixels.shape[0]
    slot_count = pixels.shape[1]
    tokens = pixels.shape[2]
    patch = pixels.shape[3]
    model_width = cotangent.shape[2]
    padded = -(-tokens // 16) * 16
    row_count = images * padded

    def pad_rows(value):
        return jnp.pad(value, ((0, 0), (0, padded - tokens), (0, 0))).reshape(row_count, -1)

    band_total = band_count[0]
    band_mask = (jnp.arange(slot_count) < band_total).astype(jnp.float32)
    hyper_params = (
        weight_tokens,
        bias_token,
        hyper_qkv,
        hyper_qv_bias,
        hyper_out,
        hyper_out_bias,
        hyper_norm1_gain,
        hyper_norm1_bias,
        hyper_ff1,
        hyper_ff1_bias,
        hyper_ff2,
        hyper_ff2_bias,
        hyper_norm2_gain,
        hyper_norm2_bias,
    )
    hyper_wide = weight_tokens.shape[1]
    flat_params = hyper_params_2d(hyper_params)
    shard_patch = kernel_gen.shape[0]
    shard_rows = proj_weight.shape[0]
    lanes = hyper_wide
    folds = model_width // lanes
    fold_rows = shard_rows // folds
    small = [
        conv_bias_gen_bias,
        norm1_gain,
        norm1_bias,
        qv_bias,
        proj_bias,
        norm2_gain,
        norm2_bias,
        fc1_bias,
        fc2_bias,
    ]
    kernel_total = slot_count * shard_patch
    own_waves = wave_rows(wave_index, hyper_wide)
    own_usable = usable_rows(band_count, slot_count, weight_tokens.shape[0])

    def hyper_call():
        return hyper_forward_call(flat_params, own_waves, own_usable, slot_count)

    def all_call(tie):
        table = jnp.concatenate([band_count, wave_index[0]])
        every = ordered_gather(together(table, tie)[0], "grp")
        waves = wave_rows(every[:, 1:], hyper_wide)
        usable = usable_rows(every[:, 0], slot_count, weight_tokens.shape[0])
        return waves, usable, hyper_forward_call(flat_params, waves, usable, slot_count)

    def kernel_call(rows):
        hidden = (rows[:slot_count] + own_waves[:slot_count]).astype(jnp.bfloat16)
        made = (
            jnp.einsum("be,pde->bpd", hidden, kernel_gen, preferred_element_type=jnp.float32)
            + kernel_gen_bias.astype(jnp.float32)[None]
        )
        made = (made * band_mask[:, None, None]).astype(jnp.bfloat16)
        *members, small_gen, _ = together(*small, conv_bias_gen, rows)
        shift = jnp.dot(
            small_gen.astype(jnp.float32), rows[slot_count], precision=highest_precision
        ) + members[0].astype(jnp.float32)
        upper = lax.optimization_barrier(shift.astype(jnp.bfloat16))
        lower = (shift - upper.astype(jnp.float32)).astype(jnp.bfloat16)
        small_rows = jnp.stack(
            [
                jnp.pad(member, (0, model_width - member.shape[0]))
                for member in [upper, lower] + members[1:]
            ]
        )
        folded = jnp.concatenate(
            [small_gen[at * fold_rows : (at + 1) * fold_rows] for at in range(folds)], axis=1
        )
        packed = jnp.concatenate([jnp.pad(small_rows, ((0, 16 - len(small) - 1), (0, 0))), folded])
        packed = jnp.pad(packed, ((0, -packed.shape[0] % 16), (0, 0)))
        return jnp.concatenate([made.reshape(kernel_total, model_width), packed])

    def rows_call(tie):
        pixels_here, cotangent_here = pixels, cotangent
        if tie is not None:
            pixels_here, cotangent_here, _ = together(pixels, cotangent, tie)
        pixel_rows = pixels_here.transpose(0, 2, 1, 3).reshape(images, tokens, slot_count * patch)
        return pad_rows(pixel_rows), pad_rows(cotangent_here)

    weights_full = gather_weights(qkv_weight, proj_weight, fc1_weight, fc2_weight)
    core_at = (lax.axis_index("img") % 2).astype(jnp.int32).reshape(1)
    line, other, (pixel_rows, upstream_low) = gather_kernels(kernel_call(hyper_call()), rows_call)
    patch_kernels, stream, normed_low = embed(
        core_at,
        line,
        other,
        pixel_rows,
        images,
        slot_count,
        kernel_total,
    )
    found_small = line[:, kernel_total:], other[:, kernel_total:]
    small_line, small_other, _ = together(*found_small, normed_low)
    packed = in_order(lax.axis_index("img") % 2, small_line, small_other, 1)
    packed = packed.reshape((shard_total,) + packed.shape[2:])
    folded = packed[:, 16 : 16 + fold_rows]
    cb_weight = jnp.concatenate(
        [folded[:, :, at : at + lanes] for at in range(0, model_width, lanes)], axis=1
    ).reshape(model_width, lanes)
    gain_one, _, qv_full, proj_shift, gain_two, shift_two, fc1_shift, fc2_shift = (
        packed[:, 2 + at, : member.shape[0]].reshape(-1) for at, member in enumerate(small[1:])
    )
    proj_full = weights_full[3, :, : weights_full.shape[2] // 3].reshape(model_width, model_width)
    full_bias = jnp.stack(
        [qv_full[:model_width], jnp.zeros((model_width,), jnp.bfloat16), qv_full[model_width:]]
    ).astype(jnp.float32)
    all_waves, all_usable, all_rows = all_call(normed_low)
    normed_low, all_rows = together(normed_low, all_rows)
    projected, attended, attn_probs = attention_forward(
        normed_low, weights_full, full_bias[:, None], images, tokens
    )
    all_rows = all_rows.reshape(group_total, SLOT_ROWS, hyper_wide)
    hidden_all = all_rows[:, :slot_count] + all_waves.reshape(all_rows.shape)[:, :slot_count]
    bias_row_all = all_rows[:, slot_count]
    middle = (
        stream
        + jnp.dot(attended, proj_full, preferred_element_type=jnp.float32)
        + proj_shift.astype(jnp.float32)
    )
    normed_two, norm_two_pull = jax.vjp(
        lambda values, norm_gain, norm_shift: layer_norm(values, norm_gain, norm_shift, norm_eps),
        middle,
        gain_two.astype(jnp.float32),
        shift_two.astype(jnp.float32),
    )
    normed_two_low = normed_two.astype(jnp.bfloat16)
    upstream = upstream_low.astype(jnp.float32)
    gate_sums, update, grad_normed_two, early_block = mlp(
        normed_two_low,
        upstream_low,
        weights_full,
        fc1_shift.astype(jnp.float32)[None],
        row_count // 2,
        group_total * shard_total if torus_block() else 32,
    )
    grad_fc2_shift = jnp.sum(upstream, axis=0)
    grad_fc1_shift = jnp.sum(gate_sums, axis=0)
    if not torus_block():
        early_block = repack(early_block, group_total * shard_total)
    early_sum = lax.psum_scatter(early_block, BOTH, scatter_dimension=0, tiled=True)[0]
    grad_middle_part, grad_gain_two, grad_shift_two = norm_two_pull(grad_normed_two)
    grad_middle = upstream + grad_middle_part
    middle_low = grad_middle.astype(jnp.bfloat16)
    grad_proj_shift = jnp.sum(middle_low.astype(jnp.float32), axis=0)
    grad_attended = jnp.einsum(
        "te,de->td", middle_low, proj_full, preferred_element_type=jnp.float32
    ).astype(jnp.bfloat16)
    grad_projected, projected_sums = attention_backward(
        projected, attn_probs, grad_attended, images
    )
    projected_sums = jnp.sum(projected_sums, axis=1)
    grad_qv = jnp.concatenate([projected_sums[0], projected_sums[2]])
    device_total = group_total * shard_total
    block_rows = model_width // device_total

    vectors = [
        grad_qv,
        grad_proj_shift,
        grad_gain_two,
        grad_shift_two,
        grad_fc1_shift,
        grad_fc2_shift,
    ]
    vector_lengths = [member.shape[0] // device_total for member in vectors]

    vector_block = jnp.concatenate(
        [member.reshape(device_total, -1) for member in vectors], axis=1
    ).astype(jnp.bfloat16)
    extra = -(-vector_block.shape[1] // model_width)
    extra += -(4 * block_rows + extra) % 8
    vector_block = jnp.pad(
        vector_block, ((0, 0), (0, extra * model_width - vector_block.shape[1]))
    ).reshape(device_total, extra, model_width)
    late, grad_projected = start_late(
        *late_gradients(core_at, normed_low, attended, grad_projected, middle_low, vector_block),
        grad_projected,
    )
    residual_reduced, keep_kernels, send_kernels, first_sums = first_backward(
        core_at,
        grad_projected,
        weights_full,
        stream,
        grad_middle,
        gain_one.astype(jnp.float32)[None],
        pixel_rows,
        images,
        shard_total,
        slot_count,
    )
    grad_gain_one, grad_shift_one, grad_conv_shift = jnp.sum(first_sums, axis=1)

    def pixels_call(tie):
        grads = residual_reduced if tie is None else together(residual_reduced, tie)[0]
        return pixel_grad(grads, patch_kernels, images, tokens, slot_count).transpose(0, 2, 1, 3)

    def out_call(tie):
        here = update if tie is None else together(update, tie)[0]
        block_out = middle + here + fc2_shift.astype(jnp.float32)
        return block_out.reshape(images, padded, model_width)[:, :tokens]

    grad_bias_row_part = jnp.dot(
        grad_conv_shift, cb_weight.astype(jnp.float32), precision=highest_precision
    )
    def code_call(group_kernels):
        grad_hidden_part = jnp.einsum(
            "bpd,pde->be",
            group_kernels.reshape(slot_count, shard_patch, model_width)
            * band_mask[:, None, None],
            kernel_gen.astype(jnp.float32),
            precision=highest_precision,
        )
        return jnp.concatenate(
            [grad_hidden_part, grad_bias_row_part[None]]
            + [
                member.reshape(-1, hyper_wide)
                for member in (grad_conv_shift, grad_gain_one, grad_shift_one)
            ]
        )

    group_width = model_width // group_total
    code_all = hidden_all.astype(jnp.bfloat16).astype(jnp.float32)

    def gen_call(group_kernels):
        group_kernels = group_kernels.reshape(slot_count, shard_patch, model_width)
        grad_pre = group_kernels * band_mask[:, None, None]
        swapped = lax.all_to_all(
            grad_pre.reshape(slot_count, shard_patch, group_total, group_width).transpose(
                2, 0, 1, 3
            ),
            "grp",
            0,
            0,
        ).reshape(group_total * slot_count, shard_patch, group_width)
        grad_gen = jnp.einsum(
            "kpd,ke->pde",
            swapped,
            code_all.reshape(group_total * slot_count, hyper_wide),
            precision=highest_precision,
        )
        return grad_gen, jnp.sum(swapped, axis=0)

    late_terms, code_grads, filled = reduce_late(
        keep_kernels, send_kernels, late, code_call, [pixels_call, out_call], gen_call
    )
    grad_pixels, block_out, (grad_gen, grad_gen_shift) = filled
    fold_total = model_width // hyper_wide
    conv_parts, gain_parts, shift_parts = (
        code_grads[:, slot_count + 1 + at * fold_total : slot_count + 1 + (at + 1) * fold_total].reshape(
            group_total, model_width
        )
        for at in range(3)
    )
    code_grads = jnp.pad(
        code_grads[:, : slot_count + 1], ((0, 0), (0, SLOT_ROWS - slot_count - 1), (0, 0))
    ).reshape(-1, hyper_wide)
    hyper_total = hyper_backward_call(flat_params, all_waves, all_usable, code_grads, slot_count)
    late_terms, *hyper_total, early_sum = together(late_terms, *hyper_total, early_sum)
    late_out = scatter_end(late_terms)
    hyper_total = [
        member.reshape(param.shape) for member, param in zip(hyper_total, hyper_params)
    ]
    early_out = early_sum.astype(jnp.float32)

    def columns_of(value, total):
        return jnp.concatenate(
            [value[at * block_rows : (at + 1) * block_rows] for at in range(total)], axis=1
        )

    fc1_out = columns_of(early_out, weights_full.shape[0])
    fc2_out = early_out[fc1_out.size // model_width :]
    qkv_out = columns_of(late_out, 3)
    proj_out = late_out[3 * block_rows : 4 * block_rows]
    vector_out = late_out[4 * block_rows :].reshape(-1)
    parts = []
    vector_at = 0
    for length in vector_lengths:
        parts.append(vector_out[vector_at : vector_at + length])
        vector_at += length
    device_at = group_at * shard_total + shard_at

    def own_part(value):
        return lax.dynamic_slice_in_dim(value, device_at * block_rows, block_rows, 1)

    conv_parts = own_part(conv_parts)
    grad_cb_weight = jnp.dot(conv_parts.T, bias_row_all, precision=highest_precision)
    reduced = (
        grad_cb_weight,
        jnp.sum(conv_parts, axis=0),
        jnp.sum(own_part(gain_parts), axis=0),
        jnp.sum(own_part(shift_parts), axis=0),
        qkv_out,
        parts[0],
        proj_out,
        parts[1],
        parts[2],
        parts[3],
        fc1_out,
        parts[4],
        fc2_out,
        parts[5],
    )
    return (
        block_out,
        grad_pixels,
        hyper_total[0],
        hyper_total[1],
        hyper_total[2],
        hyper_total[3],
        hyper_total[4],
        hyper_total[5],
        hyper_total[6],
        hyper_total[7],
        hyper_total[8],
        hyper_total[9],
        hyper_total[10],
        hyper_total[11],
        hyper_total[12],
        hyper_total[13],
        grad_gen,
        grad_gen_shift,
        reduced[0],
        reduced[1],
        reduced[2],
        reduced[3],
        reduced[4],
        reduced[5],
        reduced[6],
        reduced[7],
        reduced[8],
        reduced[9],
        reduced[10],
        reduced[11],
        reduced[12],
        reduced[13],
    )


def solution(mesh):
    return jax.shard_map(
        local,
        mesh=mesh,
        in_specs=(
            P(("grp", "img"), None, None, None),
            P(("grp", "img"), None, None),
            P("grp"),
            P("grp", None),
            P(),
            P(),
            P(),
            P(),
            P(),
            P(),
            P(),
            P(),
            P(),
            P(),
            P(),
            P(),
            P(),
            P(),
            P("img", None, None),
            P("img", None),
            P("img", None),
            P("img"),
            P("img"),
            P("img"),
            P("img", None),
            P("img"),
            P("img", None),
            P("img"),
            P("img"),
            P("img"),
            P("img", None),
            P("img"),
            P("img", None),
            P("img"),
        ),
        out_specs=(
            P(("grp", "img"), None, None),
            P(("grp", "img"), None, None, None),
            P(),
            P(),
            P(),
            P(),
            P(),
            P(),
            P(),
            P(),
            P(),
            P(),
            P(),
            P(),
            P(),
            P(),
            P("img", "grp", None),
            P("img", "grp"),
            P(("grp", "img"), None),
            P(("grp", "img")),
            P(("grp", "img")),
            P(("grp", "img")),
            P(("grp", "img"), None),
            P(("grp", "img")),
            P(("grp", "img"), None),
            P(("grp", "img")),
            P(("grp", "img")),
            P(("grp", "img")),
            P(("grp", "img"), None),
            P(("grp", "img")),
            P(("grp", "img"), None),
            P(("grp", "img")),
        ),
        check_vma=False,
    )
```

```python
import functools

import jax
import jax.numpy as jnp
from jax import lax
from jax.experimental import pallas as pl
from jax.experimental.pallas import tpu as pltpu
from jax.sharding import Mesh, PartitionSpec as P

HEADS = 12
WHEADS = 4
WAVES = 256


norm_eps = 1e-06
hyper_eps = 1e-05
highest_precision = lax.Precision.HIGHEST


def layer_norm(values, norm_gain, norm_shift, epsilon):
    centre = values - jnp.mean(values, axis=-1, keepdims=True)
    spread = jnp.mean(centre * centre, axis=-1, keepdims=True)
    return centre * lax.rsqrt(spread + epsilon) * norm_gain + norm_shift


def gelu_exact(values):
    return jax.nn.gelu(values, approximate=False)


def wave_embed(indices, hyper_width):
    half_model_width = hyper_width // 2
    wavelength = 400.0 + 2100.0 * indices.astype(jnp.float32) / (WAVES - 1)
    frequency = 1.0 / 10000.0 ** (
        jnp.arange(half_model_width, dtype=jnp.float32) / half_model_width
    )
    angles = wavelength[:, None] * frequency[None, :]
    return jnp.concatenate([jnp.sin(angles), jnp.cos(angles)], axis=-1)


def hyper_forward(params, indices, band_total):
    (
        tokens,
        bias_tok,
        qkv_w,
        qv_b,
        out_w,
        out_b,
        gain_one,
        shift_one,
        ff_in,
        ff_in_b,
        ff_out,
        ff_out_b,
        gain_two,
        shift_two,
    ) = params
    hyper_width = tokens.shape[1]
    slot_count = indices.shape[0]
    token_rows = tokens.shape[0]
    head_dim = hyper_width // WHEADS
    waves = wave_embed(indices, hyper_width)
    joined = jnp.concatenate([tokens, waves, bias_tok[None, :]], axis=0)
    query_rows = joined[token_rows:]
    queries = (
        jnp.dot(query_rows, qkv_w[:, :hyper_width], precision=highest_precision)
        + qv_b[:hyper_width]
    ).reshape(slot_count + 1, WHEADS, head_dim)
    key_rows = jnp.dot(
        joined, qkv_w[:, hyper_width : 2 * hyper_width], precision=highest_precision
    ).reshape(-1, WHEADS, head_dim)
    values = (
        jnp.dot(joined, qkv_w[:, 2 * hyper_width :], precision=highest_precision)
        + qv_b[hyper_width:]
    ).reshape(-1, WHEADS, head_dim)
    scores = jnp.einsum(
        "qhd,khd->hqk", queries, key_rows, precision=highest_precision
    ) * head_dim ** (-0.5)
    offsets = jnp.arange(joined.shape[0]) - token_rows
    usable = (offsets < band_total) | (offsets == slot_count)
    scores = jnp.where(usable[None, None, :], scores, -1e30)
    weights = jax.nn.softmax(scores, axis=-1)
    mixture = jnp.einsum("hqk,khd->qhd", weights, values, precision=highest_precision).reshape(
        slot_count + 1, hyper_width
    )
    normed_one = layer_norm(
        query_rows + jnp.dot(mixture, out_w, precision=highest_precision) + out_b,
        gain_one,
        shift_one,
        hyper_eps,
    )
    hidden = gelu_exact(jnp.dot(normed_one, ff_in, precision=highest_precision) + ff_in_b)
    normed_two = layer_norm(
        normed_one + jnp.dot(hidden, ff_out, precision=highest_precision) + ff_out_b,
        gain_two,
        shift_two,
        hyper_eps,
    )
    return (normed_two[:slot_count] + waves, normed_two[slot_count])


SHARDS = ("z", "core")
BOTH = ("grp",) + SHARDS


def torus_block():
    return lax.axis_size("grp") == 4 and lax.axis_size(SHARDS) == 8


def flipped(index, bit):
    return index ^ bit


def swap(value, bit):
    return lax.ppermute(value, BOTH, [(i, i ^ bit) for i in range(32)])


def around_z(value, shift):
    moves = [(i, i - i % 8 + (i % 8 // 2 + shift) % 4 * 2 + i % 2) for i in range(32)]
    return lax.ppermute(value, BOTH, moves)


def pick(value, index, axis=0):
    return lax.dynamic_index_in_dim(value, index, axis, keepdims=False)


def add_low(left, right):
    return (left.astype(jnp.float32) + right.astype(jnp.float32)).astype(jnp.bfloat16)


def z_index():
    return (lax.axis_index(SHARDS) // 2).astype(jnp.int32)


def scatter_start(chunks):
    z = z_index()
    return [pick(chunks, z)] + [
        around_z(pick(chunks, (z + shift) % 4), shift) for shift in range(1, 4)
    ]


def scatter_end(terms):
    return sum(term.astype(jnp.float32) for term in terms)


def gather_start(value):
    return [value] + [around_z(value, shift) for shift in range(1, 4)]


def gather_end(held):
    z = z_index()
    rows = []
    for place in range(4):
        row = held[(0 - place) % 4]
        for z_at in range(1, 4):
            row = jnp.where(z == z_at, held[(z_at - place) % 4], row)
        rows.append(row)
    return jnp.stack(rows)


def in_order(bit, own, other, axis):
    return jnp.stack(
        [jnp.where(bit == 0, own, other), jnp.where(bit == 0, other, own)], axis=axis
    )


def together(*values):
    return lax.optimization_barrier(values)


def core_half(value, axis):
    core = lax.axis_index(SHARDS) % 2
    return pick(value, core, axis), pick(value, 1 - core, axis)


def gather_small(value):
    if not torus_block():
        return lax.all_gather(value, SHARDS, axis=0, tiled=False)
    shard = lax.axis_index(SHARDS)
    value = in_order(shard % 2, value, swap(value, 1), 0)
    value = in_order(shard // 2 % 2, value, swap(value, 2), 0)
    value = in_order(shard // 4, value, swap(value, 4), 0)
    return value.reshape((8,) + value.shape[3:])


def gather_weights(qkv_weight, proj_weight, fc1_weight, fc2_weight):
    width = proj_weight.shape[1]
    hidden = fc1_weight.shape[1]
    part = hidden // 4
    if not torus_block():
        both = jnp.concatenate([qkv_weight, proj_weight], axis=1)
        both = lax.all_gather(both, SHARDS, axis=0, tiled=True)
        fc1 = lax.all_gather(fc1_weight, SHARDS, axis=0, tiled=True)
        fc2 = lax.all_gather(fc2_weight, SHARDS, axis=0, tiled=True)
        both = both.reshape(8, -1, 4, width).transpose(2, 0, 1, 3)
        fc1 = fc1.reshape(8, -1, 4, part).transpose(2, 0, 1, 3)
        fc2 = fc2.reshape(8, 4, -1, width).transpose(1, 0, 2, 3)
        return jnp.concatenate([both, fc1, fc2], axis=2)
    shard = proj_weight.shape[0]
    group = lax.axis_index("grp")
    own = jnp.concatenate(
        [
            jnp.where(
                group == 3,
                proj_weight,
                lax.dynamic_slice_in_dim(qkv_weight, jnp.minimum(group, 2) * width, width, 1),
            ),
            lax.dynamic_slice_in_dim(fc1_weight, group * part, part, 1),
            lax.dynamic_slice_in_dim(fc2_weight, group * shard, shard, 0),
        ]
    )
    return lax.all_gather(own, BOTH, axis=0, tiled=False).reshape(4, 8, 3 * shard, width)


def gather_kernels(kernels, rows_call):
    if not torus_block():
        kernels = lax.all_gather(kernels, SHARDS, axis=0, tiled=False)
        kernels = kernels.reshape((-1, 2) + kernels.shape[1:])
        return core_half(kernels, 1) + (rows_call(None),)
    held = gather_start(kernels)
    held, rows = together(held, rows_call(kernels))
    line = gather_end(held)
    return line, swap(line, 1), rows


def repack(packed, devices):
    few, rows, width = packed.shape
    each = width // few
    more = devices // few
    first = packed[:, : rows // 2].reshape(few, -1, more, each // more, width)
    first = first.transpose(0, 2, 1, 3, 4).reshape(devices, -1, width)
    return jnp.concatenate([first, packed[:, rows // 2 :].reshape(devices, -1, width)], axis=1)


def sum_cores(packed):
    if not torus_block():
        devices = lax.axis_size("grp") * lax.axis_size(SHARDS)
        packed = packed.transpose(1, 0, 2, 3).reshape((-1,) + packed.shape[2:])
        return lax.psum_scatter(
            repack(packed, devices), BOTH, scatter_dimension=0, tiled=True
        )[0]
    return lax.psum_scatter(packed, "core", scatter_dimension=0, tiled=True)[0]


def sum_groups(early):
    if not torus_block():
        return early
    early = early.reshape((4, 4) + early.shape[1:])
    return lax.psum_scatter(early, "grp", scatter_dimension=0, tiled=True)[0]


def sum_chips(early):
    if not torus_block():
        return early
    return lax.psum_scatter(early, "z", scatter_dimension=0, tiled=True)[0]


def start_late(keep, send, later):
    if not torus_block():
        late = in_order(lax.axis_index(SHARDS) % 2, keep, send, 1)
        late = late.reshape((-1,) + keep.shape[1:])
        return lax.psum_scatter(late, BOTH, scatter_dimension=0, tiled=True)[0], later
    send_in = swap(send, 1)
    keep, later = together(keep, later)
    return (keep, send_in), later


def reduce_late(keep, send, early, late, code_call, fill_calls, gen_call):
    if not torus_block():
        kernels = in_order(lax.axis_index(SHARDS) % 2, keep, send, 1)
        kernels = kernels.reshape((-1,) + keep.shape[1:])
        kernels = lax.psum_scatter(kernels, SHARDS, scatter_dimension=0, tiled=True)[0]
        kernels = kernels.astype(jnp.float32)
        code = jnp.sum(ordered_gather(code_call(kernels), SHARDS), axis=0)
        filled = [call(None) for call in fill_calls] + [gen_call(kernels)]
        return early, [late], ordered_gather(code, "grp"), filled
    group = lax.axis_index("grp")
    x, y = group % 2, group // 2
    send_in = swap(send, 1)
    late = add_low(*late).reshape((2, 2, 4) + late[0].shape[1:])
    first, second = late[:, :, :2], late[:, :, 2:]
    send_in, late_out, late_other = together(
        send_in, pick(first, 1 - x, 1), pick(second, 1 - y, 0)
    )
    first_in, second_in = swap(late_out, 8), swap(late_other, 16)
    chunks = add_low(keep, send_in)
    terms = scatter_start(chunks)
    filled = [fill_calls[0](chunks)]
    first_in, second_in, filled[0] = together(first_in, second_in, filled[0])
    first = add_low(pick(first, x, 1), first_in)
    second = add_low(pick(second, y, 0), second_in)
    first_in = swap(pick(first, 1 - y), 16)
    second_in = swap(pick(second, 1 - x), 8)
    filled.append(fill_calls[1](first))
    terms, filled[1] = together(terms, filled[1])
    kernels = scatter_end(terms)
    code = code_call(kernels)
    code = code + swap(code, 1)
    code = code + swap(code, 2)
    code, kernels, first_in, second_in, early = together(
        code, kernels, first_in, second_in, early
    )
    early = sum_chips(early)
    late = jnp.concatenate(
        [add_low(pick(first, y), first_in), add_low(pick(second, x), second_in)]
    )
    late_terms = scatter_start(late)
    code = code + swap(code, 4)
    code = in_order(x, code, swap(code, 8), 0)
    code = in_order(y, code, swap(code, 16), 0).reshape((4,) + code.shape[1:])
    filled.append(gen_call(kernels))
    return early, late_terms, code, filled


def lane_half(shape):
    return lax.broadcasted_iota(jnp.int32, shape, len(shape) - 1) % 128 < 64


def attention_forward_kernel(
    tokens, rows_ref, query_ref, key_ref, value_ref, bias_ref, projected_ref, attended_ref, probs_ref
):
    rows, width = rows_ref.shape
    for at, ref in enumerate((query_ref, key_ref, value_ref)):
        made = jnp.dot(
            rows_ref[...], ref[...].reshape(width, width), preferred_element_type=jnp.float32
        )
        projected_ref[at] = (made + bias_ref[at]).astype(jnp.bfloat16)
    low_half = lane_half((rows, 128))
    real_key = lax.broadcasted_iota(jnp.int32, (rows, rows), 0) < tokens
    for pair in range(width // 128):
        at = pair * 128
        queries = projected_ref[0, :, at : at + 128] * jnp.bfloat16(0.125)
        key_rows = projected_ref[1, :, at : at + 128]
        values = projected_ref[2, :, at : at + 128]
        halves = []
        for half in range(2):
            chosen = low_half if half == 0 else ~low_half
            own_queries = jnp.where(chosen, queries, jnp.bfloat16(0))
            scores = lax.dot_general(
                key_rows, own_queries, (((1,), (1,)), ((), ())), preferred_element_type=jnp.float32
            )
            scores = jnp.where(real_key, scores, -1e30)
            raised = jnp.exp(scores - jnp.max(scores, axis=0, keepdims=True))
            probs = raised * (1.0 / jnp.sum(raised, axis=0, keepdims=True))
            probs = probs.astype(jnp.bfloat16)
            probs_ref[2 * pair + half] = probs
            halves.append(
                lax.dot_general(
                    probs, values, (((0,), (0,)), ((), ())), preferred_element_type=jnp.float32
                )
            )
        attended_ref[:, at : at + 128] = jnp.where(low_half, halves[0], halves[1]).astype(
            jnp.bfloat16
        )


def weight_spec(weights, column, section=0):
    _, eighths, rows, width = weights.shape
    return pl.BlockSpec((None, eighths, rows // 3, width), lambda i: (column, 0, section, 0))


def attention_forward(normed, weights, bias, images, tokens):
    total, width = normed.shape
    rows = total // images
    heads = width // 64
    return pl.pallas_call(
        functools.partial(attention_forward_kernel, tokens),
        grid=(images,),
        in_specs=[
            pl.BlockSpec((rows, width), lambda i: (i, 0)),
            weight_spec(weights, 0),
            weight_spec(weights, 1),
            weight_spec(weights, 2),
            pl.BlockSpec((3, 1, width), lambda i: (0, 0, 0)),
        ],
        out_specs=[
            pl.BlockSpec((3, rows, width), lambda i: (0, i, 0)),
            pl.BlockSpec((rows, width), lambda i: (i, 0)),
            pl.BlockSpec((None, heads, rows, rows), lambda i: (i, 0, 0, 0)),
        ],
        out_shape=[
            jax.ShapeDtypeStruct((3, total, width), jnp.bfloat16),
            jax.ShapeDtypeStruct((total, width), jnp.bfloat16),
            jax.ShapeDtypeStruct((images, heads, rows, rows), jnp.bfloat16),
        ],
        compiler_params=pltpu.CompilerParams(vmem_limit_bytes=48 << 20),
        cost_estimate=pl.CostEstimate(
            flops=images * heads * rows * rows * 64 * 4 + 6 * total * width * width,
            bytes_accessed=images * rows * (8 * width + 2 * heads * rows) + 6 * width * width,
            transcendentals=images * heads * rows * rows,
        ),
        name="attention_forward",
    )(normed, weights, weights, weights, bias)


def attention_backward_kernel(
    projected_ref,
    probs_ref,
    normed_grad_ref,
    upstream_ref,
    middle_ref,
    proj_ref,
    gain_ref,
    out_ref,
    middle_grad_ref,
    low_ref,
    sums_ref,
    grad_ref,
):
    _, rows, width = projected_ref.shape
    low_half = lane_half((rows, 128))

    @pl.when(pl.program_id(0) == 0)
    def _():
        sums_ref[...] = jnp.zeros_like(sums_ref)

    def folded(value):
        return jnp.sum(value.reshape(rows // 8, 8, width), axis=0)

    middle = middle_ref[...]
    centre = middle - jnp.mean(middle, axis=-1, keepdims=True)
    spread = jnp.mean(centre * centre, axis=-1, keepdims=True)
    scale = lax.rsqrt(spread + norm_eps)
    normed = centre * scale
    grads = normed_grad_ref[...]
    sums_ref[3] += folded(grads * normed)
    sums_ref[4] += folded(grads)
    grads = grads * gain_ref[...]
    grads = scale * (
        grads
        - jnp.mean(grads, axis=-1, keepdims=True)
        - normed * jnp.mean(grads * normed, axis=-1, keepdims=True)
    )
    grads = upstream_ref[...].astype(jnp.float32) + grads
    middle_grad_ref[...] = grads
    low = grads.astype(jnp.bfloat16)
    low_ref[...] = low
    sums_ref[5] += folded(low.astype(jnp.float32))
    grad_ref[...] = lax.dot_general(
        low,
        proj_ref[...].reshape(width, width),
        (((1,), (1,)), ((), ())),
        preferred_element_type=jnp.float32,
    ).astype(jnp.bfloat16)
    for pair in range(width // 128):
        at = pair * 128
        queries = projected_ref[0, :, at : at + 128]
        key_rows = projected_ref[1, :, at : at + 128]
        values = projected_ref[2, :, at : at + 128]
        grads = grad_ref[:, at : at + 128]
        found = []
        for half in range(2):
            chosen = low_half if half == 0 else ~low_half
            probs = probs_ref[2 * pair + half]
            own_grads = jnp.where(chosen, grads, jnp.bfloat16(0))
            grad_values = jnp.dot(probs, grads, preferred_element_type=jnp.float32)
            grad_probs = lax.dot_general(
                values, own_grads, (((1,), (1,)), ((), ())), preferred_element_type=jnp.float32
            )
            wide = probs.astype(jnp.float32)
            weighted = grad_probs * wide
            total = jnp.sum(weighted, axis=0, keepdims=True)
            grad_scores = (weighted - wide * total).astype(jnp.bfloat16)
            grad_keys = jnp.dot(grad_scores, queries, preferred_element_type=jnp.float32) * 0.125
            grad_queries = (
                lax.dot_general(
                    grad_scores,
                    key_rows,
                    (((0,), (0,)), ((), ())),
                    preferred_element_type=jnp.float32,
                )
                * 0.125
            )
            found.append((grad_queries, grad_keys, grad_values))
        for kind in range(3):
            joined = jnp.where(low_half, found[0][kind], found[1][kind]).astype(jnp.bfloat16)
            place = slice(at, at + 128)
            out_ref[kind, :, place] = joined
            sums_ref[kind, :, place] += jnp.sum(
                joined.astype(jnp.float32).reshape(rows // 8, 8, 128), axis=0
            )


def attention_backward(projected, probs, normed_grad, upstream, middle, weights, gain, images):
    _, total, width = projected.shape
    rows = total // images
    heads = width // 64
    row = pl.BlockSpec((rows, width), lambda i: (i, 0))
    return pl.pallas_call(
        attention_backward_kernel,
        grid=(images,),
        in_specs=[
            pl.BlockSpec((3, rows, width), lambda i: (0, i, 0)),
            pl.BlockSpec((None, heads, rows, rows), lambda i: (i, 0, 0, 0)),
            row,
            row,
            row,
            weight_spec(weights, 3),
            pl.BlockSpec((1, width), lambda i: (0, 0)),
        ],
        out_specs=[
            pl.BlockSpec((3, rows, width), lambda i: (0, i, 0)),
            row,
            row,
            pl.BlockSpec((6, 8, width), lambda i: (0, 0, 0)),
        ],
        out_shape=[
            pltpu.HBM((3, total, width), jnp.bfloat16),
            pltpu.HBM((total, width), jnp.float32),
            pltpu.HBM((total, width), jnp.bfloat16),
            jax.ShapeDtypeStruct((6, 8, width), jnp.float32),
        ],
        scratch_shapes=[pltpu.VMEM((rows, width), jnp.bfloat16)],
        compiler_params=pltpu.CompilerParams(vmem_limit_bytes=48 << 20),
        cost_estimate=pl.CostEstimate(flops=0, bytes_accessed=0, transcendentals=0),
        name="attention_backward",
    )(projected, probs, normed_grad, upstream, middle, weights, gain)


SLOT_ROWS = 16


def exact_dot(left, right, contract=((1,), (0,))):
    return lax.dot_general(
        left,
        right,
        (contract, ((), ())),
        precision=highest_precision,
        preferred_element_type=jnp.float32,
    )


def rows_norm(values, norm_gain, norm_shift, epsilon):
    centre = values - jnp.mean(values, axis=-1, keepdims=True)
    spread = jnp.mean(centre * centre, axis=-1, keepdims=True)
    return centre * lax.rsqrt(spread + epsilon) * norm_gain + norm_shift


def gelu_rows(values):
    return values * (0.5 + 0.5 * lax.erf(values * 0.7071067811865476))


def hyper_rows(params, waves, usable, slots):
    (
        tokens,
        bias_tok,
        qkv_w,
        qv_b,
        out_w,
        out_b,
        gain_one,
        shift_one,
        ff_in,
        ff_in_b,
        ff_out,
        ff_out_b,
        gain_two,
        shift_two,
    ) = params
    width = tokens.shape[1]
    head_dim = width // WHEADS
    total = waves.shape[0]
    place = lax.broadcasted_iota(jnp.int32, (total, 1), 0) & (SLOT_ROWS - 1)
    query_rows = jnp.where(place == slots, jnp.broadcast_to(bias_tok, (total, width)), waves)
    joined = jnp.concatenate([tokens, query_rows], axis=0)
    queries = exact_dot(query_rows, qkv_w[:, :width]) + qv_b[:, :width]
    key_rows = exact_dot(joined, qkv_w[:, width : 2 * width])
    values = exact_dot(joined, qkv_w[:, 2 * width :]) + qv_b[:, width:]
    head_at = lax.broadcasted_iota(jnp.int32, (1, width), 1)
    mixture = jnp.zeros((total, width), jnp.float32)
    for head in range(WHEADS):
        own = ((head_at >= head * head_dim) & (head_at < (head + 1) * head_dim)).astype(jnp.float32)
        scores = exact_dot(queries * own, key_rows, ((1,), (1,))) * head_dim ** (-0.5)
        scores = jnp.where(usable > 0, scores, -1e30)
        raised = jnp.exp(scores - lax.stop_gradient(jnp.max(scores, axis=-1, keepdims=True)))
        weights = raised / jnp.sum(raised, axis=-1, keepdims=True)
        mixture = mixture + exact_dot(weights, values) * own
    first = rows_norm(query_rows + exact_dot(mixture, out_w) + out_b, gain_one, shift_one, hyper_eps)
    hidden = gelu_rows(exact_dot(first, ff_in) + ff_in_b)
    return rows_norm(first + exact_dot(hidden, ff_out) + ff_out_b, gain_two, shift_two, hyper_eps)


def usable_rows(band_counts, slots, token_rows):
    groups = band_counts.shape[0]
    total = groups * SLOT_ROWS
    row = jnp.arange(total)
    own_group = row[:, None] // SLOT_ROWS == row[None, :] // SLOT_ROWS
    place = row % SLOT_ROWS
    present = (place < jnp.repeat(band_counts, SLOT_ROWS)) | (place == slots)
    return jnp.concatenate(
        [jnp.ones((total, token_rows)), (own_group & present[None, :]).astype(jnp.float32)], axis=1
    )


def hyper_params_2d(params):
    return tuple(member[None] if member.ndim == 1 else member for member in params)


def wave_rows(indices, width):
    groups, slots = indices.shape
    waves = jax.vmap(lambda row: wave_embed(row, width))(indices)
    return jnp.pad(waves, ((0, 0), (0, SLOT_ROWS - slots), (0, 0))).reshape(-1, width)


def hyper_forward_kernel(slots, waves_ref, usable_ref, *refs):
    refs[-1][...] = hyper_rows(
        tuple(ref[...] for ref in refs[:-1]), waves_ref[...], usable_ref[...], slots
    )


def hyper_backward_kernel(slots, waves_ref, usable_ref, grads_ref, *refs):
    count = len(refs) // 2
    waves, usable = waves_ref[...], usable_ref[...]
    _, pull = jax.vjp(
        lambda params: hyper_rows(params, waves, usable, slots),
        tuple(ref[...] for ref in refs[:count]),
    )
    (found,) = pull(grads_ref[...])
    for ref, value in zip(refs[count:], found):
        ref[...] = value


def hyper_forward_call(params, waves, usable, slots):
    return pl.pallas_call(
        functools.partial(hyper_forward_kernel, slots),
        out_shape=jax.ShapeDtypeStruct(waves.shape, jnp.float32),
        name="hyper_forward",
    )(waves, usable, *params)


def hyper_backward_call(params, waves, usable, grads, slots):
    return pl.pallas_call(
        functools.partial(hyper_backward_kernel, slots),
        out_shape=[jax.ShapeDtypeStruct(member.shape, jnp.float32) for member in params],
        name="hyper_backward",
    )(waves, usable, grads, *params)


def embed_kernel(
    bands, small_at, core_ref, line_ref, other_ref, pixels_ref, kernels_ref, stream_ref, normed_ref, rows_ref
):
    chips, _, width = line_ref.shape
    part = kernels_ref.shape[0] // (2 * chips * bands)
    shard = width // (2 * chips)

    @pl.when(pl.program_id(0) == 0)
    def _():
        for core in range(2):
            low_ref, high_ref = (line_ref, other_ref) if core == 0 else (other_ref, line_ref)

            @pl.when((core_ref[0] == 0) == (core == 0))
            def _():
                for chip in range(chips):
                    for band in range(bands):
                        place = (band * chips + chip) * 2 * part
                        here = slice(band * part, (band + 1) * part)
                        kernels_ref[place : place + part] = low_ref[chip, here]
                        kernels_ref[place + part : place + 2 * part] = high_ref[chip, here]
                    for which, ref in enumerate((low_ref, high_ref)):
                        small = ref[chip, small_at : small_at + 16, :shard].astype(jnp.float32)
                        at = (chip * 2 + which) * shard
                        rows_ref[:, at : at + shard] = small

    shift = rows_ref[0:1] + rows_ref[1:2]
    stream = (
        jnp.dot(pixels_ref[...], kernels_ref[...], preferred_element_type=jnp.float32) + shift
    )
    stream_ref[...] = stream
    centre = stream - jnp.mean(stream, axis=-1, keepdims=True)
    spread = jnp.mean(centre * centre, axis=-1, keepdims=True)
    normed = centre * lax.rsqrt(spread + norm_eps) * rows_ref[2:3] + rows_ref[3:4]
    normed_ref[...] = normed.astype(jnp.bfloat16)


def embed(core, line, other, pixel_rows, images, bands, small_at):
    width = line.shape[2]
    total, depth = pixel_rows.shape
    rows = total // images
    part_spec = pl.BlockSpec(line.shape, lambda i, core_ref: (0, 0, 0))
    row = pl.BlockSpec((rows, width), lambda i, core_ref: (i, 0))
    return pl.pallas_call(
        functools.partial(embed_kernel, bands, small_at),
        grid_spec=pltpu.PrefetchScalarGridSpec(
            num_scalar_prefetch=1,
            grid=(images,),
            in_specs=[
                part_spec,
                part_spec,
                pl.BlockSpec((rows, depth), lambda i, core_ref: (i, 0)),
            ],
            out_specs=[pl.BlockSpec((depth, width), lambda i, core_ref: (0, 0)), row, row],
            scratch_shapes=[pltpu.VMEM((16, width), jnp.float32)],
        ),
        out_shape=[
            jax.ShapeDtypeStruct((depth, width), jnp.bfloat16),
            jax.ShapeDtypeStruct((total, width), jnp.float32),
            jax.ShapeDtypeStruct((total, width), jnp.bfloat16),
        ],
        compiler_params=pltpu.CompilerParams(vmem_limit_bytes=48 << 20),
        cost_estimate=pl.CostEstimate(
            flops=2 * total * width * depth,
            bytes_accessed=total * (2 * depth + 6 * width) + 4 * depth * width,
            transcendentals=total,
        ),
        name="embed",
    )(core, line, other, pixel_rows)


def first_backward_kernel(
    bands,
    core_ref,
    projected_ref,
    query_ref,
    key_ref,
    value_ref,
    stream_ref,
    residual_ref,
    gain_ref,
    pixels_ref,
    out_ref,
    keep_ref,
    send_ref,
    sums_ref,
    low_ref,
    total_ref,
):
    rows, width = stream_ref.shape
    chips, part, _ = keep_ref.shape
    part //= bands

    @pl.when(pl.program_id(0) == 0)
    def _():
        sums_ref[...] = jnp.zeros_like(sums_ref)

    def folded(value):
        return jnp.sum(value.reshape(rows // 8, 8, width), axis=0)

    grads = sum(
        lax.dot_general(
            projected_ref[at],
            ref[...].reshape(width, width),
            (((1,), (1,)), ((), ())),
            preferred_element_type=jnp.float32,
        )
        for at, ref in enumerate((query_ref, key_ref, value_ref))
    )
    stream = stream_ref[...]
    centre = stream - jnp.mean(stream, axis=-1, keepdims=True)
    spread = jnp.mean(centre * centre, axis=-1, keepdims=True)
    scale = lax.rsqrt(spread + norm_eps)
    normed = centre * scale
    sums_ref[0] += folded(grads * normed)
    sums_ref[1] += folded(grads)
    grads = grads * gain_ref[...]
    grads = scale * (
        grads
        - jnp.mean(grads, axis=-1, keepdims=True)
        - normed * jnp.mean(grads * normed, axis=-1, keepdims=True)
    )
    low = (residual_ref[...] + grads).astype(jnp.bfloat16)
    out_ref[...] = low
    sums_ref[2] += folded(low.astype(jnp.float32))
    low_ref[pl.ds(pl.multiple_of(pl.program_id(0) * rows, 16), rows), :] = low

    @pl.when(pl.program_id(0) == pl.num_programs(0) - 1)
    def _():
        total_ref[...] = jnp.dot(
            pixels_ref[...], low_ref[...], preferred_element_type=jnp.float32
        ).astype(jnp.bfloat16)

    for core in range(2):
        low_ref, high_ref = (keep_ref, send_ref) if core == 0 else (send_ref, keep_ref)

        @pl.when((pl.program_id(0) == pl.num_programs(0) - 1) & ((core_ref[0] == 0) == (core == 0)))
        def _():
            for chip in range(chips):
                for band in range(bands):
                    place = (band * chips + chip) * 2 * part
                    here = slice(band * part, (band + 1) * part)
                    made = total_ref[place : place + 2 * part]
                    low_ref[chip, here] = made[:part]
                    high_ref[chip, here] = made[part:]


def first_backward(
    core, grad_projected, weights, stream, residual, gain, pixel_columns, images, shards, bands
):
    total, width = stream.shape
    rows = total // images
    depth = pixel_columns.shape[0]
    row = pl.BlockSpec((rows, width), lambda i, core_ref: (i, 0))
    made = (shards // 2, depth // shards, width)
    part = pl.BlockSpec(made, lambda i, core_ref: (0, 0, 0))

    def column(at):
        _, eighths, shard, _ = weights.shape
        return pl.BlockSpec(
            (None, eighths, shard // 3, width), lambda i, core_ref: (at, 0, 0, 0)
        )

    return pl.pallas_call(
        functools.partial(first_backward_kernel, bands),
        grid_spec=pltpu.PrefetchScalarGridSpec(
            num_scalar_prefetch=1,
            grid=(images,),
        in_specs=[
            pl.BlockSpec((3, rows, width), lambda i, core_ref: (0, i, 0)),
            column(0),
            column(1),
            column(2),
            row,
            row,
            pl.BlockSpec((1, width), lambda i, core_ref: (0, 0)),
            pl.BlockSpec((depth, total), lambda i, core_ref: (0, 0)),
        ],
        out_specs=[
            row,
            part,
            part,
            pl.BlockSpec((3, 8, width), lambda i, core_ref: (0, 0, 0)),
        ],
        scratch_shapes=[
                pltpu.VMEM((total, width), jnp.bfloat16),
                pltpu.VMEM((depth, width), jnp.bfloat16),
            ],
        ),
        out_shape=[
            jax.ShapeDtypeStruct((total, width), jnp.bfloat16),
            jax.ShapeDtypeStruct(made, jnp.bfloat16),
            jax.ShapeDtypeStruct(made, jnp.bfloat16),
            jax.ShapeDtypeStruct((3, 8, width), jnp.float32),
        ],
        compiler_params=pltpu.CompilerParams(vmem_limit_bytes=48 << 20),
        cost_estimate=pl.CostEstimate(flops=0, bytes_accessed=0, transcendentals=0),
        name="first_backward",
    )(core, grad_projected, weights, weights, weights, stream, residual, gain, pixel_columns)


def late_kernel(
    core_ref,
    normed_ref,
    attended_ref,
    projected_ref,
    branch_ref,
    vectors_ref,
    keep_ref,
    send_ref,
    turned_ref,
    made_ref,
):
    at_step = pl.program_id(0)
    width = normed_ref.shape[1]
    pairs = keep_ref.shape[0]
    each = width // (2 * pairs)

    @pl.when(at_step == 0)
    def _():
        turned_ref[...] = normed_ref[...].T

    @pl.when(at_step == 3)
    def _():
        turned_ref[...] = attended_ref[...].T

    @pl.when(at_step < 3)
    def _():
        made = jnp.dot(turned_ref[...], projected_ref[...], preferred_element_type=jnp.float32)
        made_ref[...] = made.astype(jnp.bfloat16).reshape(made_ref.shape)

    @pl.when(at_step == 3)
    def _():
        made = jnp.dot(turned_ref[...], branch_ref[...], preferred_element_type=jnp.float32)
        made_ref[...] = made.astype(jnp.bfloat16).reshape(made_ref.shape)

    for core in range(2):
        low_ref, high_ref = (keep_ref, send_ref) if core == 0 else (send_ref, keep_ref)
        for step in range(4):

            @pl.when((at_step == step) & ((core_ref[0] == 0) == (core == 0)))
            def _():
                here = slice(step * each, (step + 1) * each)
                for pair in range(pairs):
                    low_ref[pair, here] = made_ref[2 * pair]
                    high_ref[pair, here] = made_ref[2 * pair + 1]
                    if step == 0:
                        low_ref[pair, 4 * each :] = vectors_ref[2 * pair]
                        high_ref[pair, 4 * each :] = vectors_ref[2 * pair + 1]


def late_gradients(core, normed, attended, grad_projected, branch, vectors):
    total, width = normed.shape
    devices, extra, _ = vectors.shape
    each = width // devices
    made = (devices // 2, 4 * each + extra, width)
    whole = pl.BlockSpec((total, width), lambda i, core_ref: (0, 0))
    part = pl.BlockSpec(made, lambda i, core_ref: (0, 0, 0))
    return pl.pallas_call(
        late_kernel,
        grid_spec=pltpu.PrefetchScalarGridSpec(
            num_scalar_prefetch=1,
            grid=(4,),
            in_specs=[
                whole,
                whole,
                pl.BlockSpec((None, total, width), lambda i, core_ref: (jnp.minimum(i, 2), 0, 0)),
                whole,
                pl.BlockSpec(vectors.shape, lambda i, core_ref: (0, 0, 0)),
            ],
            out_specs=[part, part],
            scratch_shapes=[
                pltpu.VMEM((width, total), jnp.bfloat16),
                pltpu.VMEM((devices, each, width), jnp.bfloat16),
            ],
        ),
        out_shape=[jax.ShapeDtypeStruct(made, jnp.bfloat16)] * 2,
        compiler_params=pltpu.CompilerParams(vmem_limit_bytes=48 << 20),
        cost_estimate=pl.CostEstimate(flops=0, bytes_accessed=0, transcendentals=0),
        name="late_gradients",
    )(core, normed, attended, grad_projected, branch, vectors)


def mlp_kernel(
    block,
    devices,
    rows_ref,
    upstream_ref,
    first_weight_ref,
    second_weight_ref,
    b1_ref,
    sums_ref,
    out_ref,
    grad_ref,
    packed_ref,
    turned_ref,
    act_ref,
    gate_ref,
    first_ref,
    second_ref,
    sems,
):
    at_step = pl.program_id(0)
    steps = pl.num_programs(0)
    total, width = rows_ref.shape
    eighths, shard, hidden_block = first_weight_ref.shape
    quarters, group, _, _ = second_weight_ref.shape
    w1 = first_weight_ref[...].reshape(width, hidden_block)
    w2 = jnp.concatenate(
        [second_weight_ref[at, eighth] for eighth in range(group) for at in range(quarters)]
    )
    first_rows = width // devices
    second_devices = devices // steps
    second_rows = hidden_block // second_devices

    def copies(step):
        found = []
        for core in range(2):
            found.append(
                pltpu.make_async_copy(
                    first_ref.at[:, core],
                    packed_ref.at[core, :, pl.ds(step * first_rows, first_rows), :],
                    sems.at[2 * core],
                )
            )
            found.append(
                pltpu.make_async_copy(
                    second_ref.at[:, core],
                    packed_ref.at[
                        core,
                        pl.ds(step * (second_devices // 2), second_devices // 2),
                        pl.ds(steps * first_rows, second_rows),
                        :,
                    ],
                    sems.at[2 * core + 1],
                )
            )
        return found

    @pl.when(at_step == 0)
    def _():
        out_ref[...] = jnp.zeros_like(out_ref)
        grad_ref[...] = jnp.zeros_like(grad_ref)
        turned_ref[...] = rows_ref[...].T

    for at in range(0, total, block):
        here = slice(at, at + block)
        gate_in = (
            jnp.dot(rows_ref[here], w1, preferred_element_type=jnp.float32) + b1_ref[...]
        )
        grad_act = lax.dot_general(
            upstream_ref[here],
            w2,
            (((1,), (1,)), ((), ())),
            preferred_element_type=jnp.float32,
        )
        chance = 0.5 + 0.5 * lax.erf(gate_in * 0.7071067811865476)
        density = 0.3989422804014327 * jnp.exp(-0.5 * gate_in * gate_in)
        act = (gate_in * chance).astype(jnp.bfloat16)
        gate = (grad_act * (chance + gate_in * density)).astype(jnp.bfloat16)
        act_ref[here] = act
        gate_ref[here] = gate
        wide = gate.astype(jnp.float32)
        part = jnp.sum(wide.reshape(block // 8, 8, wide.shape[1]), axis=0)
        sums_ref[...] = part if at == 0 else sums_ref[...] + part
        out_ref[here] += jnp.dot(act, w2, preferred_element_type=jnp.float32)
        grad_ref[here] += lax.dot_general(
            gate, w1, (((1,), (1,)), ((), ())), preferred_element_type=jnp.float32
        )

    @pl.when(at_step > 0)
    def _():
        for copy in copies(at_step - 1):
            copy.wait()

    first = jnp.dot(turned_ref[...], gate_ref[...], preferred_element_type=jnp.float32)
    first_ref[...] = first.astype(jnp.bfloat16).reshape(first_ref.shape)
    second = lax.dot_general(
        act_ref[...], upstream_ref[...], (((0,), (0,)), ((), ())), preferred_element_type=jnp.float32
    )
    second_ref[...] = second.astype(jnp.bfloat16).reshape(second_ref.shape)
    for copy in copies(at_step):
        copy.start()

    @pl.when(at_step == steps - 1)
    def _():
        for copy in copies(at_step):
            copy.wait()


def mlp(rows, upstream, weights, b1, row_block, devices):
    total, width = rows.shape
    steps, eighths, shard, hidden_block = weights.shape
    shard //= 3
    hidden = steps * hidden_block
    whole = pl.BlockSpec((total, width), lambda i: (0, 0))
    packed_rows = (width * steps + hidden) // devices
    return pl.pallas_call(
        functools.partial(mlp_kernel, row_block, devices),
        grid=(steps,),
        in_specs=[
            whole,
            whole,
            pl.BlockSpec((None, eighths, shard, hidden_block), lambda i: (i, 0, 1, 0)),
            pl.BlockSpec((steps, eighths // steps, shard, width), lambda i: (0, i, 2, 0)),
            pl.BlockSpec((1, hidden_block), lambda i: (0, i)),
        ],
        out_specs=[
            pl.BlockSpec((8, hidden_block), lambda i: (0, i)),
            whole,
            whole,
            pl.BlockSpec(memory_space=pl.ANY),
        ],
        out_shape=[
            jax.ShapeDtypeStruct((8, hidden), jnp.float32),
            jax.ShapeDtypeStruct((total, width), jnp.float32),
            jax.ShapeDtypeStruct((total, width), jnp.float32),
            jax.ShapeDtypeStruct((2, devices // 2, packed_rows, width), jnp.bfloat16),
        ],
        scratch_shapes=[
            pltpu.VMEM((width, total), jnp.bfloat16),
            pltpu.VMEM((total, hidden_block), jnp.bfloat16),
            pltpu.VMEM((total, hidden_block), jnp.bfloat16),
            pltpu.VMEM((devices // 2, 2, width // devices, width), jnp.bfloat16),
            pltpu.VMEM((devices // steps // 2, 2, hidden // devices, width), jnp.bfloat16),
            pltpu.SemaphoreType.DMA((4,)),
        ],
        compiler_params=pltpu.CompilerParams(vmem_limit_bytes=52 << 20),
        cost_estimate=pl.CostEstimate(
            flops=12 * total * width * hidden,
            bytes_accessed=8 * width * hidden + 12 * total * width,
            transcendentals=2 * total * hidden,
        ),
        name="mlp",
    )(rows, upstream, weights, weights, b1)


def pixel_grad_kernel(grad_ref, kernels_ref, out_ref):
    tokens, bands, patch = out_ref.shape
    for band in range(bands):
        found = lax.dot_general(
            grad_ref[...],
            kernels_ref[band * patch : (band + 1) * patch, :],
            (((1,), (1,)), ((), ())),
            preferred_element_type=jnp.float32,
        )
        out_ref[:, band, :] = found[:tokens]


def pixel_grad(grads, kernels, images, tokens, bands):
    total, width = grads.shape
    patch = kernels.shape[0] // bands
    return pl.pallas_call(
        pixel_grad_kernel,
        grid=(images,),
        in_specs=[
            pl.BlockSpec((total // images, width), lambda i: (i, 0)),
            pl.BlockSpec(kernels.shape, lambda i: (0, 0)),
        ],
        out_specs=pl.BlockSpec((None, tokens, bands, patch), lambda i: (i, 0, 0, 0)),
        out_shape=jax.ShapeDtypeStruct((images, tokens, bands, patch), jnp.float32),
        compiler_params=pltpu.CompilerParams(vmem_limit_bytes=48 << 20),
        cost_estimate=pl.CostEstimate(flops=0, bytes_accessed=0, transcendentals=0),
        name="pixel_grad",
    )(grads, kernels)


def ordered_gather(value, axis):
    total = lax.axis_size(axis)
    at = lax.axis_index(axis)
    slots = jnp.arange(total).reshape((total,) + (1,) * value.ndim)
    gathered = jnp.where(slots == at, value[None], jnp.zeros((), value.dtype))
    for shift in range(1, total):
        moved = lax.ppermute(value, axis, [(i, (i + shift) % total) for i in range(total)])
        gathered = jnp.where(slots == (at - shift) % total, moved[None], gathered)
    return gathered


def local(
    pixels,
    cotangent,
    band_count,
    wave_index,
    weight_tokens,
    bias_token,
    hyper_qkv,
    hyper_qv_bias,
    hyper_out,
    hyper_out_bias,
    hyper_norm1_gain,
    hyper_norm1_bias,
    hyper_ff1,
    hyper_ff1_bias,
    hyper_ff2,
    hyper_ff2_bias,
    hyper_norm2_gain,
    hyper_norm2_bias,
    kernel_gen,
    kernel_gen_bias,
    conv_bias_gen,
    conv_bias_gen_bias,
    norm1_gain,
    norm1_bias,
    qkv_weight,
    qv_bias,
    proj_weight,
    proj_bias,
    norm2_gain,
    norm2_bias,
    fc1_weight,
    fc1_bias,
    fc2_weight,
    fc2_bias,
):
    group_total = lax.axis_size("grp")
    shard_total = lax.axis_size(SHARDS)
    group_at = lax.axis_index("grp")
    shard_at = lax.axis_index(SHARDS)
    images = pixels.shape[0]
    slot_count = pixels.shape[1]
    tokens = pixels.shape[2]
    patch = pixels.shape[3]
    model_width = cotangent.shape[2]
    padded = -(-tokens // 16) * 16
    row_count = images * padded

    def pad_rows(value):
        return jnp.pad(value, ((0, 0), (0, padded - tokens), (0, 0))).reshape(row_count, -1)

    band_total = band_count[0]
    band_mask = (jnp.arange(slot_count) < band_total).astype(jnp.float32)
    hyper_params = (
        weight_tokens,
        bias_token,
        hyper_qkv,
        hyper_qv_bias,
        hyper_out,
        hyper_out_bias,
        hyper_norm1_gain,
        hyper_norm1_bias,
        hyper_ff1,
        hyper_ff1_bias,
        hyper_ff2,
        hyper_ff2_bias,
        hyper_norm2_gain,
        hyper_norm2_bias,
    )
    hyper_wide = weight_tokens.shape[1]
    flat_params = hyper_params_2d(hyper_params)
    shard_patch = kernel_gen.shape[0]
    shard_rows = proj_weight.shape[0]
    lanes = hyper_wide
    folds = model_width // lanes
    fold_rows = shard_rows // folds
    small = [
        conv_bias_gen_bias,
        norm1_gain,
        norm1_bias,
        qv_bias,
        proj_bias,
        norm2_gain,
        norm2_bias,
        fc1_bias,
        fc2_bias,
    ]
    kernel_total = slot_count * shard_patch
    own_waves = wave_rows(wave_index, hyper_wide)
    own_usable = usable_rows(band_count, slot_count, weight_tokens.shape[0])

    def hyper_call():
        return hyper_forward_call(flat_params, own_waves, own_usable, slot_count)

    def all_call(tie):
        table = jnp.concatenate([band_count, wave_index[0]])
        every = ordered_gather(together(table, tie)[0], "grp")
        waves = wave_rows(every[:, 1:], hyper_wide)
        usable = usable_rows(every[:, 0], slot_count, weight_tokens.shape[0])
        return waves, usable, hyper_forward_call(flat_params, waves, usable, slot_count)

    def kernel_call(rows):
        hidden = (rows[:slot_count] + own_waves[:slot_count]).astype(jnp.bfloat16)
        made = (
            jnp.einsum("be,pde->bpd", hidden, kernel_gen, preferred_element_type=jnp.float32)
            + kernel_gen_bias.astype(jnp.float32)[None]
        )
        made = (made * band_mask[:, None, None]).astype(jnp.bfloat16)
        *members, small_gen, _ = together(*small, conv_bias_gen, rows)
        shift = jnp.dot(
            small_gen.astype(jnp.float32), rows[slot_count], precision=highest_precision
        ) + members[0].astype(jnp.float32)
        upper = lax.optimization_barrier(shift.astype(jnp.bfloat16))
        lower = (shift - upper.astype(jnp.float32)).astype(jnp.bfloat16)
        small_rows = jnp.stack(
            [
                jnp.pad(member, (0, model_width - member.shape[0]))
                for member in [upper, lower] + members[1:]
            ]
        )
        folded = jnp.concatenate(
            [small_gen[at * fold_rows : (at + 1) * fold_rows] for at in range(folds)], axis=1
        )
        packed = jnp.concatenate([jnp.pad(small_rows, ((0, 16 - len(small) - 1), (0, 0))), folded])
        packed = jnp.pad(packed, ((0, -packed.shape[0] % 16), (0, 0)))
        return jnp.concatenate([made.reshape(kernel_total, model_width), packed])

    def rows_call(tie):
        pixels_here, cotangent_here = pixels, cotangent
        if tie is not None:
            pixels_here, cotangent_here, _ = together(pixels, cotangent, tie)
        pixel_rows = pixels_here.transpose(0, 2, 1, 3).reshape(images, tokens, slot_count * patch)
        pixel_rows = pad_rows(pixel_rows)
        return pixel_rows, pad_rows(cotangent_here), pixel_rows.T

    weights_full = gather_weights(qkv_weight, proj_weight, fc1_weight, fc2_weight)
    core_at = (lax.axis_index(SHARDS) % 2).astype(jnp.int32).reshape(1)
    line, other, (pixel_rows, upstream_low, pixel_columns) = gather_kernels(kernel_call(hyper_call()), rows_call)
    patch_kernels, stream, normed_low = embed(
        core_at,
        line,
        other,
        pixel_rows,
        images,
        slot_count,
        kernel_total,
    )
    found_small = line[:, kernel_total:], other[:, kernel_total:]
    small_line, small_other, _ = together(*found_small, normed_low)
    packed = in_order(lax.axis_index(SHARDS) % 2, small_line, small_other, 1)
    packed = packed.reshape((shard_total,) + packed.shape[2:])
    folded = packed[:, 16 : 16 + fold_rows]
    cb_weight = jnp.concatenate(
        [folded[:, :, at : at + lanes] for at in range(0, model_width, lanes)], axis=1
    ).reshape(model_width, lanes)
    gain_one, _, qv_full, proj_shift, gain_two, shift_two, fc1_shift, fc2_shift = (
        packed[:, 2 + at, : member.shape[0]].reshape(-1) for at, member in enumerate(small[1:])
    )
    proj_full = weights_full[3, :, : weights_full.shape[2] // 3].reshape(model_width, model_width)
    full_bias = jnp.stack(
        [qv_full[:model_width], jnp.zeros((model_width,), jnp.bfloat16), qv_full[model_width:]]
    ).astype(jnp.float32)
    all_waves, all_usable, all_rows = all_call(normed_low)
    normed_low, all_rows = together(normed_low, all_rows)
    projected, attended, attn_probs = attention_forward(
        normed_low, weights_full, full_bias[:, None], images, tokens
    )
    all_rows = all_rows.reshape(group_total, SLOT_ROWS, hyper_wide)
    hidden_all = all_rows[:, :slot_count] + all_waves.reshape(all_rows.shape)[:, :slot_count]
    bias_row_all = all_rows[:, slot_count]
    middle = (
        stream
        + jnp.dot(attended, proj_full, preferred_element_type=jnp.float32)
        + proj_shift.astype(jnp.float32)
    )
    normed_two = layer_norm(
        middle, gain_two.astype(jnp.float32), shift_two.astype(jnp.float32), norm_eps
    )
    normed_two_low = normed_two.astype(jnp.bfloat16)
    upstream = upstream_low.astype(jnp.float32)
    gate_sums, update, grad_normed_two, early_block = mlp(
        normed_two_low,
        upstream_low,
        weights_full,
        fc1_shift.astype(jnp.float32)[None],
        row_count // 2,
        group_total * shard_total if torus_block() else 32,
    )
    grad_fc2_shift = jnp.sum(upstream, axis=0)
    grad_fc1_shift = jnp.sum(gate_sums, axis=0)
    early = sum_cores(early_block)
    grad_projected, grad_middle, middle_low, block_sums = attention_backward(
        projected,
        attn_probs,
        grad_normed_two,
        upstream_low,
        middle,
        weights_full,
        gain_two.astype(jnp.float32)[None],
        images,
    )
    early, grad_projected = together(early, grad_projected)
    early = sum_groups(early)
    block_sums = jnp.sum(block_sums, axis=1)
    grad_qv = jnp.concatenate([block_sums[0], block_sums[2]])
    grad_gain_two, grad_shift_two, grad_proj_shift = block_sums[3:]
    device_total = group_total * shard_total
    block_rows = model_width // device_total

    vectors = [
        grad_qv,
        grad_proj_shift,
        grad_gain_two,
        grad_shift_two,
        grad_fc1_shift,
        grad_fc2_shift,
    ]
    vector_lengths = [member.shape[0] // device_total for member in vectors]

    vector_block = jnp.concatenate(
        [member.reshape(device_total, -1) for member in vectors], axis=1
    ).astype(jnp.bfloat16)
    extra = -(-vector_block.shape[1] // model_width)
    extra += -(4 * block_rows + extra) % 8
    vector_block = jnp.pad(
        vector_block, ((0, 0), (0, extra * model_width - vector_block.shape[1]))
    ).reshape(device_total, extra, model_width)
    late, grad_projected = start_late(
        *late_gradients(core_at, normed_low, attended, grad_projected, middle_low, vector_block),
        grad_projected,
    )
    residual_reduced, keep_kernels, send_kernels, first_sums = first_backward(
        core_at,
        grad_projected,
        weights_full,
        stream,
        grad_middle,
        gain_one.astype(jnp.float32)[None],
        pixel_columns,
        images,
        shard_total,
        slot_count,
    )
    grad_gain_one, grad_shift_one, grad_conv_shift = jnp.sum(first_sums, axis=1)

    def pixels_call(tie):
        grads = residual_reduced if tie is None else together(residual_reduced, tie)[0]
        return pixel_grad(grads, patch_kernels, images, tokens, slot_count).transpose(0, 2, 1, 3)

    def out_call(tie):
        here = update if tie is None else together(update, tie)[0]
        block_out = middle + here + fc2_shift.astype(jnp.float32)
        return block_out.reshape(images, padded, model_width)[:, :tokens]

    grad_bias_row_part = jnp.dot(
        grad_conv_shift, cb_weight.astype(jnp.float32), precision=highest_precision
    )
    def code_call(group_kernels):
        grad_hidden_part = jnp.einsum(
            "bpd,pde->be",
            group_kernels.reshape(slot_count, shard_patch, model_width)
            * band_mask[:, None, None],
            kernel_gen.astype(jnp.float32),
            precision=highest_precision,
        )
        return jnp.concatenate(
            [grad_hidden_part, grad_bias_row_part[None]]
            + [
                member.reshape(-1, hyper_wide)
                for member in (grad_conv_shift, grad_gain_one, grad_shift_one)
            ]
        )

    group_width = model_width // group_total
    code_all = hidden_all.astype(jnp.bfloat16).astype(jnp.float32)

    def gen_call(group_kernels):
        group_kernels = group_kernels.reshape(slot_count, shard_patch, model_width)
        grad_pre = group_kernels * band_mask[:, None, None]
        swapped = lax.all_to_all(
            grad_pre.reshape(slot_count, shard_patch, group_total, group_width).transpose(
                2, 0, 1, 3
            ),
            "grp",
            0,
            0,
        ).reshape(group_total * slot_count, shard_patch, group_width)
        grad_gen = jnp.einsum(
            "kpd,ke->pde",
            swapped,
            code_all.reshape(group_total * slot_count, hyper_wide),
            precision=highest_precision,
        )
        return grad_gen, jnp.sum(swapped, axis=0)

    early_sum, late_terms, code_grads, filled = reduce_late(
        keep_kernels, send_kernels, early, late, code_call, [pixels_call, out_call], gen_call
    )
    grad_pixels, block_out, (grad_gen, grad_gen_shift) = filled
    fold_total = model_width // hyper_wide
    conv_parts, gain_parts, shift_parts = (
        code_grads[:, slot_count + 1 + at * fold_total : slot_count + 1 + (at + 1) * fold_total].reshape(
            group_total, model_width
        )
        for at in range(3)
    )
    code_grads = jnp.pad(
        code_grads[:, : slot_count + 1], ((0, 0), (0, SLOT_ROWS - slot_count - 1), (0, 0))
    ).reshape(-1, hyper_wide)
    hyper_total = hyper_backward_call(flat_params, all_waves, all_usable, code_grads, slot_count)
    late_terms, *hyper_total, early_sum = together(late_terms, *hyper_total, early_sum)
    late_out = scatter_end(late_terms)
    hyper_total = [
        member.reshape(param.shape) for member, param in zip(hyper_total, hyper_params)
    ]
    early_out = early_sum.astype(jnp.float32)

    def columns_of(value, total):
        return jnp.concatenate(
            [value[at * block_rows : (at + 1) * block_rows] for at in range(total)], axis=1
        )

    fc1_out = columns_of(early_out, weights_full.shape[0])
    fc2_out = early_out[fc1_out.size // model_width :]
    qkv_out = columns_of(late_out, 3)
    proj_out = late_out[3 * block_rows : 4 * block_rows]
    vector_out = late_out[4 * block_rows :].reshape(-1)
    parts = []
    vector_at = 0
    for length in vector_lengths:
        parts.append(vector_out[vector_at : vector_at + length])
        vector_at += length
    device_at = group_at * shard_total + shard_at

    def own_part(value):
        return lax.dynamic_slice_in_dim(value, device_at * block_rows, block_rows, 1)

    conv_parts = own_part(conv_parts)
    grad_cb_weight = jnp.dot(conv_parts.T, bias_row_all, precision=highest_precision)
    reduced = (
        grad_cb_weight,
        jnp.sum(conv_parts, axis=0),
        jnp.sum(own_part(gain_parts), axis=0),
        jnp.sum(own_part(shift_parts), axis=0),
        qkv_out,
        parts[0],
        proj_out,
        parts[1],
        parts[2],
        parts[3],
        fc1_out,
        parts[4],
        fc2_out,
        parts[5],
    )
    return (
        block_out,
        grad_pixels,
        hyper_total[0],
        hyper_total[1],
        hyper_total[2],
        hyper_total[3],
        hyper_total[4],
        hyper_total[5],
        hyper_total[6],
        hyper_total[7],
        hyper_total[8],
        hyper_total[9],
        hyper_total[10],
        hyper_total[11],
        hyper_total[12],
        hyper_total[13],
        grad_gen,
        grad_gen_shift,
        reduced[0],
        reduced[1],
        reduced[2],
        reduced[3],
        reduced[4],
        reduced[5],
        reduced[6],
        reduced[7],
        reduced[8],
        reduced[9],
        reduced[10],
        reduced[11],
        reduced[12],
        reduced[13],
    )


def solution(mesh):
    groups, shards = mesh.devices.shape
    return jax.shard_map(
        local,
        mesh=Mesh(mesh.devices.reshape(groups, shards // 2, 2), BOTH),
        in_specs=(
            P(BOTH, None, None, None),
            P(BOTH, None, None),
            P("grp"),
            P("grp", None),
            P(),
            P(),
            P(),
            P(),
            P(),
            P(),
            P(),
            P(),
            P(),
            P(),
            P(),
            P(),
            P(),
            P(),
            P(SHARDS, None, None),
            P(SHARDS, None),
            P(SHARDS, None),
            P(SHARDS),
            P(SHARDS),
            P(SHARDS),
            P(SHARDS, None),
            P(SHARDS),
            P(SHARDS, None),
            P(SHARDS),
            P(SHARDS),
            P(SHARDS),
            P(SHARDS, None),
            P(SHARDS),
            P(SHARDS, None),
            P(SHARDS),
        ),
        out_specs=(
            P(BOTH, None, None),
            P(BOTH, None, None, None),
            P(),
            P(),
            P(),
            P(),
            P(),
            P(),
            P(),
            P(),
            P(),
            P(),
            P(),
            P(),
            P(),
            P(),
            P(SHARDS, "grp", None),
            P(SHARDS, "grp"),
            P(BOTH, None),
            P(BOTH),
            P(BOTH),
            P(BOTH),
            P(BOTH, None),
            P(BOTH),
            P(BOTH, None),
            P(BOTH),
            P(BOTH),
            P(BOTH),
            P(BOTH, None),
            P(BOTH),
            P(BOTH, None),
            P(BOTH),
        ),
        check_vma=False,
    )
```

```python
import functools

import jax
import jax.numpy as jnp
from jax import lax
from jax.experimental import pallas as pl
from jax.experimental.pallas import tpu as pltpu
from jax.sharding import Mesh, PartitionSpec as P

HEADS = 12
WHEADS = 4
WAVES = 256


norm_eps = 1e-06
hyper_eps = 1e-05
highest_precision = lax.Precision.HIGHEST


def layer_norm(values, norm_gain, norm_shift, epsilon):
    centre = values - jnp.mean(values, axis=-1, keepdims=True)
    spread = jnp.mean(centre * centre, axis=-1, keepdims=True)
    return centre * lax.rsqrt(spread + epsilon) * norm_gain + norm_shift


def gelu_exact(values):
    return jax.nn.gelu(values, approximate=False)


def wave_embed(indices, hyper_width):
    half_model_width = hyper_width // 2
    wavelength = 400.0 + 2100.0 * indices.astype(jnp.float32) / (WAVES - 1)
    frequency = 1.0 / 10000.0 ** (
        jnp.arange(half_model_width, dtype=jnp.float32) / half_model_width
    )
    angles = wavelength[:, None] * frequency[None, :]
    return jnp.concatenate([jnp.sin(angles), jnp.cos(angles)], axis=-1)


def hyper_forward(params, indices, band_total):
    (
        tokens,
        bias_tok,
        qkv_w,
        qv_b,
        out_w,
        out_b,
        gain_one,
        shift_one,
        ff_in,
        ff_in_b,
        ff_out,
        ff_out_b,
        gain_two,
        shift_two,
    ) = params
    hyper_width = tokens.shape[1]
    slot_count = indices.shape[0]
    token_rows = tokens.shape[0]
    head_dim = hyper_width // WHEADS
    waves = wave_embed(indices, hyper_width)
    joined = jnp.concatenate([tokens, waves, bias_tok[None, :]], axis=0)
    query_rows = joined[token_rows:]
    queries = (
        jnp.dot(query_rows, qkv_w[:, :hyper_width], precision=highest_precision)
        + qv_b[:hyper_width]
    ).reshape(slot_count + 1, WHEADS, head_dim)
    key_rows = jnp.dot(
        joined, qkv_w[:, hyper_width : 2 * hyper_width], precision=highest_precision
    ).reshape(-1, WHEADS, head_dim)
    values = (
        jnp.dot(joined, qkv_w[:, 2 * hyper_width :], precision=highest_precision)
        + qv_b[hyper_width:]
    ).reshape(-1, WHEADS, head_dim)
    scores = jnp.einsum(
        "qhd,khd->hqk", queries, key_rows, precision=highest_precision
    ) * head_dim ** (-0.5)
    offsets = jnp.arange(joined.shape[0]) - token_rows
    usable = (offsets < band_total) | (offsets == slot_count)
    scores = jnp.where(usable[None, None, :], scores, -1e30)
    weights = jax.nn.softmax(scores, axis=-1)
    mixture = jnp.einsum("hqk,khd->qhd", weights, values, precision=highest_precision).reshape(
        slot_count + 1, hyper_width
    )
    normed_one = layer_norm(
        query_rows + jnp.dot(mixture, out_w, precision=highest_precision) + out_b,
        gain_one,
        shift_one,
        hyper_eps,
    )
    hidden = gelu_exact(jnp.dot(normed_one, ff_in, precision=highest_precision) + ff_in_b)
    normed_two = layer_norm(
        normed_one + jnp.dot(hidden, ff_out, precision=highest_precision) + ff_out_b,
        gain_two,
        shift_two,
        hyper_eps,
    )
    return (normed_two[:slot_count] + waves, normed_two[slot_count])


SHARDS = ("z", "core")
BOTH = ("grp",) + SHARDS


def torus_block():
    return lax.axis_size("grp") == 4 and lax.axis_size(SHARDS) == 8


def flipped(index, bit):
    return index ^ bit


def swap(value, bit):
    return lax.ppermute(value, BOTH, [(i, i ^ bit) for i in range(32)])


def around_z(value, shift):
    moves = [(i, i - i % 8 + (i % 8 // 2 + shift) % 4 * 2 + i % 2) for i in range(32)]
    return lax.ppermute(value, BOTH, moves)


def pick(value, index, axis=0):
    return lax.dynamic_index_in_dim(value, index, axis, keepdims=False)


def add_low(left, right):
    return (left.astype(jnp.float32) + right.astype(jnp.float32)).astype(jnp.bfloat16)


def z_index():
    return (lax.axis_index(SHARDS) // 2).astype(jnp.int32)


def scatter_start(chunks):
    z = z_index()
    return [pick(chunks, z)] + [
        around_z(pick(chunks, (z + shift) % 4), shift) for shift in range(1, 4)
    ]


def scatter_end(terms):
    return sum(term.astype(jnp.float32) for term in terms)


def gather_start(value):
    return [value] + [around_z(value, shift) for shift in range(1, 4)]


def gather_end(held):
    z = z_index()
    rows = []
    for place in range(4):
        row = held[(0 - place) % 4]
        for z_at in range(1, 4):
            row = jnp.where(z == z_at, held[(z_at - place) % 4], row)
        rows.append(row)
    return jnp.stack(rows)


def in_order(bit, own, other, axis):
    return jnp.stack(
        [jnp.where(bit == 0, own, other), jnp.where(bit == 0, other, own)], axis=axis
    )


def together(*values):
    return lax.optimization_barrier(values)


def core_half(value, axis):
    core = lax.axis_index(SHARDS) % 2
    return pick(value, core, axis), pick(value, 1 - core, axis)


def gather_small(value):
    if not torus_block():
        return lax.all_gather(value, SHARDS, axis=0, tiled=False)
    shard = lax.axis_index(SHARDS)
    value = in_order(shard % 2, value, swap(value, 1), 0)
    value = in_order(shard // 2 % 2, value, swap(value, 2), 0)
    value = in_order(shard // 4, value, swap(value, 4), 0)
    return value.reshape((8,) + value.shape[3:])


def gather_weights(qkv_weight, proj_weight, fc1_weight, fc2_weight):
    width = proj_weight.shape[1]
    hidden = fc1_weight.shape[1]
    part = hidden // 4
    if not torus_block():
        both = jnp.concatenate([qkv_weight, proj_weight], axis=1)
        both = lax.all_gather(both, SHARDS, axis=0, tiled=True)
        fc1 = lax.all_gather(fc1_weight, SHARDS, axis=0, tiled=True)
        fc2 = lax.all_gather(fc2_weight, SHARDS, axis=0, tiled=True)
        both = both.reshape(8, -1, 4, width).transpose(2, 0, 1, 3)
        fc1 = fc1.reshape(8, -1, 4, part).transpose(2, 0, 1, 3)
        fc2 = fc2.reshape(8, 4, -1, width).transpose(1, 0, 2, 3)
        return jnp.concatenate([both, fc1, fc2], axis=2)
    shard = proj_weight.shape[0]
    group = lax.axis_index("grp")
    own = jnp.concatenate(
        [
            jnp.where(
                group == 3,
                proj_weight,
                lax.dynamic_slice_in_dim(qkv_weight, jnp.minimum(group, 2) * width, width, 1),
            ),
            lax.dynamic_slice_in_dim(fc1_weight, group * part, part, 1),
            lax.dynamic_slice_in_dim(fc2_weight, group * shard, shard, 0),
        ]
    )
    return lax.all_gather(own, BOTH, axis=0, tiled=False).reshape(4, 8, 3 * shard, width)


def gather_kernels(kernels, rows_call):
    if not torus_block():
        kernels = lax.all_gather(kernels, SHARDS, axis=0, tiled=False)
        kernels = kernels.reshape((-1, 2) + kernels.shape[1:])
        return core_half(kernels, 1) + (rows_call(None),)
    held = gather_start(kernels)
    held, rows = together(held, rows_call(kernels))
    line = gather_end(held)
    return line, swap(line, 1), rows


def repack(packed, devices):
    few, rows, width = packed.shape
    each = width // few
    more = devices // few
    first = packed[:, : rows // 2].reshape(few, -1, more, each // more, width)
    first = first.transpose(0, 2, 1, 3, 4).reshape(devices, -1, width)
    return jnp.concatenate([first, packed[:, rows // 2 :].reshape(devices, -1, width)], axis=1)


def sum_cores(packed):
    if not torus_block():
        devices = lax.axis_size("grp") * lax.axis_size(SHARDS)
        packed = packed.transpose(1, 0, 2, 3).reshape((-1,) + packed.shape[2:])
        return lax.psum_scatter(
            repack(packed, devices), BOTH, scatter_dimension=0, tiled=True
        )[0]
    return lax.psum_scatter(packed, "core", scatter_dimension=0, tiled=True)[0]


def sum_groups(early):
    if not torus_block():
        return early
    early = early.reshape((4, 4) + early.shape[1:])
    return lax.psum_scatter(early, "grp", scatter_dimension=0, tiled=True)[0]


def sum_chips(early):
    if not torus_block():
        return early
    return lax.psum_scatter(early, "z", scatter_dimension=0, tiled=True)[0]


def start_late(keep, send, later):
    if not torus_block():
        late = in_order(lax.axis_index(SHARDS) % 2, keep, send, 1)
        late = late.reshape((-1,) + keep.shape[1:])
        return lax.psum_scatter(late, BOTH, scatter_dimension=0, tiled=True)[0], later
    send_in = swap(send, 1)
    keep, later = together(keep, later)
    return (keep, send_in), later


def reduce_late(keep, send, early, late, code_call, fill_calls, gen_call):
    if not torus_block():
        kernels = in_order(lax.axis_index(SHARDS) % 2, keep, send, 1)
        kernels = kernels.reshape((-1,) + keep.shape[1:])
        kernels = lax.psum_scatter(kernels, SHARDS, scatter_dimension=0, tiled=True)[0]
        kernels = kernels.astype(jnp.float32)
        code = jnp.sum(ordered_gather(code_call(kernels), SHARDS), axis=0)
        filled = [call(None) for call in fill_calls] + [gen_call(kernels)]
        return early, [late], ordered_gather(code, "grp"), filled
    group = lax.axis_index("grp")
    x, y = group % 2, group // 2
    send_in = swap(send, 1)
    late = add_low(*late).reshape((2, 2, 4) + late[0].shape[1:])
    first, second = late[:, :, :2], late[:, :, 2:]
    send_in, late_out, late_other = together(
        send_in, pick(first, 1 - x, 1), pick(second, 1 - y, 0)
    )
    first_in, second_in = swap(late_out, 8), swap(late_other, 16)
    chunks = add_low(keep, send_in)
    terms = scatter_start(chunks)
    filled = [fill_calls[0](chunks)]
    first_in, second_in, filled[0] = together(first_in, second_in, filled[0])
    first = add_low(pick(first, x, 1), first_in)
    second = add_low(pick(second, y, 0), second_in)
    first_in = swap(pick(first, 1 - y), 16)
    second_in = swap(pick(second, 1 - x), 8)
    filled.append(fill_calls[1](first))
    terms, filled[1] = together(terms, filled[1])
    kernels = scatter_end(terms)
    code = code_call(kernels)
    code = code + swap(code, 1)
    code = code + swap(code, 2)
    code, kernels, first_in, second_in, early = together(
        code, kernels, first_in, second_in, early
    )
    early = sum_chips(early)
    late = jnp.concatenate(
        [add_low(pick(first, y), first_in), add_low(pick(second, x), second_in)]
    )
    late_terms = scatter_start(late)
    code = code + swap(code, 4)
    code = in_order(x, code, swap(code, 8), 0)
    code = in_order(y, code, swap(code, 16), 0).reshape((4,) + code.shape[1:])
    filled.append(gen_call(kernels))
    return early, late_terms, code, filled


def lane_half(shape):
    return lax.broadcasted_iota(jnp.int32, shape, len(shape) - 1) % 128 < 64


def attention_forward_kernel(
    tokens, rows_ref, query_ref, key_ref, value_ref, bias_ref, projected_ref, attended_ref, probs_ref
):
    rows, width = rows_ref.shape
    for at, ref in enumerate((query_ref, key_ref, value_ref)):
        made = jnp.dot(
            rows_ref[...], ref[...].reshape(width, width), preferred_element_type=jnp.float32
        )
        projected_ref[at] = (made + bias_ref[at]).astype(jnp.bfloat16)
    low_half = lane_half((rows, 128))
    real_key = lax.broadcasted_iota(jnp.int32, (rows, rows), 0) < tokens
    for pair in range(width // 128):
        at = pair * 128
        queries = projected_ref[0, :, at : at + 128] * jnp.bfloat16(0.125)
        key_rows = projected_ref[1, :, at : at + 128]
        values = projected_ref[2, :, at : at + 128]
        halves = []
        for half in range(2):
            chosen = low_half if half == 0 else ~low_half
            own_queries = jnp.where(chosen, queries, jnp.bfloat16(0))
            scores = lax.dot_general(
                key_rows, own_queries, (((1,), (1,)), ((), ())), preferred_element_type=jnp.float32
            )
            scores = jnp.where(real_key, scores, -1e30)
            raised = jnp.exp(scores - jnp.max(scores, axis=0, keepdims=True))
            probs = raised * (1.0 / jnp.sum(raised, axis=0, keepdims=True))
            probs = probs.astype(jnp.bfloat16)
            probs_ref[2 * pair + half] = probs
            halves.append(
                lax.dot_general(
                    probs, values, (((0,), (0,)), ((), ())), preferred_element_type=jnp.float32
                )
            )
        attended_ref[:, at : at + 128] = jnp.where(low_half, halves[0], halves[1]).astype(
            jnp.bfloat16
        )


def weight_spec(weights, column, section=0):
    _, eighths, rows, width = weights.shape
    return pl.BlockSpec((None, eighths, rows // 3, width), lambda i: (column, 0, section, 0))


def attention_forward(normed, weights, bias, images, tokens):
    total, width = normed.shape
    rows = total // images
    heads = width // 64
    return pl.pallas_call(
        functools.partial(attention_forward_kernel, tokens),
        grid=(images,),
        in_specs=[
            pl.BlockSpec((rows, width), lambda i: (i, 0)),
            weight_spec(weights, 0),
            weight_spec(weights, 1),
            weight_spec(weights, 2),
            pl.BlockSpec((3, 1, width), lambda i: (0, 0, 0)),
        ],
        out_specs=[
            pl.BlockSpec((3, rows, width), lambda i: (0, i, 0)),
            pl.BlockSpec((rows, width), lambda i: (i, 0)),
            pl.BlockSpec((None, heads, rows, rows), lambda i: (i, 0, 0, 0)),
        ],
        out_shape=[
            jax.ShapeDtypeStruct((3, total, width), jnp.bfloat16),
            jax.ShapeDtypeStruct((total, width), jnp.bfloat16),
            jax.ShapeDtypeStruct((images, heads, rows, rows), jnp.bfloat16),
        ],
        compiler_params=pltpu.CompilerParams(vmem_limit_bytes=48 << 20),
        cost_estimate=pl.CostEstimate(
            flops=images * heads * rows * rows * 64 * 4 + 6 * total * width * width,
            bytes_accessed=images * rows * (8 * width + 2 * heads * rows) + 6 * width * width,
            transcendentals=images * heads * rows * rows,
        ),
        name="attention_forward",
    )(normed, weights, weights, weights, bias)


def attention_backward_kernel(
    projected_ref,
    probs_ref,
    normed_grad_ref,
    upstream_ref,
    middle_ref,
    proj_ref,
    gain_ref,
    out_ref,
    middle_grad_ref,
    low_ref,
    sums_ref,
    grad_ref,
):
    _, rows, width = projected_ref.shape
    low_half = lane_half((rows, 128))

    @pl.when(pl.program_id(0) == 0)
    def _():
        sums_ref[...] = jnp.zeros_like(sums_ref)

    def folded(value):
        return jnp.sum(value.reshape(rows // 8, 8, width), axis=0)

    middle = middle_ref[...]
    centre = middle - jnp.mean(middle, axis=-1, keepdims=True)
    spread = jnp.mean(centre * centre, axis=-1, keepdims=True)
    scale = lax.rsqrt(spread + norm_eps)
    normed = centre * scale
    grads = normed_grad_ref[...]
    sums_ref[3] += folded(grads * normed)
    sums_ref[4] += folded(grads)
    grads = grads * gain_ref[...]
    grads = scale * (
        grads
        - jnp.mean(grads, axis=-1, keepdims=True)
        - normed * jnp.mean(grads * normed, axis=-1, keepdims=True)
    )
    grads = upstream_ref[...].astype(jnp.float32) + grads
    middle_grad_ref[...] = grads
    low = grads.astype(jnp.bfloat16)
    low_ref[...] = low
    sums_ref[5] += folded(low.astype(jnp.float32))
    grad_ref[...] = lax.dot_general(
        low,
        proj_ref[...].reshape(width, width),
        (((1,), (1,)), ((), ())),
        preferred_element_type=jnp.float32,
    ).astype(jnp.bfloat16)
    for pair in range(width // 128):
        at = pair * 128
        queries = projected_ref[0, :, at : at + 128]
        key_rows = projected_ref[1, :, at : at + 128]
        values = projected_ref[2, :, at : at + 128]
        grads = grad_ref[:, at : at + 128]
        found = []
        for half in range(2):
            chosen = low_half if half == 0 else ~low_half
            probs = probs_ref[2 * pair + half]
            own_grads = jnp.where(chosen, grads, jnp.bfloat16(0))
            grad_values = jnp.dot(probs, grads, preferred_element_type=jnp.float32)
            grad_probs = lax.dot_general(
                values, own_grads, (((1,), (1,)), ((), ())), preferred_element_type=jnp.float32
            )
            wide = probs.astype(jnp.float32)
            weighted = grad_probs * wide
            total = jnp.sum(weighted, axis=0, keepdims=True)
            grad_scores = (weighted - wide * total).astype(jnp.bfloat16)
            grad_keys = jnp.dot(grad_scores, queries, preferred_element_type=jnp.float32) * 0.125
            grad_queries = (
                lax.dot_general(
                    grad_scores,
                    key_rows,
                    (((0,), (0,)), ((), ())),
                    preferred_element_type=jnp.float32,
                )
                * 0.125
            )
            found.append((grad_queries, grad_keys, grad_values))
        for kind in range(3):
            joined = jnp.where(low_half, found[0][kind], found[1][kind]).astype(jnp.bfloat16)
            place = slice(at, at + 128)
            out_ref[kind, :, place] = joined
            sums_ref[kind, :, place] += jnp.sum(
                joined.astype(jnp.float32).reshape(rows // 8, 8, 128), axis=0
            )


def attention_backward(projected, probs, normed_grad, upstream, middle, weights, gain, images):
    _, total, width = projected.shape
    rows = total // images
    heads = width // 64
    row = pl.BlockSpec((rows, width), lambda i: (i, 0))
    return pl.pallas_call(
        attention_backward_kernel,
        grid=(images,),
        in_specs=[
            pl.BlockSpec((3, rows, width), lambda i: (0, i, 0)),
            pl.BlockSpec((None, heads, rows, rows), lambda i: (i, 0, 0, 0)),
            row,
            row,
            row,
            weight_spec(weights, 3),
            pl.BlockSpec((1, width), lambda i: (0, 0)),
        ],
        out_specs=[
            pl.BlockSpec((3, rows, width), lambda i: (0, i, 0)),
            row,
            row,
            pl.BlockSpec((6, 8, width), lambda i: (0, 0, 0)),
        ],
        out_shape=[
            pltpu.HBM((3, total, width), jnp.bfloat16),
            pltpu.HBM((total, width), jnp.float32),
            pltpu.HBM((total, width), jnp.bfloat16),
            jax.ShapeDtypeStruct((6, 8, width), jnp.float32),
        ],
        scratch_shapes=[pltpu.VMEM((rows, width), jnp.bfloat16)],
        compiler_params=pltpu.CompilerParams(vmem_limit_bytes=62 << 20),
        cost_estimate=pl.CostEstimate(flops=0, bytes_accessed=0, transcendentals=0),
        name="attention_backward",
    )(projected, probs, normed_grad, upstream, middle, weights, gain)


SLOT_ROWS = 16


def exact_dot(left, right, contract=((1,), (0,))):
    return lax.dot_general(
        left,
        right,
        (contract, ((), ())),
        precision=highest_precision,
        preferred_element_type=jnp.float32,
    )


def rows_norm(values, norm_gain, norm_shift, epsilon):
    centre = values - jnp.mean(values, axis=-1, keepdims=True)
    spread = jnp.mean(centre * centre, axis=-1, keepdims=True)
    return centre * lax.rsqrt(spread + epsilon) * norm_gain + norm_shift


def gelu_rows(values):
    return values * (0.5 + 0.5 * lax.erf(values * 0.7071067811865476))


def hyper_rows(params, waves, usable, slots):
    (
        tokens,
        bias_tok,
        qkv_w,
        qv_b,
        out_w,
        out_b,
        gain_one,
        shift_one,
        ff_in,
        ff_in_b,
        ff_out,
        ff_out_b,
        gain_two,
        shift_two,
    ) = params
    width = tokens.shape[1]
    head_dim = width // WHEADS
    total = waves.shape[0]
    place = lax.broadcasted_iota(jnp.int32, (total, 1), 0) & (SLOT_ROWS - 1)
    query_rows = jnp.where(place == slots, jnp.broadcast_to(bias_tok, (total, width)), waves)
    joined = jnp.concatenate([tokens, query_rows], axis=0)
    queries = exact_dot(query_rows, qkv_w[:, :width]) + qv_b[:, :width]
    key_rows = exact_dot(joined, qkv_w[:, width : 2 * width])
    values = exact_dot(joined, qkv_w[:, 2 * width :]) + qv_b[:, width:]
    head_at = lax.broadcasted_iota(jnp.int32, (1, width), 1)
    mixture = jnp.zeros((total, width), jnp.float32)
    for head in range(WHEADS):
        own = ((head_at >= head * head_dim) & (head_at < (head + 1) * head_dim)).astype(jnp.float32)
        scores = exact_dot(queries * own, key_rows, ((1,), (1,))) * head_dim ** (-0.5)
        scores = jnp.where(usable > 0, scores, -1e30)
        raised = jnp.exp(scores - lax.stop_gradient(jnp.max(scores, axis=-1, keepdims=True)))
        weights = raised / jnp.sum(raised, axis=-1, keepdims=True)
        mixture = mixture + exact_dot(weights, values) * own
    first = rows_norm(query_rows + exact_dot(mixture, out_w) + out_b, gain_one, shift_one, hyper_eps)
    hidden = gelu_rows(exact_dot(first, ff_in) + ff_in_b)
    return rows_norm(first + exact_dot(hidden, ff_out) + ff_out_b, gain_two, shift_two, hyper_eps)


def usable_rows(band_counts, slots, token_rows):
    groups = band_counts.shape[0]
    total = groups * SLOT_ROWS
    row = jnp.arange(total)
    own_group = row[:, None] // SLOT_ROWS == row[None, :] // SLOT_ROWS
    place = row % SLOT_ROWS
    present = (place < jnp.repeat(band_counts, SLOT_ROWS)) | (place == slots)
    return jnp.concatenate(
        [jnp.ones((total, token_rows)), (own_group & present[None, :]).astype(jnp.float32)], axis=1
    )


def hyper_params_2d(params):
    return tuple(member[None] if member.ndim == 1 else member for member in params)


def wave_rows(indices, width):
    groups, slots = indices.shape
    waves = jax.vmap(lambda row: wave_embed(row, width))(indices)
    return jnp.pad(waves, ((0, 0), (0, SLOT_ROWS - slots), (0, 0))).reshape(-1, width)


def hyper_forward_kernel(slots, waves_ref, usable_ref, *refs):
    refs[-1][...] = hyper_rows(
        tuple(ref[...] for ref in refs[:-1]), waves_ref[...], usable_ref[...], slots
    )


def hyper_backward_kernel(slots, waves_ref, usable_ref, grads_ref, *refs):
    count = len(refs) // 2
    waves, usable = waves_ref[...], usable_ref[...]
    _, pull = jax.vjp(
        lambda params: hyper_rows(params, waves, usable, slots),
        tuple(ref[...] for ref in refs[:count]),
    )
    (found,) = pull(grads_ref[...])
    for ref, value in zip(refs[count:], found):
        ref[...] = value


def hyper_forward_call(params, waves, usable, slots):
    return pl.pallas_call(
        functools.partial(hyper_forward_kernel, slots),
        out_shape=jax.ShapeDtypeStruct(waves.shape, jnp.float32),
        name="hyper_forward",
    )(waves, usable, *params)


def hyper_backward_call(params, waves, usable, grads, slots):
    return pl.pallas_call(
        functools.partial(hyper_backward_kernel, slots),
        out_shape=[jax.ShapeDtypeStruct(member.shape, jnp.float32) for member in params],
        name="hyper_backward",
    )(waves, usable, grads, *params)


def embed_kernel(
    bands, small_at, core_ref, line_ref, other_ref, pixels_ref, kernels_ref, stream_ref, normed_ref, rows_ref
):
    chips, _, width = line_ref.shape
    part = kernels_ref.shape[0] // (2 * chips * bands)
    shard = width // (2 * chips)

    @pl.when(pl.program_id(0) == 0)
    def _():
        for core in range(2):
            low_ref, high_ref = (line_ref, other_ref) if core == 0 else (other_ref, line_ref)

            @pl.when((core_ref[0] == 0) == (core == 0))
            def _():
                for chip in range(chips):
                    for band in range(bands):
                        place = (band * chips + chip) * 2 * part
                        here = slice(band * part, (band + 1) * part)
                        kernels_ref[place : place + part] = low_ref[chip, here]
                        kernels_ref[place + part : place + 2 * part] = high_ref[chip, here]
                    for which, ref in enumerate((low_ref, high_ref)):
                        small = ref[chip, small_at : small_at + 16, :shard].astype(jnp.float32)
                        at = (chip * 2 + which) * shard
                        rows_ref[:, at : at + shard] = small

    shift = rows_ref[0:1] + rows_ref[1:2]
    stream = (
        jnp.dot(pixels_ref[...], kernels_ref[...], preferred_element_type=jnp.float32) + shift
    )
    stream_ref[...] = stream
    centre = stream - jnp.mean(stream, axis=-1, keepdims=True)
    spread = jnp.mean(centre * centre, axis=-1, keepdims=True)
    normed = centre * lax.rsqrt(spread + norm_eps) * rows_ref[2:3] + rows_ref[3:4]
    normed_ref[...] = normed.astype(jnp.bfloat16)


def embed(core, line, other, pixel_rows, images, bands, small_at):
    width = line.shape[2]
    total, depth = pixel_rows.shape
    rows = total // images
    part_spec = pl.BlockSpec(line.shape, lambda i, core_ref: (0, 0, 0))
    row = pl.BlockSpec((rows, width), lambda i, core_ref: (i, 0))
    return pl.pallas_call(
        functools.partial(embed_kernel, bands, small_at),
        grid_spec=pltpu.PrefetchScalarGridSpec(
            num_scalar_prefetch=1,
            grid=(images,),
            in_specs=[
                part_spec,
                part_spec,
                pl.BlockSpec((rows, depth), lambda i, core_ref: (i, 0)),
            ],
            out_specs=[pl.BlockSpec((depth, width), lambda i, core_ref: (0, 0)), row, row],
            scratch_shapes=[pltpu.VMEM((16, width), jnp.float32)],
        ),
        out_shape=[
            jax.ShapeDtypeStruct((depth, width), jnp.bfloat16),
            jax.ShapeDtypeStruct((total, width), jnp.float32),
            jax.ShapeDtypeStruct((total, width), jnp.bfloat16),
        ],
        compiler_params=pltpu.CompilerParams(vmem_limit_bytes=48 << 20),
        cost_estimate=pl.CostEstimate(
            flops=2 * total * width * depth,
            bytes_accessed=total * (2 * depth + 6 * width) + 4 * depth * width,
            transcendentals=total,
        ),
        name="embed",
    )(core, line, other, pixel_rows)


def first_backward_kernel(
    bands,
    core_ref,
    projected_ref,
    query_ref,
    key_ref,
    value_ref,
    stream_ref,
    residual_ref,
    gain_ref,
    pixels_ref,
    out_ref,
    keep_ref,
    send_ref,
    sums_ref,
    low_ref,
    total_ref,
):
    rows, width = stream_ref.shape
    chips, part, _ = keep_ref.shape
    part //= bands

    @pl.when(pl.program_id(0) == 0)
    def _():
        sums_ref[...] = jnp.zeros_like(sums_ref)

    def folded(value):
        return jnp.sum(value.reshape(rows // 8, 8, width), axis=0)

    grads = sum(
        lax.dot_general(
            projected_ref[at],
            ref[...].reshape(width, width),
            (((1,), (1,)), ((), ())),
            preferred_element_type=jnp.float32,
        )
        for at, ref in enumerate((query_ref, key_ref, value_ref))
    )
    stream = stream_ref[...]
    centre = stream - jnp.mean(stream, axis=-1, keepdims=True)
    spread = jnp.mean(centre * centre, axis=-1, keepdims=True)
    scale = lax.rsqrt(spread + norm_eps)
    normed = centre * scale
    sums_ref[0] += folded(grads * normed)
    sums_ref[1] += folded(grads)
    grads = grads * gain_ref[...]
    grads = scale * (
        grads
        - jnp.mean(grads, axis=-1, keepdims=True)
        - normed * jnp.mean(grads * normed, axis=-1, keepdims=True)
    )
    low = (residual_ref[...] + grads).astype(jnp.bfloat16)
    out_ref[...] = low
    sums_ref[2] += folded(low.astype(jnp.float32))
    low_ref[pl.ds(pl.multiple_of(pl.program_id(0) * rows, 16), rows), :] = low

    @pl.when(pl.program_id(0) == pl.num_programs(0) - 1)
    def _():
        total_ref[...] = jnp.dot(
            pixels_ref[...], low_ref[...], preferred_element_type=jnp.float32
        ).astype(jnp.bfloat16)

    for core in range(2):
        low_ref, high_ref = (keep_ref, send_ref) if core == 0 else (send_ref, keep_ref)

        @pl.when((pl.program_id(0) == pl.num_programs(0) - 1) & ((core_ref[0] == 0) == (core == 0)))
        def _():
            for chip in range(chips):
                for band in range(bands):
                    place = (band * chips + chip) * 2 * part
                    here = slice(band * part, (band + 1) * part)
                    made = total_ref[place : place + 2 * part]
                    low_ref[chip, here] = made[:part]
                    high_ref[chip, here] = made[part:]


def first_backward(
    core, grad_projected, weights, stream, residual, gain, pixel_columns, images, shards, bands
):
    total, width = stream.shape
    rows = total // images
    depth = pixel_columns.shape[0]
    row = pl.BlockSpec((rows, width), lambda i, core_ref: (i, 0))
    made = (shards // 2, depth // shards, width)
    part = pl.BlockSpec(made, lambda i, core_ref: (0, 0, 0))

    def column(at):
        _, eighths, shard, _ = weights.shape
        return pl.BlockSpec(
            (None, eighths, shard // 3, width), lambda i, core_ref: (at, 0, 0, 0)
        )

    return pl.pallas_call(
        functools.partial(first_backward_kernel, bands),
        grid_spec=pltpu.PrefetchScalarGridSpec(
            num_scalar_prefetch=1,
            grid=(images,),
        in_specs=[
            pl.BlockSpec((3, rows, width), lambda i, core_ref: (0, i, 0)),
            column(0),
            column(1),
            column(2),
            row,
            row,
            pl.BlockSpec((1, width), lambda i, core_ref: (0, 0)),
            pl.BlockSpec((depth, total), lambda i, core_ref: (0, 0)),
        ],
        out_specs=[
            row,
            part,
            part,
            pl.BlockSpec((3, 8, width), lambda i, core_ref: (0, 0, 0)),
        ],
        scratch_shapes=[
                pltpu.VMEM((total, width), jnp.bfloat16),
                pltpu.VMEM((depth, width), jnp.bfloat16),
            ],
        ),
        out_shape=[
            jax.ShapeDtypeStruct((total, width), jnp.bfloat16),
            jax.ShapeDtypeStruct(made, jnp.bfloat16),
            jax.ShapeDtypeStruct(made, jnp.bfloat16),
            jax.ShapeDtypeStruct((3, 8, width), jnp.float32),
        ],
        compiler_params=pltpu.CompilerParams(vmem_limit_bytes=48 << 20),
        cost_estimate=pl.CostEstimate(flops=0, bytes_accessed=0, transcendentals=0),
        name="first_backward",
    )(core, grad_projected, weights, weights, weights, stream, residual, gain, pixel_columns)


def late_kernel(
    core_ref,
    normed_ref,
    attended_ref,
    projected_ref,
    branch_ref,
    vectors_ref,
    keep_ref,
    send_ref,
    turned_ref,
    made_ref,
):
    at_step = pl.program_id(0)
    width = normed_ref.shape[1]
    pairs = keep_ref.shape[0]
    each = width // (2 * pairs)

    @pl.when(at_step == 0)
    def _():
        turned_ref[...] = normed_ref[...].T

    @pl.when(at_step == 3)
    def _():
        turned_ref[...] = attended_ref[...].T

    @pl.when(at_step < 3)
    def _():
        made = jnp.dot(turned_ref[...], projected_ref[...], preferred_element_type=jnp.float32)
        made_ref[...] = made.astype(jnp.bfloat16).reshape(made_ref.shape)

    @pl.when(at_step == 3)
    def _():
        made = jnp.dot(turned_ref[...], branch_ref[...], preferred_element_type=jnp.float32)
        made_ref[...] = made.astype(jnp.bfloat16).reshape(made_ref.shape)

    for core in range(2):
        low_ref, high_ref = (keep_ref, send_ref) if core == 0 else (send_ref, keep_ref)
        for step in range(4):

            @pl.when((at_step == step) & ((core_ref[0] == 0) == (core == 0)))
            def _():
                here = slice(step * each, (step + 1) * each)
                for pair in range(pairs):
                    low_ref[pair, here] = made_ref[2 * pair]
                    high_ref[pair, here] = made_ref[2 * pair + 1]
                    if step == 0:
                        low_ref[pair, 4 * each :] = vectors_ref[2 * pair]
                        high_ref[pair, 4 * each :] = vectors_ref[2 * pair + 1]


def late_gradients(core, normed, attended, grad_projected, branch, vectors):
    total, width = normed.shape
    devices, extra, _ = vectors.shape
    each = width // devices
    made = (devices // 2, 4 * each + extra, width)
    whole = pl.BlockSpec((total, width), lambda i, core_ref: (0, 0))
    part = pl.BlockSpec(made, lambda i, core_ref: (0, 0, 0))
    return pl.pallas_call(
        late_kernel,
        grid_spec=pltpu.PrefetchScalarGridSpec(
            num_scalar_prefetch=1,
            grid=(4,),
            in_specs=[
                whole,
                whole,
                pl.BlockSpec((None, total, width), lambda i, core_ref: (jnp.minimum(i, 2), 0, 0)),
                whole,
                pl.BlockSpec(vectors.shape, lambda i, core_ref: (0, 0, 0)),
            ],
            out_specs=[part, part],
            scratch_shapes=[
                pltpu.VMEM((width, total), jnp.bfloat16),
                pltpu.VMEM((devices, each, width), jnp.bfloat16),
            ],
        ),
        out_shape=[jax.ShapeDtypeStruct(made, jnp.bfloat16)] * 2,
        compiler_params=pltpu.CompilerParams(vmem_limit_bytes=48 << 20),
        cost_estimate=pl.CostEstimate(flops=0, bytes_accessed=0, transcendentals=0),
        name="late_gradients",
    )(core, normed, attended, grad_projected, branch, vectors)


def mlp_kernel(
    block,
    devices,
    rows_ref,
    upstream_ref,
    first_weight_ref,
    second_weight_ref,
    b1_ref,
    sums_ref,
    out_ref,
    grad_ref,
    packed_ref,
    turned_ref,
    act_ref,
    gate_ref,
    first_ref,
    second_ref,
    sems,
):
    at_step = pl.program_id(0)
    steps = pl.num_programs(0)
    total, width = rows_ref.shape
    eighths, shard, hidden_block = first_weight_ref.shape
    quarters, group, _, _ = second_weight_ref.shape
    w1 = first_weight_ref[...].reshape(width, hidden_block)
    w2 = jnp.concatenate(
        [second_weight_ref[at, eighth] for eighth in range(group) for at in range(quarters)]
    )
    first_rows = width // devices
    second_devices = devices // steps
    second_rows = hidden_block // second_devices

    def copies(step):
        found = []
        for core in range(2):
            found.append(
                pltpu.make_async_copy(
                    first_ref.at[:, core],
                    packed_ref.at[core, :, pl.ds(step * first_rows, first_rows), :],
                    sems.at[2 * core],
                )
            )
            found.append(
                pltpu.make_async_copy(
                    second_ref.at[:, core],
                    packed_ref.at[
                        core,
                        pl.ds(step * (second_devices // 2), second_devices // 2),
                        pl.ds(steps * first_rows, second_rows),
                        :,
                    ],
                    sems.at[2 * core + 1],
                )
            )
        return found

    @pl.when(at_step == 0)
    def _():
        out_ref[...] = jnp.zeros_like(out_ref)
        grad_ref[...] = jnp.zeros_like(grad_ref)
        turned_ref[...] = rows_ref[...].T

    for at in range(0, total, block):
        here = slice(at, at + block)
        gate_in = (
            jnp.dot(rows_ref[here], w1, preferred_element_type=jnp.float32) + b1_ref[...]
        )
        grad_act = lax.dot_general(
            upstream_ref[here],
            w2,
            (((1,), (1,)), ((), ())),
            preferred_element_type=jnp.float32,
        )
        chance = 0.5 + 0.5 * lax.erf(gate_in * 0.7071067811865476)
        density = 0.3989422804014327 * jnp.exp(-0.5 * gate_in * gate_in)
        act = (gate_in * chance).astype(jnp.bfloat16)
        gate = (grad_act * (chance + gate_in * density)).astype(jnp.bfloat16)
        act_ref[here] = act
        gate_ref[here] = gate
        wide = gate.astype(jnp.float32)
        part = jnp.sum(wide.reshape(block // 8, 8, wide.shape[1]), axis=0)
        sums_ref[...] = part if at == 0 else sums_ref[...] + part
        out_ref[here] += jnp.dot(act, w2, preferred_element_type=jnp.float32)
        grad_ref[here] += lax.dot_general(
            gate, w1, (((1,), (1,)), ((), ())), preferred_element_type=jnp.float32
        )

    @pl.when(at_step > 0)
    def _():
        for copy in copies(at_step - 1):
            copy.wait()

    first = jnp.dot(turned_ref[...], gate_ref[...], preferred_element_type=jnp.float32)
    first_ref[...] = first.astype(jnp.bfloat16).reshape(first_ref.shape)
    second = lax.dot_general(
        act_ref[...], upstream_ref[...], (((0,), (0,)), ((), ())), preferred_element_type=jnp.float32
    )
    second_ref[...] = second.astype(jnp.bfloat16).reshape(second_ref.shape)
    for copy in copies(at_step):
        copy.start()

    @pl.when(at_step == steps - 1)
    def _():
        for copy in copies(at_step):
            copy.wait()


def mlp(rows, upstream, weights, b1, row_block, devices):
    total, width = rows.shape
    steps, eighths, shard, hidden_block = weights.shape
    shard //= 3
    hidden = steps * hidden_block
    whole = pl.BlockSpec((total, width), lambda i: (0, 0))
    packed_rows = (width * steps + hidden) // devices
    return pl.pallas_call(
        functools.partial(mlp_kernel, row_block, devices),
        grid=(steps,),
        in_specs=[
            whole,
            whole,
            pl.BlockSpec((None, eighths, shard, hidden_block), lambda i: (i, 0, 1, 0)),
            pl.BlockSpec((steps, eighths // steps, shard, width), lambda i: (0, i, 2, 0)),
            pl.BlockSpec((1, hidden_block), lambda i: (0, i)),
        ],
        out_specs=[
            pl.BlockSpec((8, hidden_block), lambda i: (0, i)),
            whole,
            whole,
            pl.BlockSpec(memory_space=pl.ANY),
        ],
        out_shape=[
            jax.ShapeDtypeStruct((8, hidden), jnp.float32),
            jax.ShapeDtypeStruct((total, width), jnp.float32),
            jax.ShapeDtypeStruct((total, width), jnp.float32),
            jax.ShapeDtypeStruct((2, devices // 2, packed_rows, width), jnp.bfloat16),
        ],
        scratch_shapes=[
            pltpu.VMEM((width, total), jnp.bfloat16),
            pltpu.VMEM((total, hidden_block), jnp.bfloat16),
            pltpu.VMEM((total, hidden_block), jnp.bfloat16),
            pltpu.VMEM((devices // 2, 2, width // devices, width), jnp.bfloat16),
            pltpu.VMEM((devices // steps // 2, 2, hidden // devices, width), jnp.bfloat16),
            pltpu.SemaphoreType.DMA((4,)),
        ],
        compiler_params=pltpu.CompilerParams(vmem_limit_bytes=52 << 20),
        cost_estimate=pl.CostEstimate(
            flops=12 * total * width * hidden,
            bytes_accessed=8 * width * hidden + 12 * total * width,
            transcendentals=2 * total * hidden,
        ),
        name="mlp",
    )(rows, upstream, weights, weights, b1)


def pixel_grad_kernel(grad_ref, kernels_ref, out_ref):
    tokens, bands, patch = out_ref.shape
    for band in range(bands):
        found = lax.dot_general(
            grad_ref[...],
            kernels_ref[band * patch : (band + 1) * patch, :],
            (((1,), (1,)), ((), ())),
            preferred_element_type=jnp.float32,
        )
        out_ref[:, band, :] = found[:tokens]


def pixel_grad(grads, kernels, images, tokens, bands):
    total, width = grads.shape
    patch = kernels.shape[0] // bands
    return pl.pallas_call(
        pixel_grad_kernel,
        grid=(images,),
        in_specs=[
            pl.BlockSpec((total // images, width), lambda i: (i, 0)),
            pl.BlockSpec(kernels.shape, lambda i: (0, 0)),
        ],
        out_specs=pl.BlockSpec((None, tokens, bands, patch), lambda i: (i, 0, 0, 0)),
        out_shape=jax.ShapeDtypeStruct((images, tokens, bands, patch), jnp.float32),
        compiler_params=pltpu.CompilerParams(vmem_limit_bytes=48 << 20),
        cost_estimate=pl.CostEstimate(flops=0, bytes_accessed=0, transcendentals=0),
        name="pixel_grad",
    )(grads, kernels)


def ordered_gather(value, axis):
    total = lax.axis_size(axis)
    at = lax.axis_index(axis)
    slots = jnp.arange(total).reshape((total,) + (1,) * value.ndim)
    gathered = jnp.where(slots == at, value[None], jnp.zeros((), value.dtype))
    for shift in range(1, total):
        moved = lax.ppermute(value, axis, [(i, (i + shift) % total) for i in range(total)])
        gathered = jnp.where(slots == (at - shift) % total, moved[None], gathered)
    return gathered


def local(
    pixels,
    cotangent,
    band_count,
    wave_index,
    weight_tokens,
    bias_token,
    hyper_qkv,
    hyper_qv_bias,
    hyper_out,
    hyper_out_bias,
    hyper_norm1_gain,
    hyper_norm1_bias,
    hyper_ff1,
    hyper_ff1_bias,
    hyper_ff2,
    hyper_ff2_bias,
    hyper_norm2_gain,
    hyper_norm2_bias,
    kernel_gen,
    kernel_gen_bias,
    conv_bias_gen,
    conv_bias_gen_bias,
    norm1_gain,
    norm1_bias,
    qkv_weight,
    qv_bias,
    proj_weight,
    proj_bias,
    norm2_gain,
    norm2_bias,
    fc1_weight,
    fc1_bias,
    fc2_weight,
    fc2_bias,
):
    group_total = lax.axis_size("grp")
    shard_total = lax.axis_size(SHARDS)
    group_at = lax.axis_index("grp")
    shard_at = lax.axis_index(SHARDS)
    images = pixels.shape[0]
    slot_count = pixels.shape[1]
    tokens = pixels.shape[2]
    patch = pixels.shape[3]
    model_width = cotangent.shape[2]
    padded = -(-tokens // 16) * 16
    row_count = images * padded

    def pad_rows(value):
        return jnp.pad(value, ((0, 0), (0, padded - tokens), (0, 0))).reshape(row_count, -1)

    band_total = band_count[0]
    band_mask = (jnp.arange(slot_count) < band_total).astype(jnp.float32)
    hyper_params = (
        weight_tokens,
        bias_token,
        hyper_qkv,
        hyper_qv_bias,
        hyper_out,
        hyper_out_bias,
        hyper_norm1_gain,
        hyper_norm1_bias,
        hyper_ff1,
        hyper_ff1_bias,
        hyper_ff2,
        hyper_ff2_bias,
        hyper_norm2_gain,
        hyper_norm2_bias,
    )
    hyper_wide = weight_tokens.shape[1]
    flat_params = hyper_params_2d(hyper_params)
    shard_patch = kernel_gen.shape[0]
    shard_rows = proj_weight.shape[0]
    lanes = hyper_wide
    folds = model_width // lanes
    fold_rows = shard_rows // folds
    small = [
        conv_bias_gen_bias,
        norm1_gain,
        norm1_bias,
        qv_bias,
        proj_bias,
        norm2_gain,
        norm2_bias,
        fc1_bias,
        fc2_bias,
    ]
    kernel_total = slot_count * shard_patch
    own_waves = wave_rows(wave_index, hyper_wide)
    own_usable = usable_rows(band_count, slot_count, weight_tokens.shape[0])

    def hyper_call():
        return hyper_forward_call(flat_params, own_waves, own_usable, slot_count)

    def all_call(tie):
        table = jnp.concatenate([band_count, wave_index[0]])
        every = ordered_gather(together(table, tie)[0], "grp")
        waves = wave_rows(every[:, 1:], hyper_wide)
        usable = usable_rows(every[:, 0], slot_count, weight_tokens.shape[0])
        return waves, usable, hyper_forward_call(flat_params, waves, usable, slot_count)

    def kernel_call(rows):
        hidden = (rows[:slot_count] + own_waves[:slot_count]).astype(jnp.bfloat16)
        made = (
            jnp.einsum("be,pde->bpd", hidden, kernel_gen, preferred_element_type=jnp.float32)
            + kernel_gen_bias.astype(jnp.float32)[None]
        )
        made = (made * band_mask[:, None, None]).astype(jnp.bfloat16)
        *members, small_gen, _ = together(*small, conv_bias_gen, rows)
        shift = jnp.dot(
            small_gen.astype(jnp.float32), rows[slot_count], precision=highest_precision
        ) + members[0].astype(jnp.float32)
        upper = lax.optimization_barrier(shift.astype(jnp.bfloat16))
        lower = (shift - upper.astype(jnp.float32)).astype(jnp.bfloat16)
        small_rows = jnp.stack(
            [
                jnp.pad(member, (0, model_width - member.shape[0]))
                for member in [upper, lower] + members[1:]
            ]
        )
        folded = jnp.concatenate(
            [small_gen[at * fold_rows : (at + 1) * fold_rows] for at in range(folds)], axis=1
        )
        packed = jnp.concatenate([jnp.pad(small_rows, ((0, 16 - len(small) - 1), (0, 0))), folded])
        packed = jnp.pad(packed, ((0, -packed.shape[0] % 16), (0, 0)))
        return jnp.concatenate([made.reshape(kernel_total, model_width), packed])

    def rows_call(tie):
        pixels_here, cotangent_here = pixels, cotangent
        if tie is not None:
            pixels_here, cotangent_here, _ = together(pixels, cotangent, tie)
        pixel_rows = pixels_here.transpose(0, 2, 1, 3).reshape(images, tokens, slot_count * patch)
        pixel_rows = pad_rows(pixel_rows)
        return pixel_rows, pad_rows(cotangent_here), pixel_rows.T

    weights_full = gather_weights(qkv_weight, proj_weight, fc1_weight, fc2_weight)
    core_at = (lax.axis_index(SHARDS) % 2).astype(jnp.int32).reshape(1)
    line, other, (pixel_rows, upstream_low, pixel_columns) = gather_kernels(kernel_call(hyper_call()), rows_call)
    patch_kernels, stream, normed_low = embed(
        core_at,
        line,
        other,
        pixel_rows,
        images,
        slot_count,
        kernel_total,
    )
    found_small = line[:, kernel_total:], other[:, kernel_total:]
    small_line, small_other, _ = together(*found_small, normed_low)
    packed = in_order(lax.axis_index(SHARDS) % 2, small_line, small_other, 1)
    packed = packed.reshape((shard_total,) + packed.shape[2:])
    folded = packed[:, 16 : 16 + fold_rows]
    cb_weight = jnp.concatenate(
        [folded[:, :, at : at + lanes] for at in range(0, model_width, lanes)], axis=1
    ).reshape(model_width, lanes)
    gain_one, _, qv_full, proj_shift, gain_two, shift_two, fc1_shift, fc2_shift = (
        packed[:, 2 + at, : member.shape[0]].reshape(-1) for at, member in enumerate(small[1:])
    )
    proj_full = weights_full[3, :, : weights_full.shape[2] // 3].reshape(model_width, model_width)
    full_bias = jnp.stack(
        [qv_full[:model_width], jnp.zeros((model_width,), jnp.bfloat16), qv_full[model_width:]]
    ).astype(jnp.float32)
    all_waves, all_usable, all_rows = all_call(normed_low)
    normed_low, all_rows = together(normed_low, all_rows)
    projected, attended, attn_probs = attention_forward(
        normed_low, weights_full, full_bias[:, None], images, tokens
    )
    all_rows = all_rows.reshape(group_total, SLOT_ROWS, hyper_wide)
    hidden_all = all_rows[:, :slot_count] + all_waves.reshape(all_rows.shape)[:, :slot_count]
    bias_row_all = all_rows[:, slot_count]
    middle = (
        stream
        + jnp.dot(attended, proj_full, preferred_element_type=jnp.float32)
        + proj_shift.astype(jnp.float32)
    )
    normed_two = layer_norm(
        middle, gain_two.astype(jnp.float32), shift_two.astype(jnp.float32), norm_eps
    )
    normed_two_low = normed_two.astype(jnp.bfloat16)
    upstream = upstream_low.astype(jnp.float32)
    gate_sums, update, grad_normed_two, early_block = mlp(
        normed_two_low,
        upstream_low,
        weights_full,
        fc1_shift.astype(jnp.float32)[None],
        row_count // 2,
        group_total * shard_total if torus_block() else 32,
    )
    grad_fc2_shift = jnp.sum(upstream, axis=0)
    grad_fc1_shift = jnp.sum(gate_sums, axis=0)
    early = sum_cores(early_block)
    grad_projected, grad_middle, middle_low, block_sums = attention_backward(
        projected,
        attn_probs,
        grad_normed_two,
        upstream_low,
        middle,
        weights_full,
        gain_two.astype(jnp.float32)[None],
        images,
    )
    early, grad_projected = together(early, grad_projected)
    early = sum_groups(early)
    block_sums = jnp.sum(block_sums, axis=1)
    grad_qv = jnp.concatenate([block_sums[0], block_sums[2]])
    grad_gain_two, grad_shift_two, grad_proj_shift = block_sums[3:]
    device_total = group_total * shard_total
    block_rows = model_width // device_total

    vectors = [
        grad_qv,
        grad_proj_shift,
        grad_gain_two,
        grad_shift_two,
        grad_fc1_shift,
        grad_fc2_shift,
    ]
    vector_lengths = [member.shape[0] // device_total for member in vectors]

    vector_block = jnp.concatenate(
        [member.reshape(device_total, -1) for member in vectors], axis=1
    ).astype(jnp.bfloat16)
    extra = -(-vector_block.shape[1] // model_width)
    extra += -(4 * block_rows + extra) % 8
    vector_block = jnp.pad(
        vector_block, ((0, 0), (0, extra * model_width - vector_block.shape[1]))
    ).reshape(device_total, extra, model_width)
    late, grad_projected = start_late(
        *late_gradients(core_at, normed_low, attended, grad_projected, middle_low, vector_block),
        grad_projected,
    )
    residual_reduced, keep_kernels, send_kernels, first_sums = first_backward(
        core_at,
        grad_projected,
        weights_full,
        stream,
        grad_middle,
        gain_one.astype(jnp.float32)[None],
        pixel_columns,
        images,
        shard_total,
        slot_count,
    )
    grad_gain_one, grad_shift_one, grad_conv_shift = jnp.sum(first_sums, axis=1)

    def pixels_call(tie):
        grads = residual_reduced if tie is None else together(residual_reduced, tie)[0]
        return pixel_grad(grads, patch_kernels, images, tokens, slot_count).transpose(0, 2, 1, 3)

    def out_call(tie):
        here = update if tie is None else together(update, tie)[0]
        block_out = middle + here + fc2_shift.astype(jnp.float32)
        return block_out.reshape(images, padded, model_width)[:, :tokens]

    grad_bias_row_part = jnp.dot(
        grad_conv_shift, cb_weight.astype(jnp.float32), precision=highest_precision
    )
    def code_call(group_kernels):
        grad_hidden_part = jnp.einsum(
            "bpd,pde->be",
            group_kernels.reshape(slot_count, shard_patch, model_width)
            * band_mask[:, None, None],
            kernel_gen.astype(jnp.float32),
            precision=highest_precision,
        )
        return jnp.concatenate(
            [grad_hidden_part, grad_bias_row_part[None]]
            + [
                member.reshape(-1, hyper_wide)
                for member in (grad_conv_shift, grad_gain_one, grad_shift_one)
            ]
        )

    group_width = model_width // group_total
    code_all = hidden_all.astype(jnp.bfloat16).astype(jnp.float32)

    def gen_call(group_kernels):
        group_kernels = group_kernels.reshape(slot_count, shard_patch, model_width)
        grad_pre = group_kernels * band_mask[:, None, None]
        swapped = lax.all_to_all(
            grad_pre.reshape(slot_count, shard_patch, group_total, group_width).transpose(
                2, 0, 1, 3
            ),
            "grp",
            0,
            0,
        ).reshape(group_total * slot_count, shard_patch, group_width)
        grad_gen = jnp.einsum(
            "kpd,ke->pde",
            swapped,
            code_all.reshape(group_total * slot_count, hyper_wide),
            precision=highest_precision,
        )
        return grad_gen, jnp.sum(swapped, axis=0)

    early_sum, late_terms, code_grads, filled = reduce_late(
        keep_kernels, send_kernels, early, late, code_call, [pixels_call, out_call], gen_call
    )
    grad_pixels, block_out, (grad_gen, grad_gen_shift) = filled
    fold_total = model_width // hyper_wide
    conv_parts, gain_parts, shift_parts = (
        code_grads[:, slot_count + 1 + at * fold_total : slot_count + 1 + (at + 1) * fold_total].reshape(
            group_total, model_width
        )
        for at in range(3)
    )
    code_grads = jnp.pad(
        code_grads[:, : slot_count + 1], ((0, 0), (0, SLOT_ROWS - slot_count - 1), (0, 0))
    ).reshape(-1, hyper_wide)
    hyper_total = hyper_backward_call(flat_params, all_waves, all_usable, code_grads, slot_count)
    late_terms, *hyper_total, early_sum = together(late_terms, *hyper_total, early_sum)
    late_out = scatter_end(late_terms)
    hyper_total = [
        member.reshape(param.shape) for member, param in zip(hyper_total, hyper_params)
    ]
    early_out = early_sum.astype(jnp.float32)

    def columns_of(value, total):
        return jnp.concatenate(
            [value[at * block_rows : (at + 1) * block_rows] for at in range(total)], axis=1
        )

    fc1_out = columns_of(early_out, weights_full.shape[0])
    fc2_out = early_out[fc1_out.size // model_width :]
    qkv_out = columns_of(late_out, 3)
    proj_out = late_out[3 * block_rows : 4 * block_rows]
    vector_out = late_out[4 * block_rows :].reshape(-1)
    parts = []
    vector_at = 0
    for length in vector_lengths:
        parts.append(vector_out[vector_at : vector_at + length])
        vector_at += length
    device_at = group_at * shard_total + shard_at

    def own_part(value):
        return lax.dynamic_slice_in_dim(value, device_at * block_rows, block_rows, 1)

    conv_parts = own_part(conv_parts)
    grad_cb_weight = jnp.dot(conv_parts.T, bias_row_all, precision=highest_precision)
    reduced = (
        grad_cb_weight,
        jnp.sum(conv_parts, axis=0),
        jnp.sum(own_part(gain_parts), axis=0),
        jnp.sum(own_part(shift_parts), axis=0),
        qkv_out,
        parts[0],
        proj_out,
        parts[1],
        parts[2],
        parts[3],
        fc1_out,
        parts[4],
        fc2_out,
        parts[5],
    )
    return (
        block_out,
        grad_pixels,
        hyper_total[0],
        hyper_total[1],
        hyper_total[2],
        hyper_total[3],
        hyper_total[4],
        hyper_total[5],
        hyper_total[6],
        hyper_total[7],
        hyper_total[8],
        hyper_total[9],
        hyper_total[10],
        hyper_total[11],
        hyper_total[12],
        hyper_total[13],
        grad_gen,
        grad_gen_shift,
        reduced[0],
        reduced[1],
        reduced[2],
        reduced[3],
        reduced[4],
        reduced[5],
        reduced[6],
        reduced[7],
        reduced[8],
        reduced[9],
        reduced[10],
        reduced[11],
        reduced[12],
        reduced[13],
    )


def solution(mesh):
    groups, shards = mesh.devices.shape
    return jax.shard_map(
        local,
        mesh=Mesh(mesh.devices.reshape(groups, shards // 2, 2), BOTH),
        in_specs=(
            P(BOTH, None, None, None),
            P(BOTH, None, None),
            P("grp"),
            P("grp", None),
            P(),
            P(),
            P(),
            P(),
            P(),
            P(),
            P(),
            P(),
            P(),
            P(),
            P(),
            P(),
            P(),
            P(),
            P(SHARDS, None, None),
            P(SHARDS, None),
            P(SHARDS, None),
            P(SHARDS),
            P(SHARDS),
            P(SHARDS),
            P(SHARDS, None),
            P(SHARDS),
            P(SHARDS, None),
            P(SHARDS),
            P(SHARDS),
            P(SHARDS),
            P(SHARDS, None),
            P(SHARDS),
            P(SHARDS, None),
            P(SHARDS),
        ),
        out_specs=(
            P(BOTH, None, None),
            P(BOTH, None, None, None),
            P(),
            P(),
            P(),
            P(),
            P(),
            P(),
            P(),
            P(),
            P(),
            P(),
            P(),
            P(),
            P(),
            P(),
            P(SHARDS, "grp", None),
            P(SHARDS, "grp"),
            P(BOTH, None),
            P(BOTH),
            P(BOTH),
            P(BOTH),
            P(BOTH, None),
            P(BOTH),
            P(BOTH, None),
            P(BOTH),
            P(BOTH),
            P(BOTH),
            P(BOTH, None),
            P(BOTH),
            P(BOTH, None),
            P(BOTH),
        ),
        check_vma=False,
    )
```
